32 devices in a mesh: grp: 4 (over x, core), mem: 8 (over z, y).
Axes of the slice: x: 2, y: 2, z: 4, core: 2. Of those that a mesh axis runs over, the one named last changes fastest.
Arguments:
- leaf_fronts: float32 [4, 4096, 4096], P('grp', None, 'mem'), as said below
- block_owner: int32 [4, 32], P('grp', 'mem'), may hold values from 0 to 31, as said below
- root_front: float32 [4096, 4096], P('grp', 'mem'), as said below
Outputs:
- root_factor: float32 [4096, 4096], P('grp', 'mem')
- log_det: float32 [5], replicated
The draws below stay inside these ranges and needn't reach their ends.
Inputs may be any that keep to these rules, and one draw needn't show every extreme that they name: Each row of block_owner is a permutation of 0 to 31. For each g, the matrix whose column block block_owner[g, t] is column block t of leaf_fronts[g] is symmetric positive definite. root_front is symmetric positive definite.
All inputs are finite; a program needn't handle non-finite values.
Results may differ from the reference program's by a relative error of at most 0.0021.
Values may be sent and summed in bfloat16 or wider, within the bound.
No kernel may reach another device: no remote copies, remote signals or barrier semaphores. Data moves between devices by JAX's collectives and lax.ppermute only.
A program may use at most 64 MiB of HBM per device.

```python
import math
import jax
import jax.numpy as jnp
from jax import lax

F = 4096
B = 128
NB = 32
PL = 3
PR = 2
LEAVES = 4


support_radius = 3.5


nugget = 0.5


leaf_amplitude = 0.5


root_amplitude = 1.5


def owner_table(key):
    leaf_keys = jax.random.split(jax.random.fold_in(key, 11), LEAVES)
    return jax.vmap(lambda leaf_key: jax.random.permutation(leaf_key, NB))(leaf_keys).astype(jnp.int32)


def site_map(key):
    return jax.random.permutation(jax.random.fold_in(key, 5), F).astype(jnp.int32)


def kernel_front(key, amplitude):
    sites = site_map(key)
    lattice = jnp.stack([sites % 16, sites // 16 % 16, sites // 256], axis=0).astype(jnp.float32)
    key_jitter = jax.random.fold_in(key, 7)
    key_scales = jax.random.fold_in(key, 9)
    jitter = jax.random.uniform(key_jitter, (3, F), jnp.float32, -0.3, 0.3)
    scales = jnp.exp(jax.random.uniform(key_scales, (F,), jnp.float32, math.log(0.6), math.log(1.7)))
    global_weight = 0.6
    global_length = 8.0
    points = lattice + jitter
    first_diff = points[0][:, None] - points[0][None, :]
    second_diff = points[1][:, None] - points[1][None, :]
    third_diff = points[2][:, None] - points[2][None, :]
    distance = jnp.sqrt(first_diff * first_diff + second_diff * second_diff + third_diff * third_diff)
    ratio = distance * (1.0 / support_radius)
    inside = jnp.maximum(1.0 - ratio, 0.0)
    kernel = inside * inside * inside * inside * (4.0 * ratio + 1.0)
    positions = jnp.arange(F)
    kernel = jnp.where(positions[:, None] == positions[None, :], 1.0 + nugget, kernel)
    kernel = kernel + global_weight * jnp.exp(distance * (-1.0 / global_length))
    return amplitude * scales[:, None] * scales[None, :] * kernel


def draw_block_owner(key, part):
    return owner_table(key)


def draw_leaf_fronts(key, part):
    owners = owner_table(key)
    leaf_keys = jax.random.split(jax.random.fold_in(key, 23), LEAVES)

    def one_leaf(pair):
        leaf_key, owner_row = pair
        front = kernel_front(leaf_key, leaf_amplitude)
        return front.reshape(F, NB, B)[:, owner_row].reshape(F, F)
    return lax.map(one_leaf, (leaf_keys, owners)).astype(jnp.float32)


def draw_root_front(key, part):
    return kernel_front(jax.random.fold_in(key, 31), root_amplitude).astype(jnp.float32)


def setup_inputs(seed: int = 0) -> dict:
    keys = jax.random.split(jax.random.key(seed), 4)
    leaf_fronts = draw_leaf_fronts(jax.random.fold_in(keys[3], 71), 0)
    block_owner = draw_block_owner(jax.random.fold_in(keys[3], 71), 0)
    root_front = draw_root_front(jax.random.fold_in(keys[3], 71), 0)
    return {"leaf_fronts": leaf_fronts, "block_owner": block_owner, "root_front": root_front}


def eliminate(matrix, section_index, slot_index):
    column = lax.dynamic_slice_in_dim(matrix, slot_index * B, B, 1)
    diagonal_block = column[section_index * B:(section_index + 1) * B]
    factor = jnp.linalg.cholesky(diagonal_block)
    panel_rows = lax.linalg.triangular_solve(factor, column, left_side=False, lower=True, transpose_a=True)
    row_ids = jnp.arange(F, dtype=jnp.int32)
    panel_rows = jnp.where((row_ids >= section_index * B)[:, None], panel_rows, jnp.zeros_like(panel_rows))
    return (panel_rows, 2.0 * jnp.sum(jnp.log(jnp.diagonal(factor))))

def leaf_pass(matrix, owner_row):
    slot_ids = jnp.arange(NB, dtype=jnp.int32)
    log_total = jnp.zeros((), jnp.float32)
    for section_index in range(PL):
        slot_index = jnp.sum(jnp.where(owner_row == section_index, slot_ids, 0)).astype(jnp.int32)
        panel_rows, log_sum = eliminate(matrix, section_index, slot_index)
        log_total = log_total + log_sum
        panel_short = panel_rows.astype(jnp.bfloat16)
        across = panel_short.reshape(NB, B, B)[owner_row].reshape(F, B)
        matrix = matrix - jnp.dot(panel_short.astype(jnp.float32), across.T.astype(jnp.float32), preferred_element_type=jnp.float32)
    keep_blocks = owner_row >= PL
    keep_mask = (keep_blocks[:, None] & keep_blocks[None, :]).astype(jnp.float32)
    moved = matrix.reshape(NB, B, F)[owner_row].reshape(NB, B, NB, B)
    extended = moved * keep_mask[:, None, :, None]
    return (extended.reshape(F, F), log_total)

def reference(leaf_fronts, block_owner, root_front):
    root_matrix = root_front
    log_list = []
    for leaf_index in range(LEAVES):
        extended, log_total = leaf_pass(leaf_fronts[leaf_index], block_owner[leaf_index])
        root_matrix = root_matrix + extended
        log_list.append(log_total / (PL * B))
    root_total = jnp.zeros((), jnp.float32)
    panel_list = []
    for section_index in range(PR):
        panel_rows, log_sum = eliminate(root_matrix, section_index, section_index)
        root_total = root_total + log_sum
        panel_short = panel_rows.astype(jnp.bfloat16)
        root_matrix = root_matrix - jnp.dot(panel_short.astype(jnp.float32), panel_short.T.astype(jnp.float32), preferred_element_type=jnp.float32)
        panel_list.append(panel_rows)
    row_ids = jnp.arange(F, dtype=jnp.int32)
    trailing = jnp.where((row_ids >= PR * B)[:, None], root_matrix, jnp.zeros_like(root_matrix))
    root_factor = trailing.at[:, :PR * B].set(jnp.concatenate(panel_list, axis=1))
    log_det = jnp.stack(log_list + [root_total / (PR * B)])
    return (root_factor, log_det)
```

```python
import jax
import jax.numpy as jnp
from jax import lax
from jax.experimental import pallas as pl
from jax.experimental.pallas import tpu as pltpu
from jax.sharding import PartitionSpec as P

PL = 3
PR = 2
HIGHEST = lax.Precision.HIGHEST
SUB = 32


def mm(lhs, rhs):
    return jnp.dot(lhs, rhs, precision=HIGHEST, preferred_element_type=jnp.float32)


def tdot(lhs, rhs):
    return lax.dot_general(
        lhs, rhs, (((0,), (0,)), ((), ())), preferred_element_type=jnp.float32
    )


def bits(size):
    out, bit = [], 1
    while bit < size:
        out.append(bit)
        bit *= 2
    return out


def flip(value, axis, bit):
    size = lax.axis_size(axis)
    return lax.ppermute(value, axis, [(i, i ^ bit) for i in range(size)])


def invert_factor(block, work, inverse_ref):
    size = block.shape[0]
    rows = lax.broadcasted_iota(jnp.int32, (size, size), 0)
    cols = lax.broadcasted_iota(jnp.int32, (size, size), 1)
    work[:, :size] = block
    work[:, size:] = jnp.where(rows == cols, 1.0, 0.0)
    sub = lax.broadcasted_iota(jnp.int32, (SUB, 1), 0)
    sub_full = lax.broadcasted_iota(jnp.int32, (SUB, 2 * size), 0)
    lane = lax.broadcasted_iota(jnp.int32, (SUB, 2 * size), 1)
    log_sum = jnp.zeros((1, 1), jnp.float32)
    for first in range(0, size, SUB):
        part = work[first : first + SUB, :]
        for i in range(SUB - 1):
            at = first + i
            factor = jnp.where(sub > i, part[:, at : at + 1] / part[i : i + 1, at : at + 1], 0.0)
            part = part - factor * part[i : i + 1, :]
        pivot = jnp.sum(jnp.where(lane == sub_full + first, part, 0.0), axis=1, keepdims=True)
        part = part * lax.rsqrt(pivot)
        inverse_ref[first : first + SUB, :] = part[:, size:]
        log_sum = log_sum + jnp.sum(jnp.log(pivot), axis=0, keepdims=True)
        if first + SUB < size:
            update = lax.dot_general(
                part[:, :size], part, (((0,), (0,)), ((), ())),
                precision=HIGHEST, preferred_element_type=jnp.float32,
            )
            work[first + SUB :, :] = work[first + SUB :, :] - update[first + SUB :, :]
    return log_sum


def leaf_first(c0_ref, w_ref, mask_ref, p_ref, inv_ref, log_ref, work):
    b = w_ref.shape[0]
    log_sum = invert_factor(c0_ref[:b, :], work, inv_ref)
    log_ref[...] = jnp.broadcast_to(log_sum, log_ref.shape)
    panel = mm(inv_ref[...], w_ref[...])
    p_ref[...] = jnp.where(mask_ref[...] > 0.0, panel, 0.0).astype(jnp.bfloat16)


def leaf_second(c_ref, w_ref, mask_ref, inv0_ref, p0_ref, p_ref, inv_ref, x01_ref, x02_ref, log_ref, work):
    b = w_ref.shape[0]
    x01 = mm(inv0_ref[...], c_ref[:b, :]).astype(jnp.bfloat16)
    x01_ref[...] = x01
    log_sum = invert_factor(c_ref[b : 2 * b, :] - tdot(x01, x01), work, inv_ref)
    log_ref[...] = jnp.broadcast_to(log_sum, log_ref.shape)
    x02_ref[...] = mm(inv0_ref[...], c_ref[2 * b : 3 * b, :]).astype(jnp.bfloat16)
    panel = mm(inv_ref[...], w_ref[...] - tdot(x01, p0_ref[...]))
    p_ref[...] = jnp.where(mask_ref[...] > 0.0, panel, 0.0).astype(jnp.bfloat16)


def leaf_third(c_ref, w_ref, mask_ref, inv1_ref, x01_ref, x02_ref, p0_ref, p1_ref, p_ref, inv_ref, log_ref, work):
    b = w_ref.shape[0]
    x02 = x02_ref[...]
    x12 = mm(inv1_ref[...], c_ref[3 * b : 4 * b, :] - tdot(x01_ref[...], x02)).astype(jnp.bfloat16)
    block = c_ref[4 * b : 5 * b, :] - tdot(x02, x02) - tdot(x12, x12)
    log_sum = invert_factor(block, work, inv_ref)
    log_ref[...] = jnp.broadcast_to(log_sum, log_ref.shape)
    panel = mm(inv_ref[...], w_ref[...] - tdot(x02, p0_ref[...]) - tdot(x12, p1_ref[...]))
    p_ref[...] = jnp.where(mask_ref[...] > 0.0, panel, 0.0).astype(jnp.bfloat16)


def root_both(t_ref, inv0_ref, inv1_ref, x_ref, log_ref, work):
    b = inv0_ref.shape[0]
    log0 = invert_factor(t_ref[:b, :b], work, inv0_ref)
    x = mm(inv0_ref[...], t_ref[:b, b:]).astype(jnp.bfloat16)
    x_ref[...] = x
    log1 = invert_factor(t_ref[b:, b:] - tdot(x, x), work, inv1_ref)
    log_ref[...] = jnp.broadcast_to(log0 + log1, log_ref.shape)


def permute_rows(source_ref, keep_ref, front_ref, mask_ref, near_ref, far_ref):
    step = pl.program_id(0)
    near_steps = 2 * pl.num_programs(0) // 3
    value = jnp.where(mask_ref[...] > 0.0, front_ref[...], 0.0)
    value = jnp.where(keep_ref[step] > 0, value, 0.0)

    @pl.when(step < near_steps)
    def _():
        near_ref[...] = value

    @pl.when(step >= near_steps)
    def _():
        far_ref[...] = value


def shape(dims, dtype):
    return jax.ShapeDtypeStruct(dims, dtype)


def local(leaf_fronts, block_owner, root_front):
    f32, bf16 = jnp.float32, jnp.bfloat16
    members = lax.axis_size("mem")
    groups = lax.axis_size("grp")
    m = lax.axis_index("mem")
    g = lax.axis_index("grp")
    front = leaf_fronts[0]
    order, cols = front.shape
    owner = block_owner[0]
    per = owner.shape[0]
    b = cols // per
    count = order // b
    quarter = order // groups
    spread = members // groups
    quarter_blocks = quarter // b
    pr = PR * b
    core, chip = 1, 2

    w = front[: PL * b]
    w_blocks = w.reshape(PL * b, per, b)
    picks = []
    for k in range(PL):
        hold = (owner == k)[None, :, None]
        picks.append(jnp.sum(jnp.where(hold, w_blocks[: (k + 1) * b], 0.0), axis=1))
    slot = jnp.arange(b, dtype=jnp.int32)
    mine = jnp.zeros((b,), f32)
    for t in range(per):
        mine = mine + jnp.where(slot == m * per + t, owner[t].astype(f32), 0.0)
    table_rows = jnp.broadcast_to(mine[None, :], (8, b))
    head = jnp.concatenate([picks[0], table_rows], axis=0)
    rest = jnp.concatenate([picks[1], picks[2]], axis=0)
    for bit in bits(members):
        head = head + flip(head, "mem", bit)
    for bit in bits(members):
        rest = rest + flip(rest, "mem", bit)
    table = head[b, :count].astype(jnp.int32)
    keep_cols = jnp.repeat(owner >= PL, b, total_repeat_length=cols)
    mask = jnp.where(keep_cols, 1.0, 0.0).astype(f32)[None, :]

    work = [pltpu.VMEM((b, 2 * b), f32)]
    sq = shape((b, b), f32)
    sqh = shape((b, b), bf16)
    wide = shape((b, cols), bf16)
    logs = shape((8, b), f32)
    p0, inv0, log0 = pl.pallas_call(
        leaf_first, out_shape=(wide, sq, logs), scratch_shapes=work, name="leaf_first"
    )(head, w[:b], mask)
    p1, inv1, x01, x02, log1 = pl.pallas_call(
        leaf_second, out_shape=(wide, sq, sqh, sqh, logs), scratch_shapes=work, name="leaf_second"
    )(jnp.concatenate([rest[: 2 * b], rest[2 * b : 3 * b]], axis=0), w[b : 2 * b], mask, inv0, p0)
    p2, _, log2 = pl.pallas_call(
        leaf_third, out_shape=(wide, sq, logs), scratch_shapes=work, name="leaf_third"
    )(rest, w[2 * b :], mask, inv1, x01, x02, p0, p1)
    panels = [p0, p1, p2]
    leaf_log = (log0 + log1 + log2) / (PL * b)

    starts = [g ^ core, g ^ (core | chip), g ^ chip, g]
    places = jnp.concatenate([s * quarter_blocks + jnp.arange(quarter_blocks) for s in starts])
    source = jnp.take(table, places)
    kept = (source >= PL).astype(jnp.int32)
    steps = 3 * quarter_blocks
    near_steps = 2 * quarter_blocks
    near, far = pl.pallas_call(
        permute_rows,
        grid_spec=pltpu.PrefetchScalarGridSpec(
            num_scalar_prefetch=2,
            grid=(steps,),
            in_specs=[
                pl.BlockSpec((b, cols), lambda i, s, k: (s[i], 0)),
                pl.BlockSpec((1, cols), lambda i, s, k: (0, 0)),
            ],
            out_specs=[
                pl.BlockSpec((b, cols), lambda i, s, k: (jnp.minimum(i, near_steps - 1), 0)),
                pl.BlockSpec((b, cols), lambda i, s, k: (jnp.maximum(i - near_steps, 0), 0)),
            ],
        ),
        out_shape=(shape((2 * quarter, cols), f32), shape((quarter, cols), f32)),
        name="permute_rows",
    )(source, kept, front, mask)
    near = flip(near, "grp", core)
    far = far + near[quarter:]
    far = flip(far, "grp", chip)
    own_rows = jnp.concatenate(
        [
            jnp.where(
                (source[3 * quarter_blocks + i] >= PL) & keep_cols[None, :],
                lax.dynamic_slice_in_dim(front, source[3 * quarter_blocks + i] * b, b, 0),
                0.0,
            )
            for i in range(quarter_blocks)
        ],
        axis=0,
    )
    base = root_front + own_rows + near[:quarter] + far

    def to_rows(value):
        zone, inner = m // spread, m % spread
        held = value
        have = [0]
        for bit in reversed(bits(groups)):
            pairs = []
            for gi in range(groups):
                for h in have:
                    for j in range(spread):
                        src = (gi ^ h) * spread + j
                        dst = (gi ^ h ^ bit) * spread + j
                        pairs.append((gi * members + src, gi * members + dst))
            got = lax.ppermute(value if len(have) == 1 else held, ("grp", "mem"), pairs)
            new = [h ^ bit for h in have]
            is_new = jnp.zeros((), jnp.bool_)
            for h in new:
                is_new = is_new | (zone == (g ^ h))
            held = jnp.where(is_new, got, held)
            have = have + new
        slots = [held]
        for i in range(1, spread):
            slots.append(flip(held, "mem", i))
        return slots

    lead_cols = min(pr, cols)
    leads = pr // lead_cols

    def from_first(value):
        value = value[:, :lead_cols]
        parts = []
        for root in range(leads):
            held = value
            for bit in reversed(bits(members)):
                pairs = [(root ^ i, root ^ i ^ bit) for i in range(0, members, 2 * bit)]
                got = lax.ppermute(held, "mem", pairs)
                held = jnp.where((m ^ root) % (2 * bit) == bit, got, held)
            parts.append(held)
        return parts[0] if leads == 1 else jnp.concatenate(parts, axis=1)

    def across(value):
        far_value = flip(value, "grp", chip)
        both = jnp.concatenate([value, far_value], axis=0)
        return jnp.concatenate([both, flip(both, "grp", core)], axis=0)

    first = jnp.concatenate(
        [
            jnp.where(
                (table[i] >= PL) & keep_cols[None, :],
                lax.dynamic_slice_in_dim(front, table[i] * b, b, 0),
                0.0,
            )
            for i in range(PR)
        ],
        axis=0,
    )
    first = first + jnp.where(g == 0, root_front[:pr], 0.0)
    first = first + flip(first, "grp", core)
    first = first + flip(first, "grp", chip)
    first_rows = to_rows(first)
    corner = from_first(first)

    col_panels, row_panels = [], []
    for panel in panels:
        whole = across(panel)
        lead = across(from_first(panel))
        col_panels.append(whole)
        row_panels.append(to_rows(whole))
        corner = corner - tdot(lead, lead)
        first = first - tdot(lead, whole)
        first_rows = [f - tdot(lead, z) for f, z in zip(first_rows, row_panels[-1])]

    rinv0, rinv1, rx, root_log = pl.pallas_call(
        root_both, out_shape=(sq, sq, sqh, logs), scratch_shapes=work, name="root_both"
    )(corner)
    root_log = root_log / pr

    def root_panel(t):
        q0 = mm(rinv0, t[:b])
        q1 = mm(rinv1, t[b:] - tdot(rx, q0.astype(bf16)))
        return q0, q1

    c0, c1 = root_panel(first)
    short_cols = jnp.concatenate([c0, c1], axis=0).astype(bf16)
    inner = m % spread
    outs = []
    for i in range(spread):
        q0, q1 = root_panel(first_rows[i])
        short_rows = jnp.concatenate([q0, q1], axis=0).astype(bf16)
        total = tdot(short_rows, short_cols)
        for k in range(PL):
            total = total + tdot(row_panels[k][i], col_panels[k])
        row0 = g * quarter + (inner ^ i) * cols
        part = lax.dynamic_slice_in_dim(base, (inner ^ i) * cols, cols, 0) - total
        rows = row0 + jnp.arange(cols)
        part = jnp.where((rows >= pr)[:, None], part, 0.0)
        keep1 = (rows >= b)[:, None]
        panel_part = jnp.concatenate([q0.T, jnp.where(keep1, q1.T, 0.0)], axis=1)
        first_col = jnp.minimum(m, leads - 1) * lead_cols
        panel_part = lax.dynamic_slice_in_dim(panel_part, first_col, lead_cols, 1)
        head_cols = jnp.where(m < leads, panel_part, part[:, :lead_cols])
        outs.append(jnp.concatenate([head_cols, part[:, lead_cols:]], axis=1))
    root_factor = jnp.zeros((quarter, cols), f32)
    for i in range(spread):
        root_factor = lax.dynamic_update_slice_in_dim(root_factor, outs[i], (inner ^ i) * cols, 0)

    all_logs = leaf_log[:1, :1]
    far_log = flip(leaf_log, "grp", chip)
    near_log = flip(leaf_log, "grp", core)
    diag_log = flip(near_log, "grp", chip)
    by_flip = [leaf_log[0, 0], near_log[0, 0], far_log[0, 0], diag_log[0, 0]]
    log_list = []
    for leaf in range(groups):
        total = jnp.zeros((), f32)
        for q in range(groups):
            total = total + jnp.where((g ^ q) == leaf, by_flip[q], 0.0)
        log_list.append(total)
    log_det = jnp.stack(log_list + [root_log[0, 0]])
    return root_factor, log_det


def solution(mesh):
    in_specs = (P("grp", None, "mem"), P("grp", "mem"), P("grp", "mem"))
    out_specs = (P("grp", "mem"), P())
    return jax.shard_map(local, mesh=mesh, in_specs=in_specs, out_specs=out_specs, check_vma=False)
```

```python
import jax
import jax.numpy as jnp
from jax import lax
from jax.experimental import pallas as pl
from jax.experimental.pallas import tpu as pltpu
from jax.sharding import PartitionSpec as P

PL = 3
PR = 2
HIGHEST = lax.Precision.HIGHEST
ROWS = 64
SUB = 16
LOG_ROWS = 16
CORE, CHIP = 1, 2
f32, bf16 = jnp.float32, jnp.bfloat16


def mm(lhs, rhs):
    return jnp.dot(lhs, rhs, precision=HIGHEST, preferred_element_type=f32)


def mm_t(lhs, rhs):
    return lax.dot_general(
        lhs, rhs, (((1,), (1,)), ((), ())), precision=HIGHEST, preferred_element_type=f32
    )


def tdot(lhs, rhs):
    return lax.dot_general(lhs, rhs, (((0,), (0,)), ((), ())), preferred_element_type=f32)


def bits(size):
    out, bit = [], 1
    while bit < size:
        out.append(bit)
        bit *= 2
    return out


def flip(value, axis, bit):
    size = lax.axis_size(axis)
    return lax.ppermute(value, axis, [(i, i ^ bit) for i in range(size)])


def shape(dims, dtype):
    return jax.ShapeDtypeStruct(dims, dtype)


def cost(us):
    return pl.CostEstimate(flops=0, bytes_accessed=int(us * 3.0e6), transcendentals=0)


def invert_factor(block, work, inverse_ref):
    size = block.shape[0]
    rows = lax.broadcasted_iota(jnp.int32, (size, size), 0)
    cols = lax.broadcasted_iota(jnp.int32, (size, size), 1)
    work[:, :size] = block
    work[:, size:] = jnp.where(rows == cols, 1.0, 0.0)
    sub = lax.broadcasted_iota(jnp.int32, (ROWS, size), 0)
    lane = lax.broadcasted_iota(jnp.int32, (ROWS, size), 1)
    log_sum = jnp.zeros((1, 1), f32)
    for first in range(0, size, ROWS):
        left = work[first : first + ROWS, :size]
        right = work[first : first + ROWS, size:]
        for start in range(0, ROWS, SUB):
            at = first + start
            columns = [
                jnp.broadcast_to(left[:, at + j : at + j + 1], (ROWS, size)) for j in range(SUB)
            ]
            for j in range(SUB):
                i = start + j
                if i == ROWS - 1:
                    break
                factor = jnp.where(sub > i, columns[j], 0.0) * (1.0 / columns[j][i : i + 1, :])
                for k in range(j + 1, SUB):
                    columns[k] = columns[k] - factor * columns[k][i : i + 1, :]
                left = left - factor * left[i : i + 1, :]
                right = right - factor * right[i : i + 1, :]
        pivot = jnp.sum(jnp.where(lane == sub + first, left, 0.0), axis=1, keepdims=True)
        scale = lax.rsqrt(pivot)
        left, right = left * scale, right * scale
        inverse_ref[first : first + ROWS, :] = right
        log_sum = log_sum + jnp.sum(jnp.log(pivot), axis=0, keepdims=True)
        if first + ROWS < size:
            update = lax.dot_general(
                left, jnp.concatenate([left, right], axis=1), (((0,), (0,)), ((), ())),
                precision=HIGHEST, preferred_element_type=f32,
            )
            work[first + ROWS :, :] = work[first + ROWS :, :] - update[first + ROWS :, :]
    return log_sum


def pick_pivots(owner_ref, at_ref, front_ref, head_ref, rest_ref, mask_ref):
    b = head_ref.shape[1]
    per = front_ref.shape[1] // b
    for k in range(PL):
        total = jnp.zeros(((k + 1) * b, b), f32)
        for t in range(per):
            part = front_ref[: (k + 1) * b, t * b : (t + 1) * b]
            total = total + jnp.where(owner_ref[t] == k, part, 0.0)
        if k == 0:
            head_ref[:b, :] = total
        elif k == 1:
            rest_ref[: 2 * b, :] = total
        else:
            rest_ref[2 * b :, :] = total
    lane = lax.broadcasted_iota(jnp.int32, (8, b), 1)
    table = jnp.zeros((8, b), f32)
    for t in range(per):
        table = table + jnp.where(lane == at_ref[0] + t, owner_ref[t].astype(f32), 0.0)
        keep = jnp.where(owner_ref[t] >= PL, 1.0, 0.0).astype(f32)
        mask_ref[:, t * b : (t + 1) * b] = jnp.full((8, b), keep, f32)
    head_ref[b:, :] = table


def leaf_first(head_ref, w_ref, mask_ref, p_ref, inv_ref, log_ref, work):
    b = w_ref.shape[0]
    log_sum = invert_factor(head_ref[:b, :], work, inv_ref)
    log_ref[...] = jnp.broadcast_to(log_sum, log_ref.shape)
    panel = mm(inv_ref[...], w_ref[...])
    p_ref[...] = jnp.where(mask_ref[:1, :] > 0.0, panel, 0.0).astype(bf16)


def leaf_others(
    rest_ref, w1_ref, w2_ref, mask_ref, inv0_ref, p0_ref, log0_ref, p_ref, log_ref, inv, work
):
    b = w1_ref.shape[0]
    c01, c11, c02, c12, c22 = [rest_ref[i * b : (i + 1) * b, :] for i in range(5)]
    keep = mask_ref[:1, :] > 0.0
    p0 = p0_ref[...]
    x01 = mm(inv0_ref[...], c01).astype(bf16)
    log1 = invert_factor(c11 - tdot(x01, x01), work, inv)
    x02 = mm(inv0_ref[...], c02).astype(bf16)
    panel = mm(inv[...], w1_ref[...] - tdot(x01, p0))
    p1 = jnp.where(keep, panel, 0.0).astype(bf16)
    p_ref[:b, :] = p1
    x12 = mm(inv[...], c12 - tdot(x01, x02)).astype(bf16)
    log2 = invert_factor(c22 - tdot(x02, x02) - tdot(x12, x12), work, inv)
    panel = mm(inv[...], w2_ref[...] - tdot(x02, p0) - tdot(x12, p1))
    p_ref[b:, :] = jnp.where(keep, panel, 0.0).astype(bf16)
    log_ref[...] = log0_ref[...] + jnp.broadcast_to(log1 + log2, log_ref.shape)


def gather_rows(ways, near_steps, *refs):
    source_ref, keep_ref = refs[:2]
    fronts = refs[2 : 2 + ways]
    mask_ref, near_ref, far_ref = refs[2 + ways :]
    step = pl.program_id(0)
    b = fronts[0].shape[0]
    keep_cols = mask_ref[:1, :] > 0.0

    def store(out_ref):
        for i, front_ref in enumerate(fronts):
            keep = keep_cols & (keep_ref[step * ways + i] > 0)
            out_ref[i * b : (i + 1) * b, :] = jnp.where(keep, front_ref[...], 0.0)

    pl.when(step < near_steps)(lambda: store(near_ref))
    pl.when(step >= near_steps)(lambda: store(far_ref))


def add_rows(ways, with_near, *refs):
    source_ref, keep_ref, scale_ref = refs[:3]
    fronts = refs[3 : 3 + ways]
    mask_ref, root_ref = refs[3 + ways : 5 + ways]
    out_ref = refs[-1]
    step = pl.program_id(0)
    b = fronts[0].shape[0]
    keep_cols = mask_ref[:1, :] > 0.0
    for i, front_ref in enumerate(fronts):
        keep = keep_cols & (keep_ref[step * ways + i] > 0)
        at = slice(i * b, (i + 1) * b)
        total = jnp.where(scale_ref[0] > 0, root_ref[at, :], 0.0)
        total = total + jnp.where(keep, front_ref[...], 0.0)
        if with_near:
            total = total + refs[5 + ways][at, :]
        out_ref[at, :] = total


def root_step(
    corner_ref, lead_ref, first_ref, d0_ref, d12_ref,
    q_ref, inv0_ref, inv1_ref, x_ref, log_ref, work,
):
    b = inv0_ref.shape[0]
    groups = d0_ref.shape[0] // b
    pitch = lead_ref.shape[0] // groups
    corner = corner_ref[...]
    top = first_ref[...]
    for q in range(groups):
        lead = lead_ref[q * pitch : q * pitch + PL * b, :]
        corner = corner - tdot(lead, lead)
        top = top - tdot(lead[:b, :], d0_ref[q * b : (q + 1) * b, :])
        top = top - tdot(lead[b:, :], d12_ref[q * 2 * b : (q + 1) * 2 * b, :])
    log0 = invert_factor(corner[:b, :b], work, inv0_ref)
    x = mm(inv0_ref[...], corner[:b, b:]).astype(bf16)
    x_ref[...] = x
    log1 = invert_factor(corner[b:, b:] - tdot(x, x), work, inv1_ref)
    log_ref[...] = jnp.broadcast_to(log0 + log1, log_ref.shape)
    q0 = mm(inv0_ref[...], top[:b, :]).astype(bf16)
    q_ref[:b, :] = q0
    q_ref[b:, :] = mm(inv1_ref[...], top[b:, :] - tdot(x, q0)).astype(bf16)


def local(leaf_fronts, block_owner, root_front):
    members = lax.axis_size("mem")
    groups = lax.axis_size("grp")
    m = lax.axis_index("mem")
    g = lax.axis_index("grp")
    front = leaf_fronts[0]
    order, cols = front.shape
    owner = block_owner[0]
    per = owner.shape[0]
    b = cols // per
    count = order // b
    quarter = order // groups
    spread = members // groups
    quarter_blocks = quarter // b
    pr = PR * b
    lead_cols = min(pr, cols)
    leads = pr // lead_cols
    zone, inner = m // spread, m % spread
    smem = pl.BlockSpec(memory_space=pltpu.SMEM)
    vmem = pl.BlockSpec(memory_space=pltpu.VMEM)

    head, rest, mask = pl.pallas_call(
        pick_pivots,
        grid=(1,),
        in_specs=[smem, smem, pl.BlockSpec((PL * b, cols), lambda i: (0, 0))],
        out_specs=[vmem, vmem, vmem],
        out_shape=(shape((b + 8, b), f32), shape((5 * b, b), f32), shape((8, cols), f32)),
        name="pick_pivots",
    )(owner, (m * per).reshape(1), front)
    for bit in bits(members):
        head = head + flip(head, "mem", bit)
    for bit in bits(members):
        rest = rest + flip(rest, "mem", bit)
    table = head[b, :count].astype(jnp.int32)

    starts = [g ^ CORE, g ^ (CORE | CHIP), g ^ CHIP, g]
    places = jnp.concatenate(
        [s * quarter_blocks + jnp.arange(quarter_blocks) for s in starts] + [jnp.arange(PR)]
    )
    source = jnp.take(table, places)
    kept = (source >= PL).astype(jnp.int32)
    ways = 4
    sent = 3 * quarter_blocks
    near_steps = 2 * quarter_blocks // ways
    steps = sent // ways

    def front_spec(i, n):
        return pl.BlockSpec((b, cols), lambda s, *pre, i=i: (pre[0][s * n + i], 0))

    mask_spec = pl.BlockSpec((8, cols), lambda s, *pre: (0, 0))
    tall = (ways * b, cols)

    def gather_kernel(*refs):
        gather_rows(ways, near_steps, *refs)

    near, far = pl.pallas_call(
        gather_kernel,
        grid_spec=pltpu.PrefetchScalarGridSpec(
            num_scalar_prefetch=2,
            grid=(steps,),
            in_specs=[front_spec(i, ways) for i in range(ways)] + [mask_spec],
            out_specs=[
                pl.BlockSpec(tall, lambda s, *pre: (jnp.minimum(s, near_steps - 1), 0)),
                pl.BlockSpec(tall, lambda s, *pre: (jnp.maximum(s - near_steps, 0), 0)),
            ],
        ),
        out_shape=(shape((2 * quarter, cols), f32), shape((quarter, cols), f32)),
        cost_estimate=cost(6),
        name="gather_rows",
    )(source[:sent], kept[:sent], *([front] * ways), mask)
    near = flip(near, "grp", CORE)

    def first_kernel(*refs):
        add_rows(PR, False, *refs)

    first = pl.pallas_call(
        first_kernel,
        grid_spec=pltpu.PrefetchScalarGridSpec(
            num_scalar_prefetch=3,
            grid=(1,),
            in_specs=[front_spec(i, PR) for i in range(PR)]
            + [mask_spec, pl.BlockSpec((pr, cols), lambda s, *pre: (0, 0))],
            out_specs=pl.BlockSpec((pr, cols), lambda s, *pre: (0, 0)),
        ),
        out_shape=shape((pr, cols), f32),
        cost_estimate=cost(2),
        name="first_rows",
    )(
        source[sent + quarter_blocks :], kept[sent + quarter_blocks :],
        (g == 0).astype(jnp.int32).reshape(1), *([front] * PR), mask, root_front,
    )
    first = first + flip(first, "grp", CORE)
    first = first + flip(first, "grp", CHIP)

    work = [pltpu.VMEM((b, 2 * b), f32)]
    sq = shape((b, b), f32)
    sqh = shape((b, b), bf16)
    logs = shape((8, b), f32)

    def w_spec(k):
        return pl.BlockSpec((b, cols), lambda i: (k, 0))

    p0, inv0, log0 = pl.pallas_call(
        leaf_first,
        grid=(1,),
        in_specs=[vmem, w_spec(0), vmem],
        out_specs=[vmem, vmem, vmem],
        out_shape=(shape((b, cols), bf16), sq, logs),
        scratch_shapes=work,
        cost_estimate=cost(6),
        name="leaf_first",
    )(head, front, mask)

    far = far + near[quarter:]
    rest, far = lax.optimization_barrier((rest, far))
    far = flip(far, "grp", CHIP)

    p12, leaf_log = pl.pallas_call(
        leaf_others,
        grid=(1,),
        in_specs=[vmem, w_spec(1), w_spec(2), vmem, vmem, vmem, vmem],
        out_specs=[vmem, vmem],
        out_shape=(shape((2 * b, cols), bf16), logs),
        scratch_shapes=[pltpu.VMEM((b, b), f32)] + work,
        cost_estimate=cost(12),
        name="leaf_others",
    )(rest, front, front, mask, inv0, p0, log0)

    def base_kernel(*refs):
        add_rows(ways, True, *refs)

    base = pl.pallas_call(
        base_kernel,
        grid_spec=pltpu.PrefetchScalarGridSpec(
            num_scalar_prefetch=3,
            grid=(quarter_blocks // ways,),
            in_specs=[front_spec(i, ways) for i in range(ways)]
            + [mask_spec]
            + [pl.BlockSpec(tall, lambda s, *pre: (s, 0))] * 2,
            out_specs=pl.BlockSpec(tall, lambda s, *pre: (s, 0)),
        ),
        out_shape=shape((quarter, cols), f32),
        cost_estimate=cost(4),
        name="base_rows",
    )(
        source[sent : sent + quarter_blocks], kept[sent : sent + quarter_blocks],
        jnp.ones((1,), jnp.int32), *([front] * ways), mask, root_front, near,
    )

    def to_rows(value):
        stages = [([0], value)]
        held = value
        for bit in reversed(bits(groups)):
            have = [h for offsets, _ in stages for h in offsets]
            pairs = []
            for gi in range(groups):
                for h in have:
                    for j in range(spread):
                        src = (gi ^ h) * spread + j
                        dst = (gi ^ h ^ bit) * spread + j
                        pairs.append((gi * members + src, gi * members + dst))
            got = lax.ppermute(held, ("grp", "mem"), pairs)
            new = [h ^ bit for h in have]
            held = jnp.where(among(new), got, held)
            stages.append((new, got))
        slots = [held]
        for i in range(1, spread):
            part = None
            for offsets, sent_part in stages:
                pairs = []
                for gi in range(groups):
                    for h in offsets:
                        for j in range(spread):
                            at = gi * members + (gi ^ h) * spread
                            pairs.append((at + j, at + (j ^ i)))
                got = lax.ppermute(sent_part, ("grp", "mem"), pairs)
                part = got if part is None else jnp.where(among(offsets), got, part)
            slots.append(part)
        return slots

    def among(offsets):
        found = jnp.zeros((), jnp.bool_)
        for h in offsets:
            found = found | (zone == (g ^ h))
        return found

    def from_first(value):
        value = value[:, :lead_cols]
        parts = []
        for root in range(leads):
            held = value
            for bit in reversed(bits(members)):
                pairs = [(root ^ i, root ^ i ^ bit) for i in range(0, members, 2 * bit)]
                got = lax.ppermute(held, "mem", pairs)
                held = jnp.where((m ^ root) % (2 * bit) == bit, got, held)
            parts.append(held)
        return parts[0] if leads == 1 else jnp.concatenate(parts, axis=1)

    def across(value):
        far_value = flip(value, "grp", CHIP)
        both = jnp.concatenate([value, far_value], axis=0)
        return jnp.concatenate([both, flip(both, "grp", CORE)], axis=0)

    corner = from_first(first)
    d0 = across(p0)
    r0 = to_rows(d0)

    log_value = leaf_log[:1, :1]
    parts = []
    for _ in range(3):
        parts.append(log_value.astype(bf16))
        log_value = log_value - parts[-1].astype(f32)
    line = lax.broadcasted_iota(jnp.int32, (LOG_ROWS, lead_cols), 0)
    log_block = jnp.zeros((LOG_ROWS, lead_cols), bf16)
    for i, part in enumerate(parts):
        log_block = jnp.where(line == i, part, log_block)
    lead = jnp.concatenate([p0[:, :lead_cols], p12[:, :lead_cols], log_block], axis=0)
    lead = across(from_first(lead))
    d12 = across(p12)
    r12 = to_rows(d12)

    q, rinv0, rinv1, rx, root_log = pl.pallas_call(
        root_step,
        out_shape=(shape((pr, cols), bf16), sq, sq, sqh, logs),
        scratch_shapes=work,
        cost_estimate=cost(18),
        name="root_step",
    )(corner, lead, first, d0, d12)
    rq = to_rows(q)

    root_factor = jnp.zeros((quarter, cols), f32)
    for i in range(spread):
        start = (inner ^ i) * cols
        rows = g * quarter + start + jnp.arange(cols)
        part = lax.dynamic_slice_in_dim(base, start, cols, 0)
        part = part + lax.dynamic_slice_in_dim(far, start, cols, 0)
        part = part - tdot(r0[i], d0) - tdot(r12[i], d12)
        if leads == 1:
            q0 = mm_t(part[:, :b], rinv0)
            inside = part[:, b:pr] - jnp.dot(q0.astype(bf16), rx, preferred_element_type=f32)
            q1 = mm_t(inside, rinv1)
        else:
            q0, q1 = rq[i][:b].T.astype(f32), rq[i][b:].T.astype(f32)
        q1 = jnp.where((rows >= b)[:, None], q1, 0.0)
        panel = jnp.concatenate([q0, q1], axis=1)
        first_col = jnp.minimum(m, leads - 1) * lead_cols
        panel = lax.dynamic_slice_in_dim(panel, first_col, lead_cols, 1)
        part = jnp.where((rows >= pr)[:, None], part - tdot(rq[i], q), 0.0)
        head_cols = jnp.where(m < leads, panel, part[:, :lead_cols])
        part = jnp.concatenate([head_cols, part[:, lead_cols:]], axis=1)
        root_factor = lax.dynamic_update_slice_in_dim(root_factor, part, start, 0)

    pitch = lead.shape[0] // groups
    sums = [
        jnp.sum(lead[t * pitch + PL * b : t * pitch + PL * b + 3, 0].astype(f32))
        for t in range(groups)
    ]
    order_of = [0, CHIP, CORE, CORE | CHIP]
    log_list = []
    for leaf in range(groups):
        total = jnp.zeros((), f32)
        for at, bit in enumerate(order_of):
            total = total + jnp.where((g ^ bit) == leaf, sums[at], 0.0)
        log_list.append(total / (PL * b))
    log_det = jnp.stack(log_list + [root_log[0, 0] / pr])
    return root_factor, log_det


def solution(mesh):
    in_specs = (P("grp", None, "mem"), P("grp", "mem"), P("grp", "mem"))
    out_specs = (P("grp", "mem"), P())
    return jax.shard_map(local, mesh=mesh, in_specs=in_specs, out_specs=out_specs, check_vma=False)
```

```python
import jax
import jax.numpy as jnp
from jax import lax
from jax.experimental import pallas as pl
from jax.experimental.pallas import tpu as pltpu
from jax.sharding import PartitionSpec as P

PL = 3
PR = 2
HIGHEST = lax.Precision.HIGHEST
ROWS = 64
SUB = 16
LOG_ROWS = 16
CORE, CHIP = 1, 2
f32, bf16 = jnp.float32, jnp.bfloat16


def mm(lhs, rhs):
    return jnp.dot(lhs, rhs, precision=HIGHEST, preferred_element_type=f32)


def mm_t(lhs, rhs):
    return lax.dot_general(
        lhs, rhs, (((1,), (1,)), ((), ())), precision=HIGHEST, preferred_element_type=f32
    )


def tdot(lhs, rhs):
    return lax.dot_general(lhs, rhs, (((0,), (0,)), ((), ())), preferred_element_type=f32)


def bits(size):
    out, bit = [], 1
    while bit < size:
        out.append(bit)
        bit *= 2
    return out


def flip(value, axis, bit):
    size = lax.axis_size(axis)
    return lax.ppermute(value, axis, [(i, i ^ bit) for i in range(size)])


def shape(dims, dtype):
    return jax.ShapeDtypeStruct(dims, dtype)


def invert_factor(block, work, inverse_ref):
    size = block.shape[0]
    rows = lax.broadcasted_iota(jnp.int32, (size, size), 0)
    cols = lax.broadcasted_iota(jnp.int32, (size, size), 1)
    work[:, :size] = block
    work[:, size:] = jnp.where(rows == cols, 1.0, 0.0)
    sub = lax.broadcasted_iota(jnp.int32, (ROWS, size), 0)
    lane = lax.broadcasted_iota(jnp.int32, (ROWS, size), 1)
    log_sum = jnp.zeros((1, 1), f32)
    for first in range(0, size, ROWS):
        left = work[first : first + ROWS, :size]
        right = work[first : first + ROWS, size:]
        for start in range(0, ROWS, SUB):
            at = first + start
            columns = [
                jnp.broadcast_to(left[:, at + j : at + j + 1], (ROWS, size)) for j in range(SUB)
            ]
            for j in range(SUB):
                i = start + j
                if i == ROWS - 1:
                    break
                factor = jnp.where(sub > i, columns[j], 0.0) * (1.0 / columns[j][i : i + 1, :])
                for k in range(j + 1, SUB):
                    columns[k] = columns[k] - factor * columns[k][i : i + 1, :]
                left = left - factor * left[i : i + 1, :]
                right = right - factor * right[i : i + 1, :]
        pivot = jnp.sum(jnp.where(lane == sub + first, left, 0.0), axis=1, keepdims=True)
        scale = lax.rsqrt(pivot)
        left, right = left * scale, right * scale
        inverse_ref[first : first + ROWS, :] = right
        log_sum = log_sum + jnp.sum(jnp.log(pivot), axis=0, keepdims=True)
        if first + ROWS < size:
            update = lax.dot_general(
                left, jnp.concatenate([left, right], axis=1), (((0,), (0,)), ((), ())),
                precision=HIGHEST, preferred_element_type=f32,
            )
            work[first + ROWS :, :] = work[first + ROWS :, :] - update[first + ROWS :, :]
    return log_sum


def pick_pivots(owner_ref, at_ref, front_ref, table_ref, head_ref, rest_ref, mask_ref, lead_ref):
    b = head_ref.shape[1]
    per = front_ref.shape[1] // b
    for k in range(PL):
        total = jnp.zeros(((k + 1) * b, b), f32)
        for t in range(per):
            part = front_ref[: (k + 1) * b, t * b : (t + 1) * b]
            total = total + jnp.where(owner_ref[t] == k, part, 0.0)
        if k == 0:
            head_ref[:b, :] = total
        elif k == 1:
            head_ref[b:, :] = total
        else:
            rest_ref[...] = total
    lane = lax.broadcasted_iota(jnp.int32, (8, b), 1)
    table = jnp.zeros((8, b), f32)
    for t in range(per):
        table = table + jnp.where(lane == at_ref[0] + t, owner_ref[t].astype(f32), 0.0)
        keep = jnp.where(owner_ref[t] >= PL, 1.0, 0.0).astype(f32)
        mask_ref[:, t * b : (t + 1) * b] = jnp.full((8, b), keep, f32)
    table_ref[...] = table
    lead_ref[...] = front_ref[:, : lead_ref.shape[1]]


def leaf_two(head_ref, w0_ref, w1_ref, mask_ref, p_ref, inv0_ref, inv1_ref, x_ref, log_ref, work):
    b = w0_ref.shape[0]
    c00, c01, c11 = [head_ref[i * b : (i + 1) * b, :] for i in range(3)]
    keep = mask_ref[:1, :] > 0.0
    log0 = invert_factor(c00, work, inv0_ref)
    x01 = mm(inv0_ref[...], c01).astype(bf16)
    x_ref[...] = x01
    p0 = mm(inv0_ref[...], w0_ref[...]).astype(bf16)
    log1 = invert_factor(c11 - tdot(x01, x01), work, inv1_ref)
    p1 = mm(inv1_ref[...], w1_ref[...] - tdot(x01, p0)).astype(bf16)
    p_ref[:b, :] = jnp.where(keep, p0, jnp.zeros_like(p0))
    p_ref[b:, :] = jnp.where(keep, p1, jnp.zeros_like(p1))
    log_ref[...] = jnp.broadcast_to(log0 + log1, log_ref.shape)


def leaf_last(
    rest_ref, w2_ref, w_lead_ref, table_ref, mask_ref, p_ref, inv0_ref, inv1_ref, x_ref, log_ref,
    p2_ref, lead_ref, inv, work,
):
    b = w2_ref.shape[0]
    wide = lead_ref.shape[1]
    c02, c12, c22 = [rest_ref[i * b : (i + 1) * b, :] for i in range(3)]
    inv0, inv1, x01 = inv0_ref[...], inv1_ref[...], x_ref[...]
    x02 = mm(inv0, c02).astype(bf16)
    x12 = mm(inv1, c12 - tdot(x01, x02)).astype(bf16)
    log2 = invert_factor(c22 - tdot(x02, x02) - tdot(x12, x12), work, inv)
    inv2 = inv[...]
    keep = mask_ref[:1, :] > 0.0
    panel = mm(inv2, w2_ref[...] - tdot(x02, p_ref[:b, :]) - tdot(x12, p_ref[b:, :])).astype(bf16)
    p2_ref[...] = jnp.where(keep, panel, jnp.zeros_like(panel))
    lane = lax.broadcasted_iota(jnp.int32, (1, wide), 1)
    block = jnp.zeros((1, wide), f32)
    for t in range(PR):
        inside = (lane >= t * b) & (lane < (t + 1) * b)
        block = jnp.where(inside, table_ref[:1, t : t + 1], block)
    keep = block > PL - 0.5
    lead0 = mm(inv0, w_lead_ref[:b, :]).astype(bf16)
    lead1 = mm(inv1, w_lead_ref[b : 2 * b, :] - tdot(x01, lead0)).astype(bf16)
    lead2 = w_lead_ref[2 * b :, :] - tdot(x02, lead0) - tdot(x12, lead1)
    lead2 = mm(inv2, lead2).astype(bf16)
    for i, lead in enumerate([lead0, lead1, lead2]):
        lead_ref[i * b : (i + 1) * b, :] = jnp.where(keep, lead, jnp.zeros_like(lead))
    value = log_ref[:1, :1] + log2
    line = lax.broadcasted_iota(jnp.int32, (LOG_ROWS, wide), 0)
    rows = jnp.zeros((LOG_ROWS, wide), f32)
    for i in range(3):
        part = value.astype(bf16).astype(f32)
        rows = jnp.where(line == i, part, rows)
        value = value - part
    lead_ref[PL * b :, :] = rows.astype(bf16)


def gather_rows(ways, near_steps, *refs):
    source_ref, keep_ref = refs[:2]
    fronts = refs[2 : 2 + ways]
    mask_ref, near_ref, far_ref = refs[2 + ways :]
    step = pl.program_id(0)
    b = fronts[0].shape[0]
    keep_cols = mask_ref[:1, :] > 0.0

    def store(out_ref):
        for i, front_ref in enumerate(fronts):
            keep = keep_cols & (keep_ref[step * ways + i] > 0)
            out_ref[i * b : (i + 1) * b, :] = jnp.where(keep, front_ref[...], 0.0)

    pl.when(step < near_steps)(lambda: store(near_ref))
    pl.when(step >= near_steps)(lambda: store(far_ref))


def add_rows(ways, with_near, *refs):
    source_ref, keep_ref, scale_ref = refs[:3]
    fronts = refs[3 : 3 + ways]
    mask_ref, root_ref = refs[3 + ways : 5 + ways]
    out_ref = refs[-1]
    step = pl.program_id(0)
    b = fronts[0].shape[0]
    keep_cols = mask_ref[:1, :] > 0.0
    for i, front_ref in enumerate(fronts):
        keep = keep_cols & (keep_ref[step * ways + i] > 0)
        at = slice(i * b, (i + 1) * b)
        total = jnp.where(scale_ref[0] > 0, root_ref[at, :], 0.0)
        total = total + jnp.where(keep, front_ref[...], 0.0)
        if with_near:
            total = total + refs[5 + ways][at, :]
        out_ref[at, :] = total


def root_step(
    corner_ref, lead_ref, first_ref, d01_ref, d2_ref,
    q_ref, inv0_ref, inv1_ref, x_ref, log_ref, work,
):
    b = inv0_ref.shape[0]
    groups = d2_ref.shape[0] // b
    pitch = lead_ref.shape[0] // groups
    corner = corner_ref[...]
    top = first_ref[...]
    for q in range(groups):
        lead = lead_ref[q * pitch : q * pitch + PL * b, :]
        corner = corner - tdot(lead, lead)
        top = top - tdot(lead[: 2 * b, :], d01_ref[q * 2 * b : (q + 1) * 2 * b, :])
        top = top - tdot(lead[2 * b :, :], d2_ref[q * b : (q + 1) * b, :])
    log0 = invert_factor(corner[:b, :b], work, inv0_ref)
    x = mm(inv0_ref[...], corner[:b, b:]).astype(bf16)
    x_ref[...] = x
    log1 = invert_factor(corner[b:, b:] - tdot(x, x), work, inv1_ref)
    log_ref[...] = jnp.broadcast_to(log0 + log1, log_ref.shape)
    q0 = mm(inv0_ref[...], top[:b, :]).astype(bf16)
    q_ref[:b, :] = q0
    q_ref[b:, :] = mm(inv1_ref[...], top[b:, :] - tdot(x, q0)).astype(bf16)


def local(leaf_fronts, block_owner, root_front):
    members = lax.axis_size("mem")
    groups = lax.axis_size("grp")
    m = lax.axis_index("mem")
    g = lax.axis_index("grp")
    front = leaf_fronts[0]
    order, cols = front.shape
    owner = block_owner[0]
    per = owner.shape[0]
    b = cols // per
    count = order // b
    quarter = order // groups
    spread = members // groups
    quarter_blocks = quarter // b
    pr = PR * b
    lead_cols = min(pr, cols)
    leads = pr // lead_cols
    zone, inner = m // spread, m % spread
    smem = pl.BlockSpec(memory_space=pltpu.SMEM)
    vmem = pl.BlockSpec(memory_space=pltpu.VMEM)

    def from_first(value):
        value = value[:, :lead_cols]
        parts = []
        for root in range(leads):
            held = value
            for bit in reversed(bits(members)):
                pairs = [(root ^ i, root ^ i ^ bit) for i in range(0, members, 2 * bit)]
                got = lax.ppermute(held, "mem", pairs)
                held = jnp.where((m ^ root) % (2 * bit) == bit, got, held)
            parts.append(held)
        return parts[0] if leads == 1 else jnp.concatenate(parts, axis=1)

    table_rows, head, rest, mask, w_lead = pl.pallas_call(
        pick_pivots,
        grid=(1,),
        in_specs=[smem, smem, pl.BlockSpec((PL * b, cols), lambda i: (0, 0))],
        out_specs=[vmem] * 5,
        out_shape=(
            shape((8, b), f32), shape((3 * b, b), f32), shape((3 * b, b), f32),
            shape((8, cols), f32), shape((PL * b, lead_cols), f32),
        ),
        name="pick_pivots",
    )(owner, (m * per).reshape(1), front)
    hops = bits(members)
    behind = 0
    for at, bit in enumerate(hops):
        table_rows = table_rows + flip(table_rows, "mem", bit)
        if at >= len(hops) - 2:
            head = head + flip(head, "mem", hops[behind])
            behind += 1
            table_rows, head = lax.optimization_barrier((table_rows, head))
    for bit in hops[behind:]:
        head = head + flip(head, "mem", bit)
    for bit in bits(members):
        rest = rest + flip(rest, "mem", bit)
    table = table_rows[0, :count].astype(jnp.int32)

    starts = [g ^ CORE, g ^ (CORE | CHIP), g ^ CHIP, g]
    places = jnp.concatenate(
        [s * quarter_blocks + jnp.arange(quarter_blocks) for s in starts] + [jnp.arange(PR)]
    )
    source = jnp.take(table, places)
    kept = (source >= PL).astype(jnp.int32)
    ways = 4
    sent = 3 * quarter_blocks
    near_steps = 2 * quarter_blocks // ways
    steps = sent // ways

    def front_spec(i, n):
        return pl.BlockSpec((b, cols), lambda s, *pre, i=i: (pre[0][s * n + i], 0))

    mask_spec = pl.BlockSpec((8, cols), lambda s, *pre: (0, 0))
    tall = (ways * b, cols)

    def gather_kernel(*refs):
        gather_rows(ways, near_steps, *refs)

    near, far = pl.pallas_call(
        gather_kernel,
        grid_spec=pltpu.PrefetchScalarGridSpec(
            num_scalar_prefetch=2,
            grid=(steps,),
            in_specs=[front_spec(i, ways) for i in range(ways)] + [mask_spec],
            out_specs=[
                pl.BlockSpec(tall, lambda s, *pre: (jnp.minimum(s, near_steps - 1), 0)),
                pl.BlockSpec(tall, lambda s, *pre: (jnp.maximum(s - near_steps, 0), 0)),
            ],
        ),
        out_shape=(shape((2 * quarter, cols), f32), shape((quarter, cols), f32)),
        name="gather_rows",
    )(source[:sent], kept[:sent], *([front] * ways), mask)
    near = flip(near, "grp", CORE)

    def first_kernel(*refs):
        add_rows(PR, False, *refs)

    first = pl.pallas_call(
        first_kernel,
        grid_spec=pltpu.PrefetchScalarGridSpec(
            num_scalar_prefetch=3,
            grid=(1,),
            in_specs=[front_spec(i, PR) for i in range(PR)]
            + [mask_spec, pl.BlockSpec((pr, cols), lambda s, *pre: (0, 0))],
            out_specs=pl.BlockSpec((pr, cols), lambda s, *pre: (0, 0)),
        ),
        out_shape=shape((pr, cols), f32),
        name="first_rows",
    )(
        source[sent + quarter_blocks :], kept[sent + quarter_blocks :],
        (g == 0).astype(jnp.int32).reshape(1), *([front] * PR), mask, root_front,
    )
    first = first + flip(first, "grp", CORE)
    first = first + flip(first, "grp", CHIP)

    work = [pltpu.VMEM((b, 2 * b), f32)]
    sq = shape((b, b), f32)
    sqh = shape((b, b), bf16)
    logs = shape((8, b), f32)

    def w_spec(k):
        return pl.BlockSpec((b, cols), lambda i: (k, 0))

    p01, inv0, inv1, x01, log01 = pl.pallas_call(
        leaf_two,
        grid=(1,),
        in_specs=[vmem, w_spec(0), w_spec(1), vmem],
        out_specs=[vmem] * 5,
        out_shape=(shape((2 * b, cols), bf16), sq, sq, sqh, logs),
        scratch_shapes=work,
        name="leaf_two",
    )(head, front, front, mask)

    far = far + near[quarter:]
    rest, far = lax.optimization_barrier((rest, far))
    far = flip(far, "grp", CHIP)

    p2, lead = pl.pallas_call(
        leaf_last,
        grid=(1,),
        in_specs=[vmem, w_spec(2)] + [vmem] * 8,
        out_specs=[vmem, vmem],
        out_shape=(shape((b, cols), bf16), shape((PL * b + LOG_ROWS, pr), bf16)),
        scratch_shapes=[pltpu.VMEM((b, b), f32)] + work,
        name="leaf_last",
    )(rest, front, from_first(w_lead), table_rows, mask, p01, inv0, inv1, x01, log01)

    def base_kernel(*refs):
        add_rows(ways, True, *refs)

    base = pl.pallas_call(
        base_kernel,
        grid_spec=pltpu.PrefetchScalarGridSpec(
            num_scalar_prefetch=3,
            grid=(quarter_blocks // ways,),
            in_specs=[front_spec(i, ways) for i in range(ways)]
            + [mask_spec]
            + [pl.BlockSpec(tall, lambda s, *pre: (s, 0))] * 2,
            out_specs=pl.BlockSpec(tall, lambda s, *pre: (s, 0)),
        ),
        out_shape=shape((quarter, cols), f32),
        name="base_rows",
    )(
        source[sent : sent + quarter_blocks], kept[sent : sent + quarter_blocks],
        jnp.ones((1,), jnp.int32), *([front] * ways), mask, root_front, near,
    )

    def to_rows(value):
        stages = [([0], value)]
        held = value
        for bit in reversed(bits(groups)):
            have = [h for offsets, _ in stages for h in offsets]
            pairs = []
            for gi in range(groups):
                for h in have:
                    for j in range(spread):
                        src = (gi ^ h) * spread + j
                        dst = (gi ^ h ^ bit) * spread + j
                        pairs.append((gi * members + src, gi * members + dst))
            got = lax.ppermute(held, ("grp", "mem"), pairs)
            new = [h ^ bit for h in have]
            held = jnp.where(among(new), got, held)
            stages.append((new, got))
        slots = [held]
        for i in range(1, spread):
            part = None
            for offsets, sent_part in stages:
                pairs = []
                for gi in range(groups):
                    for h in offsets:
                        for j in range(spread):
                            at = gi * members + (gi ^ h) * spread
                            pairs.append((at + j, at + (j ^ i)))
                got = lax.ppermute(sent_part, ("grp", "mem"), pairs)
                part = got if part is None else jnp.where(among(offsets), got, part)
            slots.append(part)
        return slots

    def among(offsets):
        found = jnp.zeros((), jnp.bool_)
        for h in offsets:
            found = found | (zone == (g ^ h))
        return found

    def across(value):
        far_value = flip(value, "grp", CHIP)
        both = jnp.concatenate([value, far_value], axis=0)
        return jnp.concatenate([both, flip(both, "grp", CORE)], axis=0)

    corner = from_first(first)
    d01 = across(p01)
    r01 = to_rows(d01)
    lead = across(lead)
    d2 = across(p2)
    r2 = to_rows(d2)
    lead, far = lax.optimization_barrier((lead, far))

    q, rinv0, rinv1, rx, root_log = pl.pallas_call(
        root_step,
        out_shape=(shape((pr, cols), bf16), sq, sq, sqh, logs),
        scratch_shapes=work,
        name="root_step",
    )(corner, lead, first, d01, d2)
    rq = to_rows(q)

    root_factor = jnp.zeros((quarter, cols), f32)
    for i in range(spread):
        start = (inner ^ i) * cols
        rows = g * quarter + start + jnp.arange(cols)
        part = lax.dynamic_slice_in_dim(base, start, cols, 0)
        part = part + lax.dynamic_slice_in_dim(far, start, cols, 0)
        part = part - tdot(r01[i], d01) - tdot(r2[i], d2)
        if leads == 1:
            q0 = mm_t(part[:, :b], rinv0)
            inside = part[:, b:pr] - jnp.dot(q0.astype(bf16), rx, preferred_element_type=f32)
            q1 = mm_t(inside, rinv1)
        else:
            q0, q1 = rq[i][:b].T.astype(f32), rq[i][b:].T.astype(f32)
        q1 = jnp.where((rows >= b)[:, None], q1, 0.0)
        panel = jnp.concatenate([q0, q1], axis=1)
        first_col = jnp.minimum(m, leads - 1) * lead_cols
        panel = lax.dynamic_slice_in_dim(panel, first_col, lead_cols, 1)
        part = jnp.where((rows >= pr)[:, None], part - tdot(rq[i], q), 0.0)
        head_cols = jnp.where(m < leads, panel, part[:, :lead_cols])
        part = jnp.concatenate([head_cols, part[:, lead_cols:]], axis=1)
        root_factor = lax.dynamic_update_slice_in_dim(root_factor, part, start, 0)

    pitch = lead.shape[0] // groups
    sums = [
        jnp.sum(lead[t * pitch + PL * b : t * pitch + PL * b + 3, 0].astype(f32))
        for t in range(groups)
    ]
    order_of = [0, CHIP, CORE, CORE | CHIP]
    log_list = []
    for leaf in range(groups):
        total = jnp.zeros((), f32)
        for at, bit in enumerate(order_of):
            total = total + jnp.where((g ^ bit) == leaf, sums[at], 0.0)
        log_list.append(total / (PL * b))
    log_det = jnp.stack(log_list + [root_log[0, 0] / pr])
    return root_factor, log_det


def solution(mesh):
    in_specs = (P("grp", None, "mem"), P("grp", "mem"), P("grp", "mem"))
    out_specs = (P("grp", "mem"), P())
    return jax.shard_map(local, mesh=mesh, in_specs=in_specs, out_specs=out_specs, check_vma=False)
```

```python
import jax
import jax.numpy as jnp
from jax import lax
from jax.experimental import pallas as pl
from jax.experimental.pallas import tpu as pltpu
from jax.sharding import PartitionSpec as P

PL = 3
PR = 2
HIGHEST = lax.Precision.HIGHEST
ROWS = 64
SUB = 16
LOG_ROWS = 32
B_ROWS = 128
CORE, CHIP = 1, 2
f32, bf16 = jnp.float32, jnp.bfloat16


def mm(lhs, rhs):
    return jnp.dot(lhs, rhs, precision=HIGHEST, preferred_element_type=f32)


def mm_t(lhs, rhs):
    return lax.dot_general(
        lhs, rhs, (((1,), (1,)), ((), ())), precision=HIGHEST, preferred_element_type=f32
    )


def tdot(lhs, rhs):
    return lax.dot_general(lhs, rhs, (((0,), (0,)), ((), ())), preferred_element_type=f32)


def bits(size):
    out, bit = [], 1
    while bit < size:
        out.append(bit)
        bit *= 2
    return out


def flip(value, axis, bit):
    size = lax.axis_size(axis)
    return lax.ppermute(value, axis, [(i, i ^ bit) for i in range(size)])


def shape(dims, dtype):
    return jax.ShapeDtypeStruct(dims, dtype)


def invert_factor(block, work, inverse_ref):
    size = block.shape[0]
    rows = lax.broadcasted_iota(jnp.int32, (size, size), 0)
    cols = lax.broadcasted_iota(jnp.int32, (size, size), 1)
    work[:, :size] = block
    work[:, size:] = jnp.where(rows == cols, 1.0, 0.0)
    sub = lax.broadcasted_iota(jnp.int32, (ROWS, size), 0)
    lane = lax.broadcasted_iota(jnp.int32, (ROWS, size), 1)
    log_sum = jnp.zeros((1, 1), f32)
    for first in range(0, size, ROWS):
        left = work[first : first + ROWS, :size]
        right = work[first : first + ROWS, size:]
        for start in range(0, ROWS, SUB):
            at = first + start
            columns = [
                jnp.broadcast_to(left[:, at + j : at + j + 1], (ROWS, size)) for j in range(SUB)
            ]
            for j in range(SUB):
                i = start + j
                if i == ROWS - 1:
                    break
                factor = jnp.where(sub > i, columns[j], 0.0) * (1.0 / columns[j][i : i + 1, :])
                for k in range(j + 1, SUB):
                    columns[k] = columns[k] - factor * columns[k][i : i + 1, :]
                left = left - factor * left[i : i + 1, :]
                right = right - factor * right[i : i + 1, :]
        pivot = jnp.sum(jnp.where(lane == sub + first, left, 0.0), axis=1, keepdims=True)
        scale = lax.rsqrt(pivot)
        left, right = left * scale, right * scale
        inverse_ref[first : first + ROWS, :] = right
        log_sum = log_sum + jnp.sum(jnp.log(pivot), axis=0, keepdims=True)
        if first + ROWS < size:
            update = lax.dot_general(
                left, jnp.concatenate([left, right], axis=1), (((0,), (0,)), ((), ())),
                precision=HIGHEST, preferred_element_type=f32,
            )
            work[first + ROWS :, :] = work[first + ROWS :, :] - update[first + ROWS :, :]
    return log_sum


def pick_pivots(owner_ref, at_ref, front_ref, table_ref, head_ref, rest_ref, mask_ref, lead_ref):
    b = head_ref.shape[1]
    per = front_ref.shape[1] // b
    for k in range(PL):
        total = jnp.zeros(((k + 1) * b, b), f32)
        for t in range(per):
            part = front_ref[: (k + 1) * b, t * b : (t + 1) * b]
            total = total + jnp.where(owner_ref[t] == k, part, 0.0)
        if k == 0:
            head_ref[:b, :] = total
        elif k == 1:
            head_ref[b:, :] = total
        else:
            rest_ref[...] = total
    lane = lax.broadcasted_iota(jnp.int32, (8, b), 1)
    table = jnp.zeros((8, b), f32)
    for t in range(per):
        table = table + jnp.where(lane == at_ref[0] + t, owner_ref[t].astype(f32), 0.0)
        keep = jnp.where(owner_ref[t] >= PL, 1.0, 0.0).astype(f32)
        mask_ref[:, t * b : (t + 1) * b] = jnp.full((8, b), keep, f32)
    table_ref[...] = table
    lead_ref[...] = front_ref[:, : lead_ref.shape[1]]


def leaf_two(head_ref, w0_ref, w1_ref, mask_ref, p_ref, inv0_ref, inv1_ref, x_ref, log_ref, work):
    b = w0_ref.shape[0]
    c00, c01, c11 = [head_ref[i * b : (i + 1) * b, :] for i in range(3)]
    keep = mask_ref[:1, :] > 0.0
    log0 = invert_factor(c00, work, inv0_ref)
    x01 = mm(inv0_ref[...], c01).astype(bf16)
    x_ref[...] = x01
    p0 = mm(inv0_ref[...], w0_ref[...]).astype(bf16)
    log1 = invert_factor(c11 - tdot(x01, x01), work, inv1_ref)
    p1 = mm(inv1_ref[...], w1_ref[...] - tdot(x01, p0)).astype(bf16)
    p_ref[:b, :] = jnp.where(keep, p0, jnp.zeros_like(p0))
    p_ref[b:, :] = jnp.where(keep, p1, jnp.zeros_like(p1))
    log_ref[...] = jnp.broadcast_to(log0 + log1, log_ref.shape)


def leaf_last(
    rest_ref, w2_ref, w_lead_ref, table_ref, mask_ref, p_ref, inv0_ref, inv1_ref, x_ref, log_ref,
    out_ref, inv, work,
):
    b, cols = w2_ref.shape
    wide = w_lead_ref.shape[1] if w_lead_ref.shape[1] > cols else PR * b
    c02, c12, c22 = [rest_ref[i * b : (i + 1) * b, :] for i in range(3)]
    inv0, inv1, x01 = inv0_ref[...], inv1_ref[...], x_ref[...]
    x02 = mm(inv0, c02).astype(bf16)
    x12 = mm(inv1, c12 - tdot(x01, x02)).astype(bf16)
    log2 = invert_factor(c22 - tdot(x02, x02) - tdot(x12, x12), work, inv)
    inv2 = inv[...]
    keep = mask_ref[:1, :] > 0.0
    panel = mm(inv2, w2_ref[...] - tdot(x02, p_ref[:b, :]) - tdot(x12, p_ref[b:, :])).astype(bf16)
    out_ref[:b, :] = jnp.where(keep, panel, jnp.zeros_like(panel))
    lane = lax.broadcasted_iota(jnp.int32, (1, wide), 1)
    block = jnp.zeros((1, wide), f32)
    for t in range(PR):
        inside = (lane >= t * b) & (lane < (t + 1) * b)
        block = jnp.where(inside, table_ref[:1, t : t + 1], block)
    keep = block > PL - 0.5
    lead0 = mm(inv0, w_lead_ref[:b, :]).astype(bf16)
    lead1 = mm(inv1, w_lead_ref[b : 2 * b, :] - tdot(x01, lead0)).astype(bf16)
    lead2 = w_lead_ref[2 * b :, :] - tdot(x02, lead0) - tdot(x12, lead1)
    lead2 = mm(inv2, lead2).astype(bf16)
    value = log_ref[:1, :1] + log2
    line = lax.broadcasted_iota(jnp.int32, (LOG_ROWS, wide), 0)
    rows = jnp.zeros((LOG_ROWS, wide), f32)
    for i in range(3):
        part = value.astype(bf16).astype(f32)
        rows = jnp.where(line == i, part, rows)
        value = value - part
    leads = [jnp.where(keep, lead, jnp.zeros_like(lead)) for lead in (lead0, lead1, lead2)]
    whole = jnp.concatenate(leads + [rows.astype(bf16)], axis=0)
    if cols >= wide:
        split = cols // wide
        tall = whole.shape[0] // split
        for i in range(split):
            out_ref[b:, i * wide : (i + 1) * wide] = whole[i * tall : (i + 1) * tall, :]
    else:
        tall = whole.shape[0]
        for i in range(wide // cols):
            out_ref[b + i * tall : b + (i + 1) * tall, :] = whole[:, i * cols : (i + 1) * cols]


def rows_kernel(ways, spans, *refs):
    keep_ref, scale_ref = refs[1:3]
    fronts = refs[3 : 3 + ways]
    mask_ref = refs[3 + ways]
    adds = refs[4 + ways : -1]
    out_ref = refs[-1]
    step = pl.program_id(0)
    b = fronts[0].shape[0]
    keep_cols = mask_ref[:1, :] > 0.0
    for i, front_ref in enumerate(fronts):
        at = slice(i * b, (i + 1) * b)
        keep = keep_cols & (keep_ref[step * ways + i] > 0)
        total = jnp.where(keep, front_ref[...], 0.0)
        for add_ref, (first, last) in zip(adds, spans):
            use = (step >= first) & (step < last) & (scale_ref[0] > 0)
            total = total + jnp.where(use, add_ref[at, :], 0.0)
        out_ref[at, :] = total


def take_rows(front, mask, source, kept, scale, ways, adds, name):
    b = B_ROWS
    cols = front.shape[1]
    steps = source.shape[0] // ways
    spans, add_specs = [], []
    for array, first, tile in adds:
        tiles = array.shape[0] // (ways * b) - tile
        last = min(steps, first + tiles)
        spans.append((first, last))

        def index(s, *pre, first=first, last=last, tile=tile):
            return (jnp.clip(s, first, last - 1) - first + tile, 0)

        add_specs.append(pl.BlockSpec((ways * b, cols), index))
    front_specs = [
        pl.BlockSpec((b, cols), lambda s, *pre, i=i: (pre[0][s * ways + i], 0)) for i in range(ways)
    ]

    def body(*refs):
        rows_kernel(ways, spans, *refs)

    return pl.pallas_call(
        body,
        grid_spec=pltpu.PrefetchScalarGridSpec(
            num_scalar_prefetch=3,
            grid=(steps,),
            in_specs=front_specs + [pl.BlockSpec((8, cols), lambda s, *pre: (0, 0))] + add_specs,
            out_specs=pl.BlockSpec((ways * b, cols), lambda s, *pre: (s, 0)),
        ),
        out_shape=shape((source.shape[0] * b, cols), f32),
        compiler_params=pltpu.CompilerParams(vmem_limit_bytes=32 << 20),
        name=name,
    )(source, kept, scale, *([front] * ways), mask, *[array for array, _, _ in adds])


def root_step(
    leaf_ref, corner_ref, first_ref, d01_ref, pack_ref,
    q_ref, inv0_ref, inv1_ref, x_ref, log_ref, work,
):
    b = inv0_ref.shape[0]
    cols = first_ref.shape[1]
    wide = corner_ref.shape[1]
    groups = d01_ref.shape[0] // (2 * b)
    pitch = pack_ref.shape[0] // groups
    corner = corner_ref[...]
    top = first_ref[...]
    lane = lax.broadcasted_iota(jnp.int32, (8, b), 1)
    logs = jnp.zeros((8, b), f32)
    for i in range(groups):
        at = i * pitch
        d2 = pack_ref[at : at + b, :]
        packed = pack_ref[at + b : at + pitch, :]
        if cols >= wide:
            parts = [packed[:, j * wide : (j + 1) * wide] for j in range(cols // wide)]
            whole = jnp.concatenate(parts, axis=0)
        else:
            tall = (pitch - b) // (wide // cols)
            parts = [packed[j * tall : (j + 1) * tall, :] for j in range(wide // cols)]
            whole = jnp.concatenate(parts, axis=1)
        lead = whole[: PL * b, :]
        corner = corner - tdot(lead, lead)
        top = top - tdot(lead[: 2 * b, :], d01_ref[i * 2 * b : (i + 1) * 2 * b, :])
        top = top - tdot(lead[2 * b :, :], d2)
        log_sum = jnp.sum(whole[PL * b : PL * b + 16, :b].astype(f32), axis=0, keepdims=True)
        logs = jnp.where(lane == leaf_ref[i], log_sum * (1.0 / (PL * b)), logs)
    log0 = invert_factor(corner[:b, :b], work, inv0_ref)
    x = mm(inv0_ref[...], corner[:b, b:]).astype(bf16)
    x_ref[...] = x
    log1 = invert_factor(corner[b:, b:] - tdot(x, x), work, inv1_ref)
    log_ref[...] = jnp.where(lane == groups, (log0 + log1) * (1.0 / wide), logs)
    q0 = mm(inv0_ref[...], top[:b, :]).astype(bf16)
    q_ref[:b, :] = q0
    q_ref[b:, :] = mm(inv1_ref[...], top[b:, :] - tdot(x, q0)).astype(bf16)


def update_kernel(slots, *refs):
    place_ref, base_ref, d01_ref, d2_ref = refs[:4]
    r01, r2 = refs[4 : 4 + slots], refs[4 + slots : 4 + 2 * slots]
    inv0_ref, inv1_ref, x_ref, out_ref, panel_ref = refs[4 + 2 * slots :]
    b = inv0_ref.shape[0]
    cols = out_ref.shape[1]

    def at_slot(i):
        total = base_ref[...] - tdot(r01[i][...], d01_ref[...]) - tdot(r2[i][...], d2_ref[...])
        out_ref[...] = total
        if cols >= PR * b:
            q0 = mm_t(total[:, :b], inv0_ref[...])
            inside = jnp.dot(q0.astype(bf16), x_ref[...], preferred_element_type=f32)
            panel_ref[:, :b] = q0
            panel_ref[:, b:] = mm_t(total[:, b : PR * b] - inside, inv1_ref[...])
        else:
            panel_ref[...] = jnp.zeros_like(panel_ref)

    for i in range(slots):
        pl.when(pl.program_id(0) == i)(lambda i=i: at_slot(i))


def finish_kernel(slots, *refs):
    place_ref, info_ref, part_ref, panel_ref, q_ref = refs[:5]
    rq, out_ref = refs[5 : 5 + slots], refs[5 + slots]
    rows, cols = out_ref.shape
    wide = q_ref.shape[0]
    b = wide // PR

    def at_slot(i):
        row = info_ref[i] + lax.broadcasted_iota(jnp.int32, (rows, cols), 0)
        total = part_ref[...] - tdot(rq[i][...], q_ref[...])
        total = jnp.where(row >= wide, total, 0.0)
        width = min(wide, cols)
        col = info_ref[slots] + lax.broadcasted_iota(jnp.int32, (rows, width), 1)
        panel = panel_ref[...]
        panel = jnp.where((row[:, :width] >= b) | (col < b), panel, 0.0)
        out_ref[:, :width] = jnp.where(col < wide, panel, total[:, :width])
        if width < cols:
            out_ref[:, width:] = total[:, width:]

    for i in range(slots):
        pl.when(pl.program_id(0) == i)(lambda i=i: at_slot(i))


def local(leaf_fronts, block_owner, root_front):
    members = lax.axis_size("mem")
    groups = lax.axis_size("grp")
    m = lax.axis_index("mem")
    g = lax.axis_index("grp")
    front = leaf_fronts[0]
    order, cols = front.shape
    owner = block_owner[0]
    per = owner.shape[0]
    b = cols // per
    count = order // b
    quarter = order // groups
    spread = members // groups
    quarter_blocks = quarter // b
    pr = PR * b
    lead_cols = min(pr, cols)
    leads = pr // lead_cols
    zone, inner = m // spread, m % spread
    smem = pl.BlockSpec(memory_space=pltpu.SMEM)
    vmem = pl.BlockSpec(memory_space=pltpu.VMEM)

    def lead_hop(value, at):
        bit = bits(members)[-1 - at]
        parts = []
        for root in range(leads):
            held = value[root]
            pairs = [(root ^ i, root ^ i ^ bit) for i in range(0, members, 2 * bit)]
            got = lax.ppermute(held, "mem", pairs)
            parts.append(jnp.where((m ^ root) % (2 * bit) == bit, got, held))
        return parts

    table_rows, head, rest, mask, w_lead = pl.pallas_call(
        pick_pivots,
        grid=(1,),
        in_specs=[smem, smem, pl.BlockSpec((PL * b, cols), lambda i: (0, 0))],
        out_specs=[vmem] * 5,
        out_shape=(
            shape((8, b), f32), shape((3 * b, b), f32), shape((3 * b, b), f32),
            shape((8, cols), f32), shape((PL * b, lead_cols), f32),
        ),
        name="pick_pivots",
    )(owner, (m * per).reshape(1), front)
    hops = bits(members)
    last = len(hops) - 1
    w_lead = [w_lead] * leads

    def table_hop(value, at):
        return value + flip(value, "mem", hops[at])

    table_rows = table_hop(table_hop(table_rows, 0), 1)
    head = table_hop(head, 0)
    table_rows, head, w_lead, rest = lax.optimization_barrier((table_rows, head, w_lead, rest))
    for at in range(2, last + 1):
        table_rows = table_hop(table_rows, at)
        head = table_hop(head, at - 1)
        rest = table_hop(rest, at - 2)
        w_lead = lead_hop(w_lead, at - 2)
        table_rows, head, rest, w_lead = lax.optimization_barrier((table_rows, head, rest, w_lead))
    table = table_rows[0, :count].astype(jnp.int32)

    starts = [g ^ (CORE | CHIP), g ^ CHIP, g ^ CORE, g]
    places = jnp.concatenate(
        [s * quarter_blocks + jnp.arange(quarter_blocks) for s in starts] + [jnp.arange(PR)]
    )
    source = jnp.take(table, places)
    kept = (source >= PL).astype(jnp.int32)
    one = jnp.ones((1,), jnp.int32)
    ways = quarter_blocks // 2
    n = quarter_blocks

    def rows_at(first, size, adds, name, scale=one, ways=ways):
        return take_rows(
            front, mask, source[first : first + size], kept[first : first + size], scale, ways,
            adds, name,
        )

    diagonal = flip(rows_at(0, n, [], "far_rows"), "grp", CORE)
    first = rows_at(
        4 * n, PR, [(root_front, 0, 0)], "first_rows", (g == 0).astype(jnp.int32).reshape(1), PR
    )
    first = first + flip(first, "grp", CORE)
    head = table_hop(head, last)
    rest = table_hop(rest, last - 1)
    head, rest, diagonal, first = lax.optimization_barrier((head, rest, diagonal, first))
    first = first + flip(first, "grp", CHIP)
    far = [rows_at(n + i * ways, ways, [(diagonal, 0, i)], "far_sum") for i in range(2)]
    head, far = lax.optimization_barrier((head, far))
    far = [flip(part, "grp", CHIP) for part in far]
    rest = table_hop(rest, last)
    w_lead = lead_hop(w_lead, last - 1)

    work = [pltpu.VMEM((b, 2 * b), f32)]
    sq = shape((b, b), f32)
    sqh = shape((b, b), bf16)
    logs = shape((8, b), f32)

    def w_spec(k):
        return pl.BlockSpec((b, cols), lambda i: (k, 0))

    p01, inv0, inv1, x01, log01 = pl.pallas_call(
        leaf_two,
        grid=(1,),
        in_specs=[vmem, w_spec(0), w_spec(1), vmem],
        out_specs=[vmem] * 5,
        out_shape=(shape((2 * b, cols), bf16), sq, sq, sqh, logs),
        scratch_shapes=work,
        name="leaf_two",
    )(head, front, front, mask)

    w_lead = lead_hop(w_lead, last)
    w_lead = w_lead[0] if leads == 1 else jnp.concatenate(w_lead, axis=1)
    lead_rows = (PL * b + LOG_ROWS) * pr // cols
    pack = pl.pallas_call(
        leaf_last,
        grid=(1,),
        in_specs=[vmem, w_spec(2)] + [vmem] * 8,
        out_specs=vmem,
        out_shape=shape((b + lead_rows, cols), bf16),
        scratch_shapes=[pltpu.VMEM((b, b), f32)] + work,
        name="leaf_last",
    )(rest, front, w_lead, table_rows, mask, p01, inv0, inv1, x01, log01)
    near = flip(rows_at(2 * n, n, [], "near_rows"), "grp", CORE)

    def among(offsets):
        found = jnp.zeros((), jnp.bool_)
        for h in offsets:
            found = found | (zone == (g ^ h))
        return found

    def to_rows(value, staged):
        have, held, ready = [0], value, None
        order = list(reversed(bits(groups)))
        for at, bit in enumerate(order):
            if at == len(order) - 1:
                ready = (list(have), held)
            pairs = []
            for gi in range(groups):
                for h in have:
                    for j in range(spread):
                        src = (gi ^ h) * spread + j
                        dst = (gi ^ h ^ bit) * spread + j
                        pairs.append((gi * members + src, gi * members + dst))
            got = lax.ppermute(held, ("grp", "mem"), pairs)
            new = [h ^ bit for h in have]
            held = jnp.where(among(new), got, held)
            have = have + new
        slots = [held]
        stages = [(have, held)]
        if staged:
            stages = [ready, (new, got)]
        for i in range(1, spread):
            part = None
            for offsets, sent_part in stages:
                pairs = []
                for gi in range(groups):
                    for h in offsets:
                        for j in range(spread):
                            at = gi * members + (gi ^ h) * spread
                            pairs.append((at + j, at + (j ^ i)))
                got = lax.ppermute(sent_part, ("grp", "mem"), pairs)
                part = got if part is None else jnp.where(among(offsets), got, part)
            slots.append(part)
        return slots

    def across(value):
        far_value = flip(value, "grp", CHIP)
        both = jnp.concatenate([value, far_value], axis=0)
        return jnp.concatenate([both, flip(both, "grp", CORE)], axis=0)

    corner = [first[:, :lead_cols]] * leads
    for at in range(last + 1):
        corner = lead_hop(corner, at)
    corner = corner[0] if leads == 1 else jnp.concatenate(corner, axis=1)
    d01 = across(p01)
    r01 = to_rows(d01, True)
    pack = across(pack)
    pack, far[0] = lax.optimization_barrier((pack, far[0]))
    d2 = pack.reshape(groups, b + lead_rows, cols)[:, :b].reshape(groups * b, cols)
    r2 = to_rows(d2, True)
    leaves = jnp.stack([g, g ^ CHIP, g ^ CORE, g ^ (CORE | CHIP)])
    q, rinv0, rinv1, rx, logs_out = pl.pallas_call(
        root_step,
        in_specs=[smem] + [vmem] * 4,
        out_shape=(shape((pr, cols), bf16), sq, sq, sqh, logs),
        scratch_shapes=work,
        compiler_params=pltpu.CompilerParams(vmem_limit_bytes=32 << 20),
        name="root_step",
    )(leaves, corner, first, d01, pack)
    rq = to_rows(q, False)

    base = rows_at(
        3 * n, n, [(root_front, 0, 0), (near, 0, 0), (far[0], 0, 0), (far[1], 1, 0)], "base_rows"
    )
    slot_of = inner ^ jnp.arange(spread, dtype=jnp.int32)

    def update_body(*refs):
        update_kernel(spread, *refs)

    def whole_spec(array):
        return pl.BlockSpec(array.shape, lambda s, *pre: (0, 0))

    fixed = [d01, d2] + r01 + r2 + [rinv0, rinv1, rx]
    part, panel = pl.pallas_call(
        update_body,
        grid_spec=pltpu.PrefetchScalarGridSpec(
            num_scalar_prefetch=1,
            grid=(spread,),
            in_specs=[pl.BlockSpec((cols, cols), lambda s, place: (place[s], 0))]
            + [whole_spec(array) for array in fixed],
            out_specs=[
                pl.BlockSpec((cols, cols), lambda s, place: (s, 0)),
                pl.BlockSpec((cols, lead_cols if leads > 1 else pr), lambda s, place: (s, 0)),
            ],
        ),
        out_shape=(shape((quarter, cols), f32), shape((quarter, lead_cols), f32)),
        compiler_params=pltpu.CompilerParams(vmem_limit_bytes=48 << 20),
        name="update",
    )(slot_of, base, *fixed)
    if leads > 1:
        first_col = jnp.minimum(m, leads - 1) * lead_cols
        panel = jnp.concatenate([rows.astype(f32).T for rows in rq], axis=0)
        panel = lax.dynamic_slice_in_dim(panel, first_col, lead_cols, 1)
    info = jnp.concatenate([g * quarter + slot_of * cols, (m * cols).reshape(1)])

    def finish_body(*refs):
        finish_kernel(spread, *refs)

    root_factor = pl.pallas_call(
        finish_body,
        grid_spec=pltpu.PrefetchScalarGridSpec(
            num_scalar_prefetch=2,
            grid=(spread,),
            in_specs=[
                pl.BlockSpec((cols, cols), lambda s, place, info: (s, 0)),
                pl.BlockSpec((cols, lead_cols), lambda s, place, info: (s, 0)),
                whole_spec(q),
            ]
            + [whole_spec(rows) for rows in rq],
            out_specs=pl.BlockSpec((cols, cols), lambda s, place, info: (place[s], 0)),
        ),
        out_shape=shape((quarter, cols), f32),
        compiler_params=pltpu.CompilerParams(vmem_limit_bytes=32 << 20),
        name="finish",
    )(slot_of, info, part, panel, q, *rq)
    return root_factor, logs_out[0, : groups + 1]


def solution(mesh):
    in_specs = (P("grp", None, "mem"), P("grp", "mem"), P("grp", "mem"))
    out_specs = (P("grp", "mem"), P())
    return jax.shard_map(local, mesh=mesh, in_specs=in_specs, out_specs=out_specs, check_vma=False)
```

```python
import jax
import jax.numpy as jnp
from jax import lax
from jax.experimental import pallas as pl
from jax.experimental.pallas import tpu as pltpu
from jax.sharding import PartitionSpec as P

PL = 3
PR = 2
HIGHEST = lax.Precision.HIGHEST
ROWS = 64
SUB = 16
LOG_ROWS = 32
B_ROWS = 128
CORE, CHIP = 1, 2
f32, bf16 = jnp.float32, jnp.bfloat16


def mm(lhs, rhs):
    return jnp.dot(lhs, rhs, precision=HIGHEST, preferred_element_type=f32)


def mm_t(lhs, rhs):
    return lax.dot_general(
        lhs, rhs, (((1,), (1,)), ((), ())), precision=HIGHEST, preferred_element_type=f32
    )


def tdot(lhs, rhs):
    return lax.dot_general(lhs, rhs, (((0,), (0,)), ((), ())), preferred_element_type=f32)


def bits(size):
    out, bit = [], 1
    while bit < size:
        out.append(bit)
        bit *= 2
    return out


def flip(value, axis, bit):
    size = lax.axis_size(axis)
    return lax.ppermute(value, axis, [(i, i ^ bit) for i in range(size)])


def shape(dims, dtype):
    return jax.ShapeDtypeStruct(dims, dtype)


def invert_factor(block, work, inverse_ref):
    size = block.shape[0]
    rows = lax.broadcasted_iota(jnp.int32, (size, size), 0)
    cols = lax.broadcasted_iota(jnp.int32, (size, size), 1)
    work[:, :size] = block
    work[:, size:] = jnp.where(rows == cols, 1.0, 0.0)
    sub = lax.broadcasted_iota(jnp.int32, (ROWS, size), 0)
    lane = lax.broadcasted_iota(jnp.int32, (ROWS, size), 1)
    log_sum = jnp.zeros((1, 1), f32)
    for first in range(0, size, ROWS):
        left = work[first : first + ROWS, :size]
        right = work[first : first + ROWS, size:]
        for start in range(0, ROWS, SUB):
            at = first + start
            columns = [
                jnp.broadcast_to(left[:, at + j : at + j + 1], (ROWS, size)) for j in range(SUB)
            ]
            for j in range(SUB):
                i = start + j
                if i == ROWS - 1:
                    break
                factor = jnp.where(sub > i, columns[j], 0.0) * (1.0 / columns[j][i : i + 1, :])
                for k in range(j + 1, SUB):
                    columns[k] = columns[k] - factor * columns[k][i : i + 1, :]
                left = left - factor * left[i : i + 1, :]
                right = right - factor * right[i : i + 1, :]
        pivot = jnp.sum(jnp.where(lane == sub + first, left, 0.0), axis=1, keepdims=True)
        scale = lax.rsqrt(pivot)
        left, right = left * scale, right * scale
        inverse_ref[first : first + ROWS, :] = right
        log_sum = log_sum + jnp.sum(jnp.log(pivot), axis=0, keepdims=True)
        if first + ROWS < size:
            update = lax.dot_general(
                left, jnp.concatenate([left, right], axis=1), (((0,), (0,)), ((), ())),
                precision=HIGHEST, preferred_element_type=f32,
            )
            work[first + ROWS :, :] = work[first + ROWS :, :] - update[first + ROWS :, :]
    return log_sum


def pick_pivots(owner_ref, at_ref, front_ref, table_ref, head_ref, rest_ref, mask_ref, lead_ref):
    b = head_ref.shape[1]
    per = front_ref.shape[1] // b
    for k in range(PL):
        total = jnp.zeros(((k + 1) * b, b), f32)
        for t in range(per):
            part = front_ref[: (k + 1) * b, t * b : (t + 1) * b]
            total = total + jnp.where(owner_ref[t] == k, part, 0.0)
        if k == 0:
            head_ref[:b, :] = total
        elif k == 1:
            head_ref[b:, :] = total
        else:
            rest_ref[...] = total
    lane = lax.broadcasted_iota(jnp.int32, (8, b), 1)
    table = jnp.zeros((8, b), f32)
    for t in range(per):
        table = table + jnp.where(lane == at_ref[0] + t, owner_ref[t].astype(f32), 0.0)
        keep = jnp.where(owner_ref[t] >= PL, 1.0, 0.0).astype(f32)
        mask_ref[:, t * b : (t + 1) * b] = jnp.full((8, b), keep, f32)
    table_ref[...] = table
    lead_ref[...] = front_ref[:, : lead_ref.shape[1]]


def leaf_two(head_ref, w0_ref, w1_ref, mask_ref, p_ref, inv0_ref, inv1_ref, x_ref, log_ref, work):
    b = w0_ref.shape[0]
    c00, c01, c11 = [head_ref[i * b : (i + 1) * b, :] for i in range(3)]
    keep = mask_ref[:1, :] > 0.0
    log0 = invert_factor(c00, work, inv0_ref)
    x01 = mm(inv0_ref[...], c01).astype(bf16)
    x_ref[...] = x01
    p0 = mm(inv0_ref[...], w0_ref[...]).astype(bf16)
    log1 = invert_factor(c11 - tdot(x01, x01), work, inv1_ref)
    p1 = mm(inv1_ref[...], w1_ref[...] - tdot(x01, p0)).astype(bf16)
    p_ref[:b, :] = jnp.where(keep, p0, jnp.zeros_like(p0))
    p_ref[b:, :] = jnp.where(keep, p1, jnp.zeros_like(p1))
    log_ref[...] = jnp.broadcast_to(log0 + log1, log_ref.shape)


def leaf_last(
    rest_ref, w2_ref, w_lead_ref, table_ref, mask_ref, p_ref, inv0_ref, inv1_ref, x_ref, log_ref,
    out_ref, inv, work,
):
    b, cols = w2_ref.shape
    wide = w_lead_ref.shape[1] if w_lead_ref.shape[1] > cols else PR * b
    c02, c12, c22 = [rest_ref[i * b : (i + 1) * b, :] for i in range(3)]
    inv0, inv1, x01 = inv0_ref[...], inv1_ref[...], x_ref[...]
    x02 = mm(inv0, c02).astype(bf16)
    x12 = mm(inv1, c12 - tdot(x01, x02)).astype(bf16)
    log2 = invert_factor(c22 - tdot(x02, x02) - tdot(x12, x12), work, inv)
    inv2 = inv[...]
    keep = mask_ref[:1, :] > 0.0
    panel = mm(inv2, w2_ref[...] - tdot(x02, p_ref[:b, :]) - tdot(x12, p_ref[b:, :])).astype(bf16)
    out_ref[:b, :] = jnp.where(keep, panel, jnp.zeros_like(panel))
    lane = lax.broadcasted_iota(jnp.int32, (1, wide), 1)
    block = jnp.zeros((1, wide), f32)
    for t in range(PR):
        inside = (lane >= t * b) & (lane < (t + 1) * b)
        block = jnp.where(inside, table_ref[:1, t : t + 1], block)
    keep = block > PL - 0.5
    lead0 = mm(inv0, w_lead_ref[:b, :]).astype(bf16)
    lead1 = mm(inv1, w_lead_ref[b : 2 * b, :] - tdot(x01, lead0)).astype(bf16)
    lead2 = w_lead_ref[2 * b :, :] - tdot(x02, lead0) - tdot(x12, lead1)
    lead2 = mm(inv2, lead2).astype(bf16)
    value = log_ref[:1, :1] + log2
    line = lax.broadcasted_iota(jnp.int32, (LOG_ROWS, wide), 0)
    rows = jnp.zeros((LOG_ROWS, wide), f32)
    for i in range(3):
        part = value.astype(bf16).astype(f32)
        rows = jnp.where(line == i, part, rows)
        value = value - part
    leads = [jnp.where(keep, lead, jnp.zeros_like(lead)) for lead in (lead0, lead1, lead2)]
    whole = jnp.concatenate(leads + [rows.astype(bf16)], axis=0)
    if cols >= wide:
        split = cols // wide
        tall = whole.shape[0] // split
        for i in range(split):
            out_ref[b:, i * wide : (i + 1) * wide] = whole[i * tall : (i + 1) * tall, :]
    else:
        tall = whole.shape[0]
        for i in range(wide // cols):
            out_ref[b + i * tall : b + (i + 1) * tall, :] = whole[:, i * cols : (i + 1) * cols]


def rows_kernel(ways, spans, *refs):
    keep_ref, scale_ref = refs[1:3]
    fronts = refs[3 : 3 + ways]
    mask_ref = refs[3 + ways]
    adds = refs[4 + ways : -1]
    out_ref = refs[-1]
    step = pl.program_id(0)
    b = fronts[0].shape[0]
    keep_cols = mask_ref[:1, :] > 0.0
    for i, front_ref in enumerate(fronts):
        at = slice(i * b, (i + 1) * b)
        keep = keep_cols & (keep_ref[step * ways + i] > 0)
        total = jnp.where(keep, front_ref[...], 0.0)
        for add_ref, (first, last) in zip(adds, spans):
            use = (step >= first) & (step < last) & (scale_ref[0] > 0)
            total = total + jnp.where(use, add_ref[at, :], 0.0)
        out_ref[at, :] = total


def take_rows(front, mask, source, kept, scale, ways, adds, name):
    b = B_ROWS
    cols = front.shape[1]
    steps = source.shape[0] // ways
    spans, add_specs = [], []
    for array, first, tile in adds:
        tiles = array.shape[0] // (ways * b) - tile
        last = min(steps, first + tiles)
        spans.append((first, last))

        def index(s, *pre, first=first, last=last, tile=tile):
            return (jnp.clip(s, first, last - 1) - first + tile, 0)

        add_specs.append(pl.BlockSpec((ways * b, cols), index))
    front_specs = [
        pl.BlockSpec((b, cols), lambda s, *pre, i=i: (pre[0][s * ways + i], 0)) for i in range(ways)
    ]

    def body(*refs):
        rows_kernel(ways, spans, *refs)

    return pl.pallas_call(
        body,
        grid_spec=pltpu.PrefetchScalarGridSpec(
            num_scalar_prefetch=3,
            grid=(steps,),
            in_specs=front_specs + [pl.BlockSpec((8, cols), lambda s, *pre: (0, 0))] + add_specs,
            out_specs=pl.BlockSpec((ways * b, cols), lambda s, *pre: (s, 0)),
        ),
        out_shape=shape((source.shape[0] * b, cols), f32),
        compiler_params=pltpu.CompilerParams(vmem_limit_bytes=60 << 20),
        name=name,
    )(source, kept, scale, *([front] * ways), mask, *[array for array, _, _ in adds])


def root_step(
    leaf_ref, corner_ref, first_ref, d01_ref, pack_ref,
    q_ref, inv0_ref, inv1_ref, x_ref, log_ref, work,
):
    b = inv0_ref.shape[0]
    cols = first_ref.shape[1]
    wide = corner_ref.shape[1]
    groups = d01_ref.shape[0] // (2 * b)
    pitch = pack_ref.shape[0] // groups
    corner = corner_ref[...]
    top = first_ref[...]
    lane = lax.broadcasted_iota(jnp.int32, (8, b), 1)
    logs = jnp.zeros((8, b), f32)
    for i in range(groups):
        at = i * pitch
        d2 = pack_ref[at : at + b, :]
        packed = pack_ref[at + b : at + pitch, :]
        if cols >= wide:
            parts = [packed[:, j * wide : (j + 1) * wide] for j in range(cols // wide)]
            whole = jnp.concatenate(parts, axis=0)
        else:
            tall = (pitch - b) // (wide // cols)
            parts = [packed[j * tall : (j + 1) * tall, :] for j in range(wide // cols)]
            whole = jnp.concatenate(parts, axis=1)
        lead = whole[: PL * b, :]
        corner = corner - tdot(lead, lead)
        top = top - tdot(lead[: 2 * b, :], d01_ref[i * 2 * b : (i + 1) * 2 * b, :])
        top = top - tdot(lead[2 * b :, :], d2)
        log_sum = jnp.sum(whole[PL * b : PL * b + 16, :b].astype(f32), axis=0, keepdims=True)
        logs = jnp.where(lane == leaf_ref[i], log_sum * (1.0 / (PL * b)), logs)
    log0 = invert_factor(corner[:b, :b], work, inv0_ref)
    x = mm(inv0_ref[...], corner[:b, b:]).astype(bf16)
    x_ref[...] = x
    log1 = invert_factor(corner[b:, b:] - tdot(x, x), work, inv1_ref)
    log_ref[...] = jnp.where(lane == groups, (log0 + log1) * (1.0 / wide), logs)
    q0 = mm(inv0_ref[...], top[:b, :]).astype(bf16)
    q_ref[:b, :] = q0
    q_ref[b:, :] = mm(inv1_ref[...], top[b:, :] - tdot(x, q0)).astype(bf16)


def update_kernel(slots, *refs):
    place_ref, base_ref, d01_ref, d2_ref = refs[:4]
    r01, r2 = refs[4 : 4 + slots], refs[4 + slots : 4 + 2 * slots]
    inv0_ref, inv1_ref, x_ref, out_ref, panel_ref = refs[4 + 2 * slots :]
    b = inv0_ref.shape[0]
    cols = out_ref.shape[1]

    def at_slot(i):
        total = base_ref[...] - tdot(r01[i][...], d01_ref[...]) - tdot(r2[i][...], d2_ref[...])
        out_ref[...] = total
        if cols >= PR * b:
            q0 = mm_t(total[:, :b], inv0_ref[...])
            inside = jnp.dot(q0.astype(bf16), x_ref[...], preferred_element_type=f32)
            panel_ref[:, :b] = q0
            panel_ref[:, b:] = mm_t(total[:, b : PR * b] - inside, inv1_ref[...])
        else:
            panel_ref[...] = jnp.zeros_like(panel_ref)

    for i in range(slots):
        pl.when(pl.program_id(0) == i)(lambda i=i: at_slot(i))


def finish_kernel(slots, *refs):
    place_ref, info_ref, part_ref, panel_ref, q_ref = refs[:5]
    rq, out_ref = refs[5 : 5 + slots], refs[5 + slots]
    rows, cols = out_ref.shape
    wide = q_ref.shape[0]
    b = wide // PR

    def at_slot(i):
        row = info_ref[i] + lax.broadcasted_iota(jnp.int32, (rows, cols), 0)
        total = part_ref[...] - tdot(rq[i][...], q_ref[...])
        total = jnp.where(row >= wide, total, 0.0)
        width = min(wide, cols)
        col = info_ref[slots] + lax.broadcasted_iota(jnp.int32, (rows, width), 1)
        panel = panel_ref[...]
        panel = jnp.where((row[:, :width] >= b) | (col < b), panel, 0.0)
        out_ref[:, :width] = jnp.where(col < wide, panel, total[:, :width])
        if width < cols:
            out_ref[:, width:] = total[:, width:]

    for i in range(slots):
        pl.when(pl.program_id(0) == i)(lambda i=i: at_slot(i))


def local(leaf_fronts, block_owner, root_front):
    members = lax.axis_size("mem")
    groups = lax.axis_size("grp")
    m = lax.axis_index("mem")
    g = lax.axis_index("grp")
    front = leaf_fronts[0]
    order, cols = front.shape
    owner = block_owner[0]
    per = owner.shape[0]
    b = cols // per
    count = order // b
    quarter = order // groups
    spread = members // groups
    quarter_blocks = quarter // b
    pr = PR * b
    lead_cols = min(pr, cols)
    leads = pr // lead_cols
    zone, inner = m // spread, m % spread
    smem = pl.BlockSpec(memory_space=pltpu.SMEM)
    vmem = pl.BlockSpec(memory_space=pltpu.VMEM)

    def lead_hop(value, at):
        bit = bits(members)[-1 - at]
        parts = []
        for root in range(leads):
            held = value[root]
            pairs = [(root ^ i, root ^ i ^ bit) for i in range(0, members, 2 * bit)]
            got = lax.ppermute(held, "mem", pairs)
            parts.append(jnp.where((m ^ root) % (2 * bit) == bit, got, held))
        return parts

    table_rows, head, rest, mask, w_lead = pl.pallas_call(
        pick_pivots,
        grid=(1,),
        in_specs=[smem, smem, pl.BlockSpec((PL * b, cols), lambda i: (0, 0))],
        out_specs=[vmem] * 5,
        out_shape=(
            shape((8, b), f32), shape((3 * b, b), f32), shape((3 * b, b), f32),
            shape((8, cols), f32), shape((PL * b, lead_cols), f32),
        ),
        name="pick_pivots",
    )(owner, (m * per).reshape(1), front)
    hops = bits(members)
    last = len(hops) - 1
    w_lead = [w_lead] * leads

    def table_hop(value, at):
        return value + flip(value, "mem", hops[at])

    table_rows = table_hop(table_hop(table_rows, 0), 1)
    head = table_hop(head, 0)
    table_rows, head, w_lead, rest = lax.optimization_barrier((table_rows, head, w_lead, rest))
    for at in range(2, last + 1):
        table_rows = table_hop(table_rows, at)
        head = table_hop(head, at - 1)
        rest = table_hop(rest, at - 2)
        table_rows, head, rest, w_lead = lax.optimization_barrier((table_rows, head, rest, w_lead))
    table = table_rows[0, :count].astype(jnp.int32)

    starts = [g ^ (CORE | CHIP), g ^ CHIP, g ^ CORE, g]
    places = jnp.concatenate(
        [s * quarter_blocks + jnp.arange(quarter_blocks) for s in starts] + [jnp.arange(PR)]
    )
    source = jnp.take(table, places)
    kept = (source >= PL).astype(jnp.int32)
    one = jnp.ones((1,), jnp.int32)
    ways = quarter_blocks // 2
    n = quarter_blocks

    def rows_at(first, size, adds, name, scale=one, ways=ways):
        return take_rows(
            front, mask, source[first : first + size], kept[first : first + size], scale, ways,
            adds, name,
        )

    diagonal = flip(rows_at(0, n, [], "far_rows"), "grp", CORE)
    first = rows_at(
        4 * n, PR, [(root_front, 0, 0)], "first_rows", (g == 0).astype(jnp.int32).reshape(1), PR
    )
    first = first + flip(first, "grp", CORE)
    head = table_hop(head, last)
    rest = table_hop(rest, last - 1)
    w_lead = lead_hop(w_lead, 0)
    head, rest, w_lead, diagonal, first = lax.optimization_barrier(
        (head, rest, w_lead, diagonal, first)
    )
    first = first + flip(first, "grp", CHIP)
    rest = table_hop(rest, last)
    for at in range(1, last):
        w_lead = lead_hop(w_lead, at)

    work = [pltpu.VMEM((b, 2 * b), f32)]
    sq = shape((b, b), f32)
    sqh = shape((b, b), bf16)
    logs = shape((8, b), f32)

    def w_spec(k):
        return pl.BlockSpec((b, cols), lambda i: (k, 0))

    p01, inv0, inv1, x01, log01 = pl.pallas_call(
        leaf_two,
        grid=(1,),
        in_specs=[vmem, w_spec(0), w_spec(1), vmem],
        out_specs=[vmem] * 5,
        out_shape=(shape((2 * b, cols), bf16), sq, sq, sqh, logs),
        scratch_shapes=work,
        name="leaf_two",
    )(head, front, front, mask)

    p01, diagonal = lax.optimization_barrier((p01, diagonal))
    far = [rows_at(n + i * ways, ways, [(diagonal, 0, i)], "far_sum") for i in range(2)]
    far = [flip(part, "grp", CHIP) for part in far]

    def across(value):
        far_value = flip(value, "grp", CHIP)
        both = jnp.concatenate([value, far_value], axis=0)
        return jnp.concatenate([both, flip(both, "grp", CORE)], axis=0)

    d01 = across(p01)
    rest, d01 = lax.optimization_barrier((rest, d01))
    w_lead = lead_hop(w_lead, last)
    w_lead = w_lead[0] if leads == 1 else jnp.concatenate(w_lead, axis=1)
    lead_rows = (PL * b + LOG_ROWS) * pr // cols
    pack = pl.pallas_call(
        leaf_last,
        grid=(1,),
        in_specs=[vmem, w_spec(2)] + [vmem] * 8,
        out_specs=vmem,
        out_shape=shape((b + lead_rows, cols), bf16),
        scratch_shapes=[pltpu.VMEM((b, b), f32)] + work,
        name="leaf_last",
    )(rest, front, w_lead, table_rows, mask, p01, inv0, inv1, x01, log01)
    near = flip(rows_at(2 * n, n, [], "near_rows"), "grp", CORE)

    def among(offsets):
        found = jnp.zeros((), jnp.bool_)
        for h in offsets:
            found = found | (zone == (g ^ h))
        return found

    def zone_hop(state):
        have, held, _ = state
        bit = groups // 2 // len(have)
        pairs = []
        for gi in range(groups):
            for h in have:
                for j in range(spread):
                    src = (gi ^ h) * spread + j
                    dst = (gi ^ h ^ bit) * spread + j
                    pairs.append((gi * members + src, gi * members + dst))
        got = lax.ppermute(held, ("grp", "mem"), pairs)
        new = [h ^ bit for h in have]
        return have + new, jnp.where(among(new), got, held), (new, got)

    def inner_hop(stage, i):
        offsets, value = stage
        pairs = []
        for gi in range(groups):
            for h in offsets:
                for j in range(spread):
                    at = gi * members + (gi ^ h) * spread
                    pairs.append((at + j, at + (j ^ i)))
        return lax.ppermute(value, ("grp", "mem"), pairs)

    def inner_hops(state, early=None):
        have, held, last_stage = state
        slots = [held]
        for i in range(1, spread):
            if early is None:
                slots.append(inner_hop((have, held), i))
            else:
                got = inner_hop(last_stage, i)
                slots.append(jnp.where(among(last_stage[0]), got, early[i - 1]))
        return slots

    def early_hops(state):
        return [inner_hop((state[0], state[1]), i) for i in range(1, spread)]

    corner = [first[:, :lead_cols]] * leads
    for at in range(last + 1):
        corner = lead_hop(corner, at)
    corner = corner[0] if leads == 1 else jnp.concatenate(corner, axis=1)
    s01 = zone_hop(([0], d01, None))
    pack, far[0] = lax.optimization_barrier((pack, far[0]))
    pack = across(pack)
    pack, held = lax.optimization_barrier((pack, s01[1]))
    s01 = (s01[0], held, None)
    early01 = early_hops(s01)
    s01 = zone_hop(s01)
    d2 = pack.reshape(groups, b + lead_rows, cols)[:, :b].reshape(groups * b, cols)
    s2 = zone_hop(([0], d2, None))
    leaves = jnp.stack([g, g ^ CHIP, g ^ CORE, g ^ (CORE | CHIP)])
    q, rinv0, rinv1, rx, logs_out = pl.pallas_call(
        root_step,
        in_specs=[smem] + [vmem] * 4,
        out_shape=(shape((pr, cols), bf16), sq, sq, sqh, logs),
        scratch_shapes=work,
        compiler_params=pltpu.CompilerParams(vmem_limit_bytes=32 << 20),
        name="root_step",
    )(leaves, corner, first, d01, pack)
    q, far[1], held = lax.optimization_barrier((q, far[1], s2[1]))
    s2 = (s2[0], held, None)
    rq = inner_hops(zone_hop(zone_hop(([0], q, None))))
    early2 = early_hops(s2)
    s2 = zone_hop(s2)
    r01 = inner_hops(s01, early01)
    r2 = inner_hops(s2, early2)

    base = rows_at(
        3 * n, n, [(root_front, 0, 0), (near, 0, 0), (far[0], 0, 0), (far[1], 1, 0)], "base_rows"
    )
    slot_of = inner ^ jnp.arange(spread, dtype=jnp.int32)

    def update_body(*refs):
        update_kernel(spread, *refs)

    def whole_spec(array):
        return pl.BlockSpec(array.shape, lambda s, *pre: (0, 0))

    fixed = [d01, d2] + r01 + r2 + [rinv0, rinv1, rx]
    part, panel = pl.pallas_call(
        update_body,
        grid_spec=pltpu.PrefetchScalarGridSpec(
            num_scalar_prefetch=1,
            grid=(spread,),
            in_specs=[pl.BlockSpec((cols, cols), lambda s, place: (place[s], 0))]
            + [whole_spec(array) for array in fixed],
            out_specs=[
                pl.BlockSpec((cols, cols), lambda s, place: (s, 0)),
                pl.BlockSpec((cols, lead_cols if leads > 1 else pr), lambda s, place: (s, 0)),
            ],
        ),
        out_shape=(shape((quarter, cols), f32), shape((quarter, lead_cols), f32)),
        compiler_params=pltpu.CompilerParams(vmem_limit_bytes=48 << 20),
        name="update",
    )(slot_of, base, *fixed)
    if leads > 1:
        first_col = jnp.minimum(m, leads - 1) * lead_cols
        panel = jnp.concatenate([rows.astype(f32).T for rows in rq], axis=0)
        panel = lax.dynamic_slice_in_dim(panel, first_col, lead_cols, 1)
    info = jnp.concatenate([g * quarter + slot_of * cols, (m * cols).reshape(1)])

    def finish_body(*refs):
        finish_kernel(spread, *refs)

    root_factor = pl.pallas_call(
        finish_body,
        grid_spec=pltpu.PrefetchScalarGridSpec(
            num_scalar_prefetch=2,
            grid=(spread,),
            in_specs=[
                pl.BlockSpec((cols, cols), lambda s, place, info: (s, 0)),
                pl.BlockSpec((cols, lead_cols), lambda s, place, info: (s, 0)),
                whole_spec(q),
            ]
            + [whole_spec(rows) for rows in rq],
            out_specs=pl.BlockSpec((cols, cols), lambda s, place, info: (place[s], 0)),
        ),
        out_shape=shape((quarter, cols), f32),
        compiler_params=pltpu.CompilerParams(vmem_limit_bytes=32 << 20),
        name="finish",
    )(slot_of, info, part, panel, q, *rq)
    return root_factor, logs_out[0, : groups + 1]


def solution(mesh):
    in_specs = (P("grp", None, "mem"), P("grp", "mem"), P("grp", "mem"))
    out_specs = (P("grp", "mem"), P())
    return jax.shard_map(local, mesh=mesh, in_specs=in_specs, out_specs=out_specs, check_vma=False)
```

```python
import jax
import jax.numpy as jnp
from jax import lax
from jax.experimental import pallas as pl
from jax.experimental.pallas import tpu as pltpu
from jax.sharding import PartitionSpec as P

PL = 3
PR = 2
HIGHEST = lax.Precision.HIGHEST
ROWS = 64
SUB = 16
LOG_ROWS = 32
B_ROWS = 128
CORE, CHIP = 1, 2
f32, bf16 = jnp.float32, jnp.bfloat16


def mm(lhs, rhs):
    return jnp.dot(lhs, rhs, precision=HIGHEST, preferred_element_type=f32)


def mm_t(lhs, rhs):
    return lax.dot_general(
        lhs, rhs, (((1,), (1,)), ((), ())), precision=HIGHEST, preferred_element_type=f32
    )


def tdot(lhs, rhs):
    return lax.dot_general(lhs, rhs, (((0,), (0,)), ((), ())), preferred_element_type=f32)


def bits(size):
    out, bit = [], 1
    while bit < size:
        out.append(bit)
        bit *= 2
    return out


def flip(value, axis, bit):
    size = lax.axis_size(axis)
    return lax.ppermute(value, axis, [(i, i ^ bit) for i in range(size)])


def shape(dims, dtype):
    return jax.ShapeDtypeStruct(dims, dtype)


def invert_factor(block, work, inverse_ref):
    size = block.shape[0]
    rows = lax.broadcasted_iota(jnp.int32, (size, size), 0)
    cols = lax.broadcasted_iota(jnp.int32, (size, size), 1)
    work[:, :size] = block
    work[:, size:] = jnp.where(rows == cols, 1.0, 0.0)
    sub = lax.broadcasted_iota(jnp.int32, (ROWS, size), 0)
    lane = lax.broadcasted_iota(jnp.int32, (ROWS, size), 1)
    log_sum = jnp.zeros((1, 1), f32)
    for first in range(0, size, ROWS):
        left = work[first : first + ROWS, :size]
        right = work[first : first + ROWS, size:]
        for start in range(0, ROWS, SUB):
            at = first + start
            columns = [
                jnp.broadcast_to(left[:, at + j : at + j + 1], (ROWS, size)) for j in range(SUB)
            ]
            for j in range(SUB):
                i = start + j
                if i == ROWS - 1:
                    break
                factor = jnp.where(sub > i, columns[j], 0.0) * (1.0 / columns[j][i : i + 1, :])
                for k in range(j + 1, SUB):
                    columns[k] = columns[k] - factor * columns[k][i : i + 1, :]
                left = left - factor * left[i : i + 1, :]
                right = right - factor * right[i : i + 1, :]
        pivot = jnp.sum(jnp.where(lane == sub + first, left, 0.0), axis=1, keepdims=True)
        scale = lax.rsqrt(pivot)
        left, right = left * scale, right * scale
        inverse_ref[first : first + ROWS, :] = right
        log_sum = log_sum + jnp.sum(jnp.log(pivot), axis=0, keepdims=True)
        if first + ROWS < size:
            update = lax.dot_general(
                left, jnp.concatenate([left, right], axis=1), (((0,), (0,)), ((), ())),
                precision=HIGHEST, preferred_element_type=f32,
            )
            work[first + ROWS :, :] = work[first + ROWS :, :] - update[first + ROWS :, :]
    return log_sum


def pick_pivots(owner_ref, at_ref, front_ref, table_ref, head_ref, rest_ref, mask_ref, lead_ref):
    b = head_ref.shape[1]
    per = front_ref.shape[1] // b
    for k in range(PL):
        total = jnp.zeros(((k + 1) * b, b), f32)
        for t in range(per):
            part = front_ref[: (k + 1) * b, t * b : (t + 1) * b]
            total = total + jnp.where(owner_ref[t] == k, part, 0.0)
        if k == 0:
            head_ref[:b, :] = total
        elif k == 1:
            head_ref[b:, :] = total
        else:
            rest_ref[...] = total
    lane = lax.broadcasted_iota(jnp.int32, (8, b), 1)
    table = jnp.zeros((8, b), f32)
    for t in range(per):
        table = table + jnp.where(lane == at_ref[0] + t, owner_ref[t].astype(f32), 0.0)
        keep = jnp.where(owner_ref[t] >= PL, 1.0, 0.0).astype(f32)
        mask_ref[:, t * b : (t + 1) * b] = jnp.full((8, b), keep, f32)
    table_ref[...] = table
    lead_ref[...] = front_ref[:, : lead_ref.shape[1]]


def leaf_two(head_ref, w0_ref, w1_ref, mask_ref, p_ref, inv0_ref, inv1_ref, x_ref, log_ref, work):
    b = w0_ref.shape[0]
    c00, c01, c11 = [head_ref[i * b : (i + 1) * b, :] for i in range(3)]
    keep = mask_ref[:1, :] > 0.0
    log0 = invert_factor(c00, work, inv0_ref)
    x01 = mm(inv0_ref[...], c01).astype(bf16)
    x_ref[...] = x01
    p0 = mm(inv0_ref[...], w0_ref[...]).astype(bf16)
    log1 = invert_factor(c11 - tdot(x01, x01), work, inv1_ref)
    p1 = mm(inv1_ref[...], w1_ref[...] - tdot(x01, p0)).astype(bf16)
    p_ref[:b, :] = jnp.where(keep, p0, jnp.zeros_like(p0))
    p_ref[b:, :] = jnp.where(keep, p1, jnp.zeros_like(p1))
    log_ref[...] = jnp.broadcast_to(log0 + log1, log_ref.shape)


def leaf_last(
    rest_ref, w2_ref, w_lead_ref, table_ref, mask_ref, p_ref, inv0_ref, inv1_ref, x_ref, log_ref,
    out_ref, inv, work,
):
    b, cols = w2_ref.shape
    wide = w_lead_ref.shape[1] if w_lead_ref.shape[1] > cols else PR * b
    c02, c12, c22 = [rest_ref[i * b : (i + 1) * b, :] for i in range(3)]
    inv0, inv1, x01 = inv0_ref[...], inv1_ref[...], x_ref[...]
    x02 = mm(inv0, c02).astype(bf16)
    x12 = mm(inv1, c12 - tdot(x01, x02)).astype(bf16)
    log2 = invert_factor(c22 - tdot(x02, x02) - tdot(x12, x12), work, inv)
    inv2 = inv[...]
    keep = mask_ref[:1, :] > 0.0
    panel = mm(inv2, w2_ref[...] - tdot(x02, p_ref[:b, :]) - tdot(x12, p_ref[b:, :])).astype(bf16)
    out_ref[:b, :] = jnp.where(keep, panel, jnp.zeros_like(panel))
    lane = lax.broadcasted_iota(jnp.int32, (1, wide), 1)
    block = jnp.zeros((1, wide), f32)
    for t in range(PR):
        inside = (lane >= t * b) & (lane < (t + 1) * b)
        block = jnp.where(inside, table_ref[:1, t : t + 1], block)
    keep = block > PL - 0.5
    lead0 = mm(inv0, w_lead_ref[:b, :]).astype(bf16)
    lead1 = mm(inv1, w_lead_ref[b : 2 * b, :] - tdot(x01, lead0)).astype(bf16)
    lead2 = w_lead_ref[2 * b :, :] - tdot(x02, lead0) - tdot(x12, lead1)
    lead2 = mm(inv2, lead2).astype(bf16)
    value = log_ref[:1, :1] + log2
    line = lax.broadcasted_iota(jnp.int32, (LOG_ROWS, wide), 0)
    rows = jnp.zeros((LOG_ROWS, wide), f32)
    for i in range(3):
        part = value.astype(bf16).astype(f32)
        rows = jnp.where(line == i, part, rows)
        value = value - part
    leads = [jnp.where(keep, lead, jnp.zeros_like(lead)) for lead in (lead0, lead1, lead2)]
    whole = jnp.concatenate(leads + [rows.astype(bf16)], axis=0)
    if cols >= wide:
        split = cols // wide
        tall = whole.shape[0] // split
        for i in range(split):
            out_ref[b:, i * wide : (i + 1) * wide] = whole[i * tall : (i + 1) * tall, :]
    else:
        tall = whole.shape[0]
        for i in range(wide // cols):
            out_ref[b + i * tall : b + (i + 1) * tall, :] = whole[:, i * cols : (i + 1) * cols]


def rows_kernel(ways, spans, *refs):
    keep_ref, scale_ref = refs[1:3]
    fronts = refs[3 : 3 + ways]
    mask_ref = refs[3 + ways]
    adds = refs[4 + ways : -1]
    out_ref = refs[-1]
    step = pl.program_id(0)
    b = fronts[0].shape[0]
    keep_cols = mask_ref[:1, :] > 0.0
    for i, front_ref in enumerate(fronts):
        at = slice(i * b, (i + 1) * b)
        keep = keep_cols & (keep_ref[step * ways + i] > 0)
        total = jnp.where(keep, front_ref[...], 0.0)
        for add_ref, (first, last) in zip(adds, spans):
            use = (step >= first) & (step < last) & (scale_ref[0] > 0)
            total = total + jnp.where(use, add_ref[at, :], 0.0)
        out_ref[at, :] = total


def take_rows(front, mask, source, kept, scale, ways, adds, name):
    b = B_ROWS
    cols = front.shape[1]
    steps = source.shape[0] // ways
    spans, add_specs = [], []
    for array, first, tile in adds:
        tiles = array.shape[0] // (ways * b) - tile
        last = min(steps, first + tiles)
        spans.append((first, last))

        def index(s, *pre, first=first, last=last, tile=tile):
            return (jnp.clip(s, first, last - 1) - first + tile, 0)

        add_specs.append(pl.BlockSpec((ways * b, cols), index))
    front_specs = [
        pl.BlockSpec((b, cols), lambda s, *pre, i=i: (pre[0][s * ways + i], 0)) for i in range(ways)
    ]

    def body(*refs):
        rows_kernel(ways, spans, *refs)

    return pl.pallas_call(
        body,
        grid_spec=pltpu.PrefetchScalarGridSpec(
            num_scalar_prefetch=3,
            grid=(steps,),
            in_specs=front_specs + [pl.BlockSpec((8, cols), lambda s, *pre: (0, 0))] + add_specs,
            out_specs=pl.BlockSpec((ways * b, cols), lambda s, *pre: (s, 0)),
        ),
        out_shape=shape((source.shape[0] * b, cols), f32),
        compiler_params=pltpu.CompilerParams(vmem_limit_bytes=60 << 20),
        name=name,
    )(source, kept, scale, *([front] * ways), mask, *[array for array, _, _ in adds])


def root_step(
    leaf_ref, corner_ref, first_ref, d01_ref, pack_ref,
    q_ref, inv0_ref, inv1_ref, x_ref, log_ref, work,
):
    b = inv0_ref.shape[0]
    cols = first_ref.shape[1]
    wide = corner_ref.shape[1]
    groups = d01_ref.shape[0] // (2 * b)
    pitch = pack_ref.shape[0] // groups
    corner = corner_ref[...]
    top = first_ref[...]
    lane = lax.broadcasted_iota(jnp.int32, (8, b), 1)
    logs = jnp.zeros((8, b), f32)
    for i in range(groups):
        at = i * pitch
        d2 = pack_ref[at : at + b, :]
        packed = pack_ref[at + b : at + pitch, :]
        if cols >= wide:
            parts = [packed[:, j * wide : (j + 1) * wide] for j in range(cols // wide)]
            whole = jnp.concatenate(parts, axis=0)
        else:
            tall = (pitch - b) // (wide // cols)
            parts = [packed[j * tall : (j + 1) * tall, :] for j in range(wide // cols)]
            whole = jnp.concatenate(parts, axis=1)
        lead = whole[: PL * b, :]
        corner = corner - tdot(lead, lead)
        top = top - tdot(lead[: 2 * b, :], d01_ref[i * 2 * b : (i + 1) * 2 * b, :])
        top = top - tdot(lead[2 * b :, :], d2)
        log_sum = jnp.sum(whole[PL * b : PL * b + 16, :b].astype(f32), axis=0, keepdims=True)
        logs = jnp.where(lane == leaf_ref[i], log_sum * (1.0 / (PL * b)), logs)
    log0 = invert_factor(corner[:b, :b], work, inv0_ref)
    x = mm(inv0_ref[...], corner[:b, b:]).astype(bf16)
    x_ref[...] = x
    log1 = invert_factor(corner[b:, b:] - tdot(x, x), work, inv1_ref)
    log_ref[...] = jnp.where(lane == groups, (log0 + log1) * (1.0 / wide), logs)
    q0 = mm(inv0_ref[...], top[:b, :]).astype(bf16)
    q_ref[:b, :] = q0
    q_ref[b:, :] = mm(inv1_ref[...], top[b:, :] - tdot(x, q0)).astype(bf16)


def update_kernel(slots, *refs):
    place_ref, base_ref, d01_ref, d2_ref = refs[:4]
    r01, r2 = refs[4 : 4 + slots], refs[4 + slots : 4 + 2 * slots]
    inv0_ref, inv1_ref, x_ref, out_ref, panel_ref = refs[4 + 2 * slots :]
    b = inv0_ref.shape[0]
    cols = out_ref.shape[1]

    def at_slot(i):
        total = base_ref[...] - tdot(r01[i][...], d01_ref[...]) - tdot(r2[i][...], d2_ref[...])
        out_ref[...] = total
        if cols >= PR * b:
            q0 = mm_t(total[:, :b], inv0_ref[...])
            inside = jnp.dot(q0.astype(bf16), x_ref[...], preferred_element_type=f32)
            panel_ref[:, :b] = q0
            panel_ref[:, b:] = mm_t(total[:, b : PR * b] - inside, inv1_ref[...])
        else:
            panel_ref[...] = jnp.zeros_like(panel_ref)

    for i in range(slots):
        pl.when(pl.program_id(0) == i)(lambda i=i: at_slot(i))


def finish_kernel(slots, *refs):
    place_ref, info_ref, part_ref, panel_ref, q_ref = refs[:5]
    rq, out_ref = refs[5 : 5 + slots], refs[5 + slots]
    rows, cols = out_ref.shape
    wide = q_ref.shape[0]
    b = wide // PR

    def at_slot(i):
        row = info_ref[i] + lax.broadcasted_iota(jnp.int32, (rows, cols), 0)
        total = part_ref[...] - tdot(rq[i][...], q_ref[...])
        total = jnp.where(row >= wide, total, 0.0)
        width = min(wide, cols)
        col = info_ref[slots] + lax.broadcasted_iota(jnp.int32, (rows, width), 1)
        panel = panel_ref[...]
        panel = jnp.where((row[:, :width] >= b) | (col < b), panel, 0.0)
        out_ref[:, :width] = jnp.where(col < wide, panel, total[:, :width])
        if width < cols:
            out_ref[:, width:] = total[:, width:]

    for i in range(slots):
        pl.when(pl.program_id(0) == i)(lambda i=i: at_slot(i))


def local(leaf_fronts, block_owner, root_front):
    members = lax.axis_size("mem")
    groups = lax.axis_size("grp")
    m = lax.axis_index("mem")
    g = lax.axis_index("grp")
    front = leaf_fronts[0]
    order, cols = front.shape
    owner = block_owner[0]
    per = owner.shape[0]
    b = cols // per
    count = order // b
    quarter = order // groups
    spread = members // groups
    quarter_blocks = quarter // b
    pr = PR * b
    lead_cols = min(pr, cols)
    leads = pr // lead_cols
    zone, inner = m // spread, m % spread
    smem = pl.BlockSpec(memory_space=pltpu.SMEM)
    vmem = pl.BlockSpec(memory_space=pltpu.VMEM)

    def lead_hop(value, at):
        bit = bits(members)[-1 - at]
        parts = []
        for root in range(leads):
            held = value[root]
            pairs = [(root ^ i, root ^ i ^ bit) for i in range(0, members, 2 * bit)]
            got = lax.ppermute(held, "mem", pairs)
            parts.append(jnp.where((m ^ root) % (2 * bit) == bit, got, held))
        return parts

    table_rows, head, rest, mask, w_lead = pl.pallas_call(
        pick_pivots,
        grid=(1,),
        in_specs=[smem, smem, pl.BlockSpec((PL * b, cols), lambda i: (0, 0))],
        out_specs=[vmem] * 5,
        out_shape=(
            shape((8, b), f32), shape((3 * b, b), f32), shape((3 * b, b), f32),
            shape((8, cols), f32), shape((PL * b, lead_cols), f32),
        ),
        name="pick_pivots",
    )(owner, (m * per).reshape(1), front)
    hops = bits(members)
    last = len(hops) - 1
    w_lead = [w_lead] * leads

    def table_hop(value, at):
        return value + flip(value, "mem", hops[at])

    tie = lax.optimization_barrier
    for at in range(last + 1):
        table_rows = table_hop(table_rows, at)
    head = table_hop(head, 0)
    table_rows, head, rest, w_lead = tie((table_rows, head, rest, w_lead))
    table = table_rows[0, :count].astype(jnp.int32)

    starts = [g ^ (CORE | CHIP), g ^ CHIP, g ^ CORE, g]
    places = jnp.concatenate(
        [s * quarter_blocks + jnp.arange(quarter_blocks) for s in starts] + [jnp.arange(PR)]
    )
    source = jnp.take(table, places)
    kept = (source >= PL).astype(jnp.int32)
    one = jnp.ones((1,), jnp.int32)
    ways = quarter_blocks // 2
    n = quarter_blocks

    def rows_at(first, size, adds, name, scale=one, ways=ways):
        return take_rows(
            front, mask, source[first : first + size], kept[first : first + size], scale, ways,
            adds, name,
        )

    diagonal = rows_at(0, n, [], "far_rows")
    first = rows_at(
        4 * n, PR, [(root_front, 0, 0)], "first_rows", (g == 0).astype(jnp.int32).reshape(1), PR
    )
    for at in range(1, last):
        head = table_hop(head, at)
        rest = table_hop(rest, at - 1)
    head, rest, diagonal, first, w_lead = tie((head, rest, diagonal, first, w_lead))
    near = rows_at(2 * n, n, [], "near_rows")
    diagonal = flip(diagonal, "grp", CORE)
    first = first + flip(first, "grp", CORE)
    head = table_hop(head, last)
    rest = table_hop(rest, last - 1)
    w_lead = lead_hop(w_lead, 0)
    head, rest, w_lead, diagonal, first, near = tie((head, rest, w_lead, diagonal, first, near))
    near = flip(near, "grp", CORE)
    first = first + flip(first, "grp", CHIP)
    rest = table_hop(rest, last)
    for at in range(1, last):
        w_lead = lead_hop(w_lead, at)

    work = [pltpu.VMEM((b, 2 * b), f32)]
    sq = shape((b, b), f32)
    sqh = shape((b, b), bf16)
    logs = shape((8, b), f32)

    def w_spec(k):
        return pl.BlockSpec((b, cols), lambda i: (k, 0))

    p01, inv0, inv1, x01, log01 = pl.pallas_call(
        leaf_two,
        grid=(1,),
        in_specs=[vmem, w_spec(0), w_spec(1), vmem],
        out_specs=[vmem] * 5,
        out_shape=(shape((2 * b, cols), bf16), sq, sq, sqh, logs),
        scratch_shapes=work,
        name="leaf_two",
    )(head, front, front, mask)

    p01, rest, w_lead, first = tie((p01, rest, w_lead, first))

    def across(value):
        far_value = flip(value, "grp", CHIP)
        both = jnp.concatenate([value, far_value], axis=0)
        return jnp.concatenate([both, flip(both, "grp", CORE)], axis=0)

    d01 = across(p01)
    rest, d01 = tie((rest, d01))
    corner = lead_hop([first[:, :lead_cols]] * leads, 0)
    w_lead = lead_hop(w_lead, last)
    w_lead = w_lead[0] if leads == 1 else jnp.concatenate(w_lead, axis=1)
    lead_rows = (PL * b + LOG_ROWS) * pr // cols
    pack = pl.pallas_call(
        leaf_last,
        grid=(1,),
        in_specs=[vmem, w_spec(2)] + [vmem] * 8,
        out_specs=vmem,
        out_shape=shape((b + lead_rows, cols), bf16),
        scratch_shapes=[pltpu.VMEM((b, b), f32)] + work,
        name="leaf_last",
    )(rest, front, w_lead, table_rows, mask, p01, inv0, inv1, x01, log01)

    def among(offsets):
        found = jnp.zeros((), jnp.bool_)
        for h in offsets:
            found = found | (zone == (g ^ h))
        return found

    def zone_hop(state):
        have, held, _ = state
        bit = groups // 2 // len(have)
        pairs = []
        for gi in range(groups):
            for h in have:
                for j in range(spread):
                    src = (gi ^ h) * spread + j
                    dst = (gi ^ h ^ bit) * spread + j
                    pairs.append((gi * members + src, gi * members + dst))
        got = lax.ppermute(held, ("grp", "mem"), pairs)
        new = [h ^ bit for h in have]
        return have + new, jnp.where(among(new), got, held), (new, got)

    def inner_hop(stage, i):
        offsets, value = stage
        pairs = []
        for gi in range(groups):
            for h in offsets:
                for j in range(spread):
                    at = gi * members + (gi ^ h) * spread
                    pairs.append((at + j, at + (j ^ i)))
        return lax.ppermute(value, ("grp", "mem"), pairs)

    def inner_hops(state, early=None):
        have, held, last_stage = state
        slots = [held]
        for i in range(1, spread):
            if early is None:
                slots.append(inner_hop((have, held), i))
            else:
                got = inner_hop(last_stage, i)
                slots.append(jnp.where(among(last_stage[0]), got, early[i - 1]))
        return slots

    def early_hops(state):
        return [inner_hop((state[0], state[1]), i) for i in range(1, spread)]

    s01 = zone_hop(([0], d01, None))
    pack_far = flip(pack, "grp", CHIP)
    pack, pack_far, diagonal, *corner = tie((pack, pack_far, diagonal, *corner))
    far_in = [rows_at(n + i * ways, ways, [(diagonal, 0, i)], "far_sum") for i in range(2)]
    for at in range(1, last + 1):
        corner = lead_hop(corner, at)
    corner = corner[0] if leads == 1 else jnp.concatenate(corner, axis=1)
    pack = jnp.concatenate([pack, pack_far], axis=0)
    pack = jnp.concatenate([pack, flip(pack, "grp", CORE)], axis=0)
    pack, held, *far_in = tie((pack, s01[1], *far_in))
    s01 = (s01[0], held, None)
    far = [flip(part, "grp", CHIP) for part in far_in]
    early01 = early_hops(s01)
    s01 = zone_hop(s01)
    d2 = pack.reshape(groups, b + lead_rows, cols)[:, :b].reshape(groups * b, cols)
    s2 = zone_hop(([0], d2, None))
    leaves = jnp.stack([g, g ^ CHIP, g ^ CORE, g ^ (CORE | CHIP)])
    q, rinv0, rinv1, rx, logs_out = pl.pallas_call(
        root_step,
        in_specs=[smem] + [vmem] * 4,
        out_shape=(shape((pr, cols), bf16), sq, sq, sqh, logs),
        scratch_shapes=work,
        compiler_params=pltpu.CompilerParams(vmem_limit_bytes=32 << 20),
        name="root_step",
    )(leaves, corner, first, d01, pack)
    q, held, far[0], *early01 = tie((q, s2[1], far[0], *early01))
    s2 = (s2[0], held, None)
    rq = inner_hops(zone_hop(zone_hop(([0], q, None))))
    early2 = early_hops(s2)
    s2 = zone_hop(s2)
    r01 = inner_hops(s01, early01)
    r2 = inner_hops(s2, early2)

    base = rows_at(
        3 * n, n, [(root_front, 0, 0), (near, 0, 0), (far[0], 0, 0), (far[1], 1, 0)], "base_rows"
    )
    slot_of = inner ^ jnp.arange(spread, dtype=jnp.int32)

    def update_body(*refs):
        update_kernel(spread, *refs)

    def whole_spec(array):
        return pl.BlockSpec(array.shape, lambda s, *pre: (0, 0))

    fixed = [d01, d2] + r01 + r2 + [rinv0, rinv1, rx]
    part, panel = pl.pallas_call(
        update_body,
        grid_spec=pltpu.PrefetchScalarGridSpec(
            num_scalar_prefetch=1,
            grid=(spread,),
            in_specs=[pl.BlockSpec((cols, cols), lambda s, place: (place[s], 0))]
            + [whole_spec(array) for array in fixed],
            out_specs=[
                pl.BlockSpec((cols, cols), lambda s, place: (s, 0)),
                pl.BlockSpec((cols, lead_cols if leads > 1 else pr), lambda s, place: (s, 0)),
            ],
        ),
        out_shape=(shape((quarter, cols), f32), shape((quarter, lead_cols), f32)),
        compiler_params=pltpu.CompilerParams(vmem_limit_bytes=48 << 20),
        name="update",
    )(slot_of, base, *fixed)
    if leads > 1:
        first_col = jnp.minimum(m, leads - 1) * lead_cols
        panel = jnp.concatenate([rows.astype(f32).T for rows in rq], axis=0)
        panel = lax.dynamic_slice_in_dim(panel, first_col, lead_cols, 1)
    info = jnp.concatenate([g * quarter + slot_of * cols, (m * cols).reshape(1)])

    def finish_body(*refs):
        finish_kernel(spread, *refs)

    root_factor = pl.pallas_call(
        finish_body,
        grid_spec=pltpu.PrefetchScalarGridSpec(
            num_scalar_prefetch=2,
            grid=(spread,),
            in_specs=[
                pl.BlockSpec((cols, cols), lambda s, place, info: (s, 0)),
                pl.BlockSpec((cols, lead_cols), lambda s, place, info: (s, 0)),
                whole_spec(q),
            ]
            + [whole_spec(rows) for rows in rq],
            out_specs=pl.BlockSpec((cols, cols), lambda s, place, info: (place[s], 0)),
        ),
        out_shape=shape((quarter, cols), f32),
        compiler_params=pltpu.CompilerParams(vmem_limit_bytes=32 << 20),
        name="finish",
    )(slot_of, info, part, panel, q, *rq)
    return root_factor, logs_out[0, : groups + 1]


def solution(mesh):
    in_specs = (P("grp", None, "mem"), P("grp", "mem"), P("grp", "mem"))
    out_specs = (P("grp", "mem"), P())
    return jax.shard_map(local, mesh=mesh, in_specs=in_specs, out_specs=out_specs, check_vma=False)
```

```python
import jax
import jax.numpy as jnp
from jax import lax
from jax.experimental import pallas as pl
from jax.experimental.pallas import tpu as pltpu
from jax.sharding import PartitionSpec as P

PL = 3
PR = 2
HIGHEST = lax.Precision.HIGHEST
ROWS = 64
SUB = 16
LOG_ROWS = 32
B_ROWS = 128
CORE, CHIP = 1, 2
f32, bf16 = jnp.float32, jnp.bfloat16


def mm(lhs, rhs):
    return jnp.dot(lhs, rhs, precision=HIGHEST, preferred_element_type=f32)


def mm_t(lhs, rhs):
    return lax.dot_general(
        lhs, rhs, (((1,), (1,)), ((), ())), precision=HIGHEST, preferred_element_type=f32
    )


def tdot(lhs, rhs):
    return lax.dot_general(lhs, rhs, (((0,), (0,)), ((), ())), preferred_element_type=f32)


def bits(size):
    out, bit = [], 1
    while bit < size:
        out.append(bit)
        bit *= 2
    return out


def flip(value, axis, bit):
    size = lax.axis_size(axis)
    return lax.ppermute(value, axis, [(i, i ^ bit) for i in range(size)])


def shape(dims, dtype):
    return jax.ShapeDtypeStruct(dims, dtype)


def invert_factor(block, work, inverse_ref):
    size = block.shape[0]
    rows = lax.broadcasted_iota(jnp.int32, (size, size), 0)
    cols = lax.broadcasted_iota(jnp.int32, (size, size), 1)
    work[:, :size] = block
    work[:, size:] = jnp.where(rows == cols, 1.0, 0.0)
    sub = lax.broadcasted_iota(jnp.int32, (ROWS, size), 0)
    lane = lax.broadcasted_iota(jnp.int32, (ROWS, size), 1)
    log_sum = jnp.zeros((1, 1), f32)
    for first in range(0, size, ROWS):
        left = work[first : first + ROWS, :size]
        right = work[first : first + ROWS, size:]
        for start in range(0, ROWS, SUB):
            at = first + start
            columns = [
                jnp.broadcast_to(left[:, at + j : at + j + 1], (ROWS, size)) for j in range(SUB)
            ]
            for j in range(SUB):
                i = start + j
                if i == ROWS - 1:
                    break
                factor = jnp.where(sub > i, columns[j], 0.0) * (1.0 / columns[j][i : i + 1, :])
                for k in range(j + 1, SUB):
                    columns[k] = columns[k] - factor * columns[k][i : i + 1, :]
                left = left - factor * left[i : i + 1, :]
                right = right - factor * right[i : i + 1, :]
        pivot = jnp.sum(jnp.where(lane == sub + first, left, 0.0), axis=1, keepdims=True)
        scale = lax.rsqrt(pivot)
        left, right = left * scale, right * scale
        inverse_ref[first : first + ROWS, :] = right
        log_sum = log_sum + jnp.sum(jnp.log(pivot), axis=0, keepdims=True)
        if first + ROWS < size:
            update = lax.dot_general(
                left, jnp.concatenate([left, right], axis=1), (((0,), (0,)), ((), ())),
                precision=HIGHEST, preferred_element_type=f32,
            )
            work[first + ROWS :, :] = work[first + ROWS :, :] - update[first + ROWS :, :]
    return log_sum


def pick_pivots(owner_ref, at_ref, front_ref, table_ref, head_ref, rest_ref, mask_ref, lead_ref):
    b = head_ref.shape[1]
    per = front_ref.shape[1] // b
    for k in range(PL):
        total = jnp.zeros(((k + 1) * b, b), f32)
        for t in range(per):
            part = front_ref[: (k + 1) * b, t * b : (t + 1) * b]
            total = total + jnp.where(owner_ref[t] == k, part, 0.0)
        if k == 0:
            head_ref[:b, :] = total
        elif k == 1:
            head_ref[b:, :] = total
        else:
            rest_ref[...] = total
    lane = lax.broadcasted_iota(jnp.int32, (8, b), 1)
    table = jnp.zeros((8, b), f32)
    for t in range(per):
        table = table + jnp.where(lane == at_ref[0] + t, owner_ref[t].astype(f32), 0.0)
        keep = jnp.where(owner_ref[t] >= PL, 1.0, 0.0).astype(f32)
        mask_ref[:, t * b : (t + 1) * b] = jnp.full((8, b), keep, f32)
    table_ref[...] = table
    lead_ref[...] = front_ref[:, : lead_ref.shape[1]]


def leaf_two(head_ref, w0_ref, w1_ref, mask_ref, p_ref, inv0_ref, inv1_ref, x_ref, log_ref, work):
    b = w0_ref.shape[0]
    c00, c01, c11 = [head_ref[i * b : (i + 1) * b, :] for i in range(3)]
    keep = mask_ref[:1, :] > 0.0
    log0 = invert_factor(c00, work, inv0_ref)
    x01 = mm(inv0_ref[...], c01).astype(bf16)
    x_ref[...] = x01
    p0 = mm(inv0_ref[...], w0_ref[...]).astype(bf16)
    log1 = invert_factor(c11 - tdot(x01, x01), work, inv1_ref)
    p1 = mm(inv1_ref[...], w1_ref[...] - tdot(x01, p0)).astype(bf16)
    p_ref[:b, :] = jnp.where(keep, p0, jnp.zeros_like(p0))
    p_ref[b:, :] = jnp.where(keep, p1, jnp.zeros_like(p1))
    log_ref[...] = jnp.broadcast_to(log0 + log1, log_ref.shape)


def leaf_last(
    rest_ref, w2_ref, w_lead_ref, table_ref, mask_ref, p_ref, inv0_ref, inv1_ref, x_ref, log_ref,
    out_ref, inv, work,
):
    b, cols = w2_ref.shape
    wide = w_lead_ref.shape[1] if w_lead_ref.shape[1] > cols else PR * b
    c02, c12, c22 = [rest_ref[i * b : (i + 1) * b, :] for i in range(3)]
    inv0, inv1, x01 = inv0_ref[...], inv1_ref[...], x_ref[...]
    x02 = mm(inv0, c02).astype(bf16)
    x12 = mm(inv1, c12 - tdot(x01, x02)).astype(bf16)
    log2 = invert_factor(c22 - tdot(x02, x02) - tdot(x12, x12), work, inv)
    inv2 = inv[...]
    keep = mask_ref[:1, :] > 0.0
    panel = mm(inv2, w2_ref[...] - tdot(x02, p_ref[:b, :]) - tdot(x12, p_ref[b:, :])).astype(bf16)
    out_ref[:b, :] = jnp.where(keep, panel, jnp.zeros_like(panel))
    lane = lax.broadcasted_iota(jnp.int32, (1, wide), 1)
    block = jnp.zeros((1, wide), f32)
    for t in range(PR):
        inside = (lane >= t * b) & (lane < (t + 1) * b)
        block = jnp.where(inside, table_ref[:1, t : t + 1], block)
    keep = block > PL - 0.5
    lead0 = mm(inv0, w_lead_ref[:b, :]).astype(bf16)
    lead1 = mm(inv1, w_lead_ref[b : 2 * b, :] - tdot(x01, lead0)).astype(bf16)
    lead2 = w_lead_ref[2 * b :, :] - tdot(x02, lead0) - tdot(x12, lead1)
    lead2 = mm(inv2, lead2).astype(bf16)
    value = log_ref[:1, :1] + log2
    line = lax.broadcasted_iota(jnp.int32, (LOG_ROWS, wide), 0)
    rows = jnp.zeros((LOG_ROWS, wide), f32)
    for i in range(3):
        part = value.astype(bf16).astype(f32)
        rows = jnp.where(line == i, part, rows)
        value = value - part
    leads = [jnp.where(keep, lead, jnp.zeros_like(lead)) for lead in (lead0, lead1, lead2)]
    whole = jnp.concatenate(leads + [rows.astype(bf16)], axis=0)
    if cols >= wide:
        split = cols // wide
        tall = whole.shape[0] // split
        for i in range(split):
            out_ref[b:, i * wide : (i + 1) * wide] = whole[i * tall : (i + 1) * tall, :]
    else:
        tall = whole.shape[0]
        for i in range(wide // cols):
            out_ref[b + i * tall : b + (i + 1) * tall, :] = whole[:, i * cols : (i + 1) * cols]


def rows_kernel(ways, spans, *refs):
    keep_ref, scale_ref = refs[1:3]
    fronts = refs[3 : 3 + ways]
    mask_ref = refs[3 + ways]
    adds = refs[4 + ways : -1]
    out_ref = refs[-1]
    step = pl.program_id(0)
    b = fronts[0].shape[0]
    keep_cols = mask_ref[:1, :] > 0.0
    for i, front_ref in enumerate(fronts):
        at = slice(i * b, (i + 1) * b)
        keep = keep_cols & (keep_ref[step * ways + i] > 0)
        total = jnp.where(keep, front_ref[...], 0.0)
        for add_ref, (first, last) in zip(adds, spans):
            use = (step >= first) & (step < last) & (scale_ref[0] > 0)
            total = total + jnp.where(use, add_ref[at, :], 0.0)
        out_ref[at, :] = total


def take_rows(front, mask, source, kept, scale, ways, adds, name):
    b = B_ROWS
    cols = front.shape[1]
    steps = source.shape[0] // ways
    spans, add_specs = [], []
    for array, first, tile in adds:
        tiles = array.shape[0] // (ways * b) - tile
        last = min(steps, first + tiles)
        spans.append((first, last))

        def index(s, *pre, first=first, last=last, tile=tile):
            return (jnp.clip(s, first, last - 1) - first + tile, 0)

        add_specs.append(pl.BlockSpec((ways * b, cols), index))
    front_specs = [
        pl.BlockSpec((b, cols), lambda s, *pre, i=i: (pre[0][s * ways + i], 0)) for i in range(ways)
    ]

    def body(*refs):
        rows_kernel(ways, spans, *refs)

    return pl.pallas_call(
        body,
        grid_spec=pltpu.PrefetchScalarGridSpec(
            num_scalar_prefetch=3,
            grid=(steps,),
            in_specs=front_specs + [pl.BlockSpec((8, cols), lambda s, *pre: (0, 0))] + add_specs,
            out_specs=pl.BlockSpec((ways * b, cols), lambda s, *pre: (s, 0)),
        ),
        out_shape=shape((source.shape[0] * b, cols), f32),
        compiler_params=pltpu.CompilerParams(vmem_limit_bytes=60 << 20),
        name=name,
    )(source, kept, scale, *([front] * ways), mask, *[array for array, _, _ in adds])


def root_step(
    leaf_ref, corner_ref, first_ref, d01_ref, pack_ref,
    q_ref, inv0_ref, inv1_ref, x_ref, log_ref, work,
):
    b = inv0_ref.shape[0]
    cols = first_ref.shape[1]
    wide = corner_ref.shape[1]
    groups = d01_ref.shape[0] // (2 * b)
    pitch = pack_ref.shape[0] // groups
    corner = corner_ref[...]
    top = first_ref[...]
    lane = lax.broadcasted_iota(jnp.int32, (8, b), 1)
    logs = jnp.zeros((8, b), f32)
    for i in range(groups):
        at = i * pitch
        d2 = pack_ref[at : at + b, :]
        packed = pack_ref[at + b : at + pitch, :]
        if cols >= wide:
            parts = [packed[:, j * wide : (j + 1) * wide] for j in range(cols // wide)]
            whole = jnp.concatenate(parts, axis=0)
        else:
            tall = (pitch - b) // (wide // cols)
            parts = [packed[j * tall : (j + 1) * tall, :] for j in range(wide // cols)]
            whole = jnp.concatenate(parts, axis=1)
        lead = whole[: PL * b, :]
        corner = corner - tdot(lead, lead)
        top = top - tdot(lead[: 2 * b, :], d01_ref[i * 2 * b : (i + 1) * 2 * b, :])
        top = top - tdot(lead[2 * b :, :], d2)
        log_sum = jnp.sum(whole[PL * b : PL * b + 16, :b].astype(f32), axis=0, keepdims=True)
        logs = jnp.where(lane == leaf_ref[i], log_sum * (1.0 / (PL * b)), logs)
    log0 = invert_factor(corner[:b, :b], work, inv0_ref)
    x = mm(inv0_ref[...], corner[:b, b:]).astype(bf16)
    x_ref[...] = x
    log1 = invert_factor(corner[b:, b:] - tdot(x, x), work, inv1_ref)
    log_ref[...] = jnp.where(lane == groups, (log0 + log1) * (1.0 / wide), logs)
    q0 = mm(inv0_ref[...], top[:b, :]).astype(bf16)
    q_ref[:b, :] = q0
    q_ref[b:, :] = mm(inv1_ref[...], top[b:, :] - tdot(x, q0)).astype(bf16)


def update_kernel(slots, *refs):
    place_ref, base_ref, d01_ref, d2_ref = refs[:4]
    r01, r2 = refs[4 : 4 + slots], refs[4 + slots : 4 + 2 * slots]
    inv0_ref, inv1_ref, x_ref, out_ref, panel_ref = refs[4 + 2 * slots :]
    b = inv0_ref.shape[0]
    cols = out_ref.shape[1]

    def at_slot(i):
        total = base_ref[...] - tdot(r01[i][...], d01_ref[...]) - tdot(r2[i][...], d2_ref[...])
        out_ref[...] = total
        if cols >= PR * b:
            q0 = mm_t(total[:, :b], inv0_ref[...])
            inside = jnp.dot(q0.astype(bf16), x_ref[...], preferred_element_type=f32)
            panel_ref[:, :b] = q0
            panel_ref[:, b:] = mm_t(total[:, b : PR * b] - inside, inv1_ref[...])
        else:
            panel_ref[...] = jnp.zeros_like(panel_ref)

    for i in range(slots):
        pl.when(pl.program_id(0) == i)(lambda i=i: at_slot(i))


def finish_kernel(slots, *refs):
    place_ref, info_ref, part_ref, panel_ref, q_ref = refs[:5]
    rq, out_ref = refs[5 : 5 + slots], refs[5 + slots]
    rows, cols = out_ref.shape
    wide = q_ref.shape[0]
    b = wide // PR

    def at_slot(i):
        row = info_ref[i] + lax.broadcasted_iota(jnp.int32, (rows, cols), 0)
        total = part_ref[...] - tdot(rq[i][...], q_ref[...])
        total = jnp.where(row >= wide, total, 0.0)
        width = min(wide, cols)
        col = info_ref[slots] + lax.broadcasted_iota(jnp.int32, (rows, width), 1)
        panel = panel_ref[...]
        panel = jnp.where((row[:, :width] >= b) | (col < b), panel, 0.0)
        out_ref[:, :width] = jnp.where(col < wide, panel, total[:, :width])
        if width < cols:
            out_ref[:, width:] = total[:, width:]

    for i in range(slots):
        pl.when(pl.program_id(0) == i)(lambda i=i: at_slot(i))


def local(leaf_fronts, block_owner, root_front):
    members = lax.axis_size("mem")
    groups = lax.axis_size("grp")
    m = lax.axis_index("mem")
    g = lax.axis_index("grp")
    front = leaf_fronts[0]
    order, cols = front.shape
    owner = block_owner[0]
    per = owner.shape[0]
    b = cols // per
    count = order // b
    quarter = order // groups
    spread = members // groups
    quarter_blocks = quarter // b
    pr = PR * b
    lead_cols = min(pr, cols)
    leads = pr // lead_cols
    zone, inner = m // spread, m % spread
    smem = pl.BlockSpec(memory_space=pltpu.SMEM)
    vmem = pl.BlockSpec(memory_space=pltpu.VMEM)

    hops = bits(members)
    last = len(hops) - 1
    lead_order = [hops[-1], hops[0]] + hops[-2:0:-1]

    def lead_hop(value, at):
        bit, used = lead_order[at], sum(lead_order[:at])
        parts = []
        for root in range(leads):
            held = value[root]
            sources = [root ^ i for i in range(members) if i & ~used == 0]
            got = lax.ppermute(held, "mem", [(src, src ^ bit) for src in sources])
            parts.append(jnp.where((m ^ root) & ~used == bit, got, held))
        return parts

    table_rows, head, rest, mask, w_lead = pl.pallas_call(
        pick_pivots,
        grid=(1,),
        in_specs=[smem, smem, pl.BlockSpec((PL * b, cols), lambda i: (0, 0))],
        out_specs=[vmem] * 5,
        out_shape=(
            shape((8, b), f32), shape((3 * b, b), f32), shape((3 * b, b), f32),
            shape((8, cols), f32), shape((PL * b, lead_cols), f32),
        ),
        name="pick_pivots",
    )(owner, (m * per).reshape(1), front)
    w_lead = [w_lead] * leads

    def table_hop(value, at):
        return value + flip(value, "mem", hops[at])

    tie = lax.optimization_barrier
    for at in range(last + 1):
        table_rows = table_hop(table_rows, at)
    head = table_hop(head, 0)
    w_lead = lead_hop(w_lead, 0)
    table_rows, head, rest, w_lead = tie((table_rows, head, rest, w_lead))
    table = table_rows[0, :count].astype(jnp.int32)

    starts = [g ^ (CORE | CHIP), g ^ CHIP, g ^ CORE, g]
    places = jnp.concatenate(
        [s * quarter_blocks + jnp.arange(quarter_blocks) for s in starts] + [jnp.arange(PR)]
    )
    source = jnp.take(table, places)
    kept = (source >= PL).astype(jnp.int32)
    one = jnp.ones((1,), jnp.int32)
    ways = quarter_blocks // 2
    n = quarter_blocks

    def rows_at(first, size, adds, name, scale=one, ways=ways):
        return take_rows(
            front, mask, source[first : first + size], kept[first : first + size], scale, ways,
            adds, name,
        )

    diagonal = rows_at(0, n, [], "far_rows")
    first = rows_at(
        4 * n, PR, [(root_front, 0, 0)], "first_rows", (g == 0).astype(jnp.int32).reshape(1), PR
    )
    for at in range(1, last):
        head = table_hop(head, at)
        rest = table_hop(rest, at - 1)
    head, rest, diagonal, first, w_lead = tie((head, rest, diagonal, first, w_lead))
    near = rows_at(2 * n, n, [], "near_rows")
    first = first + flip(first, "grp", CORE)
    head = table_hop(head, last)
    rest = table_hop(rest, last - 1)
    w_lead = lead_hop(w_lead, 1)
    head, rest, w_lead, diagonal, first, near = tie((head, rest, w_lead, diagonal, first, near))
    near = flip(near, "grp", CORE)
    diagonal = flip(diagonal, "grp", CORE)
    first = first + flip(first, "grp", CHIP)
    rest = table_hop(rest, last)
    for at in range(2, last + 1):
        w_lead = lead_hop(w_lead, at)

    work = [pltpu.VMEM((b, 2 * b), f32)]
    sq = shape((b, b), f32)
    sqh = shape((b, b), bf16)
    logs = shape((8, b), f32)

    def w_spec(k):
        return pl.BlockSpec((b, cols), lambda i: (k, 0))

    p01, inv0, inv1, x01, log01 = pl.pallas_call(
        leaf_two,
        grid=(1,),
        in_specs=[vmem, w_spec(0), w_spec(1), vmem],
        out_specs=[vmem] * 5,
        out_shape=(shape((2 * b, cols), bf16), sq, sq, sqh, logs),
        scratch_shapes=work,
        name="leaf_two",
    )(head, front, front, mask)

    p01, rest, w_lead, first = tie((p01, rest, w_lead, first))

    def across(value):
        far_value = flip(value, "grp", CHIP)
        both = jnp.concatenate([value, far_value], axis=0)
        return jnp.concatenate([both, flip(both, "grp", CORE)], axis=0)

    d01 = across(p01)
    corner = lead_hop([first[:, :lead_cols]] * leads, 0)
    rest, d01, corner = tie((rest, d01, corner))
    corner = lead_hop(corner, 1)
    w_lead = w_lead[0] if leads == 1 else jnp.concatenate(w_lead, axis=1)
    lead_rows = (PL * b + LOG_ROWS) * pr // cols
    pack = pl.pallas_call(
        leaf_last,
        grid=(1,),
        in_specs=[vmem, w_spec(2)] + [vmem] * 8,
        out_specs=vmem,
        out_shape=shape((b + lead_rows, cols), bf16),
        scratch_shapes=[pltpu.VMEM((b, b), f32)] + work,
        name="leaf_last",
    )(rest, front, w_lead, table_rows, mask, p01, inv0, inv1, x01, log01)

    def among(offsets):
        found = jnp.zeros((), jnp.bool_)
        for h in offsets:
            found = found | (zone == (g ^ h))
        return found

    def zone_hop(state):
        have, held, _ = state
        bit = groups // 2 // len(have)
        pairs = []
        for gi in range(groups):
            for h in have:
                for j in range(spread):
                    src = (gi ^ h) * spread + j
                    dst = (gi ^ h ^ bit) * spread + j
                    pairs.append((gi * members + src, gi * members + dst))
        got = lax.ppermute(held, ("grp", "mem"), pairs)
        new = [h ^ bit for h in have]
        return have + new, jnp.where(among(new), got, held), (new, got)

    def inner_hop(stage, i):
        offsets, value = stage
        pairs = []
        for gi in range(groups):
            for h in offsets:
                for j in range(spread):
                    at = gi * members + (gi ^ h) * spread
                    pairs.append((at + j, at + (j ^ i)))
        return lax.ppermute(value, ("grp", "mem"), pairs)

    def inner_hops(state, early=None):
        have, held, last_stage = state
        slots = [held]
        for i in range(1, spread):
            if early is None:
                slots.append(inner_hop((have, held), i))
            else:
                got = inner_hop(last_stage, i)
                slots.append(jnp.where(among(last_stage[0]), got, early[i - 1]))
        return slots

    def early_hops(state):
        return [inner_hop((state[0], state[1]), i) for i in range(1, spread)]

    s01 = zone_hop(([0], d01, None))
    pack_far = flip(pack, "grp", CHIP)
    pack, pack_far, diagonal, corner = tie((pack, pack_far, diagonal, corner))
    far_in = rows_at(n, ways, [(diagonal, 0, 0)], "far_sum")
    for at in range(2, last + 1):
        corner = lead_hop(corner, at)
    pack = jnp.concatenate([pack, pack_far], axis=0)
    pack = jnp.concatenate([pack, flip(pack, "grp", CORE)], axis=0)
    pack, held, far_in, corner = tie((pack, s01[1], far_in, corner))
    corner = corner[0] if leads == 1 else jnp.concatenate(corner, axis=1)
    s01 = (s01[0], held, None)
    far = [flip(far_in, "grp", CHIP)]
    early01 = early_hops(s01)
    s01 = zone_hop(s01)
    d2 = pack.reshape(groups, b + lead_rows, cols)[:, :b].reshape(groups * b, cols)
    s2 = zone_hop(([0], d2, None))
    leaves = jnp.stack([g, g ^ CHIP, g ^ CORE, g ^ (CORE | CHIP)])
    q, rinv0, rinv1, rx, logs_out = pl.pallas_call(
        root_step,
        in_specs=[smem] + [vmem] * 4,
        out_shape=(shape((pr, cols), bf16), sq, sq, sqh, logs),
        scratch_shapes=work,
        compiler_params=pltpu.CompilerParams(vmem_limit_bytes=32 << 20),
        name="root_step",
    )(leaves, corner, first, d01, pack)
    q, diagonal = tie((q, diagonal))
    sq_hop = zone_hop(([0], q, None))
    far_in = rows_at(n + ways, ways, [(diagonal, 0, 1)], "far_sum")
    far.append(flip(far_in, "grp", CHIP))
    q_held, held, far[0], s01_held, s01_got, *early01 = tie(
        (sq_hop[1], s2[1], far[0], s01[1], s01[2][1], *early01)
    )
    s01 = (s01[0], s01_held, (s01[2][0], s01_got))
    s2 = (s2[0], held, None)
    rq = inner_hops(zone_hop((sq_hop[0], q_held, None)))
    early2 = early_hops(s2)
    s2 = zone_hop(s2)
    r01 = inner_hops(s01, early01)
    r2 = inner_hops(s2, early2)

    base = rows_at(
        3 * n, n, [(root_front, 0, 0), (near, 0, 0), (far[0], 0, 0), (far[1], 1, 0)], "base_rows"
    )
    slot_of = inner ^ jnp.arange(spread, dtype=jnp.int32)

    def update_body(*refs):
        update_kernel(spread, *refs)

    def whole_spec(array):
        return pl.BlockSpec(array.shape, lambda s, *pre: (0, 0))

    fixed = [d01, d2] + r01 + r2 + [rinv0, rinv1, rx]
    part, panel = pl.pallas_call(
        update_body,
        grid_spec=pltpu.PrefetchScalarGridSpec(
            num_scalar_prefetch=1,
            grid=(spread,),
            in_specs=[pl.BlockSpec((cols, cols), lambda s, place: (place[s], 0))]
            + [whole_spec(array) for array in fixed],
            out_specs=[
                pl.BlockSpec((cols, cols), lambda s, place: (s, 0)),
                pl.BlockSpec((cols, lead_cols if leads > 1 else pr), lambda s, place: (s, 0)),
            ],
        ),
        out_shape=(shape((quarter, cols), f32), shape((quarter, lead_cols), f32)),
        compiler_params=pltpu.CompilerParams(vmem_limit_bytes=48 << 20),
        name="update",
    )(slot_of, base, *fixed)
    if leads > 1:
        first_col = jnp.minimum(m, leads - 1) * lead_cols
        panel = jnp.concatenate([rows.astype(f32).T for rows in rq], axis=0)
        panel = lax.dynamic_slice_in_dim(panel, first_col, lead_cols, 1)
    info = jnp.concatenate([g * quarter + slot_of * cols, (m * cols).reshape(1)])

    def finish_body(*refs):
        finish_kernel(spread, *refs)

    root_factor = pl.pallas_call(
        finish_body,
        grid_spec=pltpu.PrefetchScalarGridSpec(
            num_scalar_prefetch=2,
            grid=(spread,),
            in_specs=[
                pl.BlockSpec((cols, cols), lambda s, place, info: (s, 0)),
                pl.BlockSpec((cols, lead_cols), lambda s, place, info: (s, 0)),
                whole_spec(q),
            ]
            + [whole_spec(rows) for rows in rq],
            out_specs=pl.BlockSpec((cols, cols), lambda s, place, info: (place[s], 0)),
        ),
        out_shape=shape((quarter, cols), f32),
        compiler_params=pltpu.CompilerParams(vmem_limit_bytes=32 << 20),
        name="finish",
    )(slot_of, info, part, panel, q, *rq)
    return root_factor, logs_out[0, : groups + 1]


def solution(mesh):
    in_specs = (P("grp", None, "mem"), P("grp", "mem"), P("grp", "mem"))
    out_specs = (P("grp", "mem"), P())
    return jax.shard_map(local, mesh=mesh, in_specs=in_specs, out_specs=out_specs, check_vma=False)
```

```python
import jax
import jax.numpy as jnp
from jax import lax
from jax.experimental import pallas as pl
from jax.experimental.pallas import tpu as pltpu
from jax.sharding import PartitionSpec as P

PL = 3
PR = 2
HIGHEST = lax.Precision.HIGHEST
ROWS = 64
SUB = 16
LOG_ROWS = 32
B_ROWS = 128
CORE, CHIP = 1, 2
f32, bf16 = jnp.float32, jnp.bfloat16


def mm(lhs, rhs):
    return jnp.dot(lhs, rhs, precision=HIGHEST, preferred_element_type=f32)


def mm_t(lhs, rhs):
    return lax.dot_general(
        lhs, rhs, (((1,), (1,)), ((), ())), precision=HIGHEST, preferred_element_type=f32
    )


def tdot(lhs, rhs):
    return lax.dot_general(lhs, rhs, (((0,), (0,)), ((), ())), preferred_element_type=f32)


def bits(size):
    out, bit = [], 1
    while bit < size:
        out.append(bit)
        bit *= 2
    return out


def flip(value, axis, bit):
    size = lax.axis_size(axis)
    return lax.ppermute(value, axis, [(i, i ^ bit) for i in range(size)])


def shape(dims, dtype):
    return jax.ShapeDtypeStruct(dims, dtype)


def invert_factor(block, work, inverse_ref):
    size = block.shape[0]
    rows = lax.broadcasted_iota(jnp.int32, (size, size), 0)
    cols = lax.broadcasted_iota(jnp.int32, (size, size), 1)
    work[:, :size] = block
    work[:, size:] = jnp.where(rows == cols, 1.0, 0.0)
    sub = lax.broadcasted_iota(jnp.int32, (ROWS, size), 0)
    lane = lax.broadcasted_iota(jnp.int32, (ROWS, size), 1)
    log_sum = jnp.zeros((1, 1), f32)
    for first in range(0, size, ROWS):
        left = work[first : first + ROWS, :size]
        right = work[first : first + ROWS, size:]
        for start in range(0, ROWS, SUB):
            at = first + start
            columns = [
                jnp.broadcast_to(left[:, at + j : at + j + 1], (ROWS, size)) for j in range(SUB)
            ]
            for j in range(SUB):
                i = start + j
                if i == ROWS - 1:
                    break
                factor = jnp.where(sub > i, columns[j], 0.0) * (1.0 / columns[j][i : i + 1, :])
                for k in range(j + 1, SUB):
                    columns[k] = columns[k] - factor * columns[k][i : i + 1, :]
                left = left - factor * left[i : i + 1, :]
                right = right - factor * right[i : i + 1, :]
        pivot = jnp.sum(jnp.where(lane == sub + first, left, 0.0), axis=1, keepdims=True)
        scale = lax.rsqrt(pivot)
        left, right = left * scale, right * scale
        inverse_ref[first : first + ROWS, :] = right
        log_sum = log_sum + jnp.sum(jnp.log(pivot), axis=0, keepdims=True)
        if first + ROWS < size:
            update = lax.dot_general(
                left, jnp.concatenate([left, right], axis=1), (((0,), (0,)), ((), ())),
                precision=HIGHEST, preferred_element_type=f32,
            )
            work[first + ROWS :, :] = work[first + ROWS :, :] - update[first + ROWS :, :]
    return log_sum


def pick_pivots(owner_ref, at_ref, front_ref, table_ref, head_ref, rest_ref, mask_ref, lead_ref):
    b = head_ref.shape[1]
    per = front_ref.shape[1] // b
    for k in range(PL):
        total = jnp.zeros(((k + 1) * b, b), f32)
        for t in range(per):
            part = front_ref[: (k + 1) * b, t * b : (t + 1) * b]
            total = total + jnp.where(owner_ref[t] == k, part, 0.0)
        if k == 0:
            head_ref[:b, :] = total
        elif k == 1:
            head_ref[b:, :] = total
        else:
            rest_ref[...] = total
    lane = lax.broadcasted_iota(jnp.int32, (8, b), 1)
    table = jnp.zeros((8, b), f32)
    for t in range(per):
        table = table + jnp.where(lane == at_ref[0] + t, owner_ref[t].astype(f32), 0.0)
        keep = jnp.where(owner_ref[t] >= PL, 1.0, 0.0).astype(f32)
        mask_ref[:, t * b : (t + 1) * b] = jnp.full((8, b), keep, f32)
    table_ref[...] = table
    lead_ref[...] = front_ref[:, : lead_ref.shape[1]]


def leaf_two(head_ref, w0_ref, w1_ref, mask_ref, p_ref, inv0_ref, inv1_ref, x_ref, log_ref, work):
    b = w0_ref.shape[0]
    c00, c01, c11 = [head_ref[i * b : (i + 1) * b, :] for i in range(3)]
    keep = mask_ref[:1, :] > 0.0
    log0 = invert_factor(c00, work, inv0_ref)
    x01 = mm(inv0_ref[...], c01).astype(bf16)
    x_ref[...] = x01
    p0 = mm(inv0_ref[...], w0_ref[...]).astype(bf16)
    log1 = invert_factor(c11 - tdot(x01, x01), work, inv1_ref)
    p1 = mm(inv1_ref[...], w1_ref[...] - tdot(x01, p0)).astype(bf16)
    p_ref[:b, :] = jnp.where(keep, p0, jnp.zeros_like(p0))
    p_ref[b:, :] = jnp.where(keep, p1, jnp.zeros_like(p1))
    log_ref[...] = jnp.broadcast_to(log0 + log1, log_ref.shape)


def leaf_last(
    rest_ref, w2_ref, w_lead_ref, table_ref, mask_ref, p_ref, inv0_ref, inv1_ref, x_ref, log_ref,
    out_ref, inv, work,
):
    b, cols = w2_ref.shape
    wide = w_lead_ref.shape[1] if w_lead_ref.shape[1] > cols else PR * b
    c02, c12, c22 = [rest_ref[i * b : (i + 1) * b, :] for i in range(3)]
    inv0, inv1, x01 = inv0_ref[...], inv1_ref[...], x_ref[...]
    x02 = mm(inv0, c02).astype(bf16)
    x12 = mm(inv1, c12 - tdot(x01, x02)).astype(bf16)
    log2 = invert_factor(c22 - tdot(x02, x02) - tdot(x12, x12), work, inv)
    inv2 = inv[...]
    keep = mask_ref[:1, :] > 0.0
    panel = mm(inv2, w2_ref[...] - tdot(x02, p_ref[:b, :]) - tdot(x12, p_ref[b:, :])).astype(bf16)
    out_ref[:b, :] = jnp.where(keep, panel, jnp.zeros_like(panel))
    lane = lax.broadcasted_iota(jnp.int32, (1, wide), 1)
    block = jnp.zeros((1, wide), f32)
    for t in range(PR):
        inside = (lane >= t * b) & (lane < (t + 1) * b)
        block = jnp.where(inside, table_ref[:1, t : t + 1], block)
    keep = block > PL - 0.5
    lead0 = mm(inv0, w_lead_ref[:b, :]).astype(bf16)
    lead1 = mm(inv1, w_lead_ref[b : 2 * b, :] - tdot(x01, lead0)).astype(bf16)
    lead2 = w_lead_ref[2 * b :, :] - tdot(x02, lead0) - tdot(x12, lead1)
    lead2 = mm(inv2, lead2).astype(bf16)
    value = log_ref[:1, :1] + log2
    line = lax.broadcasted_iota(jnp.int32, (LOG_ROWS, wide), 0)
    rows = jnp.zeros((LOG_ROWS, wide), f32)
    for i in range(3):
        part = value.astype(bf16).astype(f32)
        rows = jnp.where(line == i, part, rows)
        value = value - part
    leads = [jnp.where(keep, lead, jnp.zeros_like(lead)) for lead in (lead0, lead1, lead2)]
    whole = jnp.concatenate(leads + [rows.astype(bf16)], axis=0)
    if cols >= wide:
        split = cols // wide
        tall = whole.shape[0] // split
        for i in range(split):
            out_ref[b:, i * wide : (i + 1) * wide] = whole[i * tall : (i + 1) * tall, :]
    else:
        tall = whole.shape[0]
        for i in range(wide // cols):
            out_ref[b + i * tall : b + (i + 1) * tall, :] = whole[:, i * cols : (i + 1) * cols]


def rows_kernel(ways, spans, *refs):
    keep_ref, scale_ref = refs[1:3]
    fronts = refs[3 : 3 + ways]
    mask_ref = refs[3 + ways]
    adds = refs[4 + ways : -1]
    out_ref = refs[-1]
    step = pl.program_id(0)
    b = fronts[0].shape[0]
    keep_cols = mask_ref[:1, :] > 0.0
    for i, front_ref in enumerate(fronts):
        at = slice(i * b, (i + 1) * b)
        keep = keep_cols & (keep_ref[step * ways + i] > 0)
        total = jnp.where(keep, front_ref[...], 0.0)
        for add_ref, (first, last) in zip(adds, spans):
            use = (step >= first) & (step < last) & (scale_ref[0] > 0)
            total = total + jnp.where(use, add_ref[at, :], 0.0)
        out_ref[at, :] = total


def take_rows(front, mask, source, kept, scale, ways, adds, name):
    b = B_ROWS
    cols = front.shape[1]
    steps = source.shape[0] // ways
    spans, add_specs = [], []
    for array, first, tile in adds:
        tiles = array.shape[0] // (ways * b) - tile
        last = min(steps, first + tiles)
        spans.append((first, last))

        def index(s, *pre, first=first, last=last, tile=tile):
            return (jnp.clip(s, first, last - 1) - first + tile, 0)

        add_specs.append(pl.BlockSpec((ways * b, cols), index))
    front_specs = [
        pl.BlockSpec((b, cols), lambda s, *pre, i=i: (pre[0][s * ways + i], 0)) for i in range(ways)
    ]

    def body(*refs):
        rows_kernel(ways, spans, *refs)

    return pl.pallas_call(
        body,
        grid_spec=pltpu.PrefetchScalarGridSpec(
            num_scalar_prefetch=3,
            grid=(steps,),
            in_specs=front_specs + [pl.BlockSpec((8, cols), lambda s, *pre: (0, 0))] + add_specs,
            out_specs=pl.BlockSpec((ways * b, cols), lambda s, *pre: (s, 0)),
        ),
        out_shape=shape((source.shape[0] * b, cols), f32),
        compiler_params=pltpu.CompilerParams(vmem_limit_bytes=60 << 20),
        name=name,
    )(source, kept, scale, *([front] * ways), mask, *[array for array, _, _ in adds])


def root_step(
    leaf_ref, corner_ref, first_ref, d01_ref, pack_ref,
    q_ref, inv0_ref, inv1_ref, x_ref, log_ref, work,
):
    b = inv0_ref.shape[0]
    cols = first_ref.shape[1]
    wide = corner_ref.shape[1]
    groups = d01_ref.shape[0] // (2 * b)
    pitch = pack_ref.shape[0] // groups
    corner = corner_ref[...]
    top = first_ref[...]
    lane = lax.broadcasted_iota(jnp.int32, (8, b), 1)
    logs = jnp.zeros((8, b), f32)
    for i in range(groups):
        at = i * pitch
        d2 = pack_ref[at : at + b, :]
        packed = pack_ref[at + b : at + pitch, :]
        if cols >= wide:
            parts = [packed[:, j * wide : (j + 1) * wide] for j in range(cols // wide)]
            whole = jnp.concatenate(parts, axis=0)
        else:
            tall = (pitch - b) // (wide // cols)
            parts = [packed[j * tall : (j + 1) * tall, :] for j in range(wide // cols)]
            whole = jnp.concatenate(parts, axis=1)
        lead = whole[: PL * b, :]
        corner = corner - tdot(lead, lead)
        top = top - tdot(lead[: 2 * b, :], d01_ref[i * 2 * b : (i + 1) * 2 * b, :])
        top = top - tdot(lead[2 * b :, :], d2)
        log_sum = jnp.sum(whole[PL * b : PL * b + 16, :b].astype(f32), axis=0, keepdims=True)
        logs = jnp.where(lane == leaf_ref[i], log_sum * (1.0 / (PL * b)), logs)
    log0 = invert_factor(corner[:b, :b], work, inv0_ref)
    x = mm(inv0_ref[...], corner[:b, b:]).astype(bf16)
    x_ref[...] = x
    log1 = invert_factor(corner[b:, b:] - tdot(x, x), work, inv1_ref)
    log_ref[...] = jnp.where(lane == groups, (log0 + log1) * (1.0 / wide), logs)
    q0 = mm(inv0_ref[...], top[:b, :]).astype(bf16)
    q_ref[:b, :] = q0
    q_ref[b:, :] = mm(inv1_ref[...], top[b:, :] - tdot(x, q0)).astype(bf16)


def update_kernel(slots, *refs):
    place_ref, base_ref, d01_ref = refs[:3]
    r01, out_ref = refs[3 : 3 + slots], refs[3 + slots]

    def at_slot(i):
        out_ref[...] = base_ref[...] - tdot(r01[i][...], d01_ref[...])

    for i in range(slots):
        pl.when(pl.program_id(0) == i)(lambda i=i: at_slot(i))


def finish_kernel(slots, whole_panel, *refs):
    place_ref, info_ref, part_ref = refs[:3]
    d2_ref, q_ref, inv0_ref, inv1_ref, x_ref, panel_ref = refs[3:9]
    r2, rq = refs[9 : 9 + slots], refs[9 + slots : 9 + 2 * slots]
    out_ref = refs[9 + 2 * slots]
    rows, cols = out_ref.shape
    wide = q_ref.shape[0]
    b = wide // PR

    def at_slot(i):
        total = part_ref[...] - tdot(r2[i][...], d2_ref[...])
        row = info_ref[i] + lax.broadcasted_iota(jnp.int32, (rows, cols), 0)
        width = min(wide, cols)
        if whole_panel:
            q0 = mm_t(total[:, :b], inv0_ref[...])
            x_part = jnp.dot(q0.astype(bf16), x_ref[...], preferred_element_type=f32)
            q1 = mm_t(total[:, b:wide] - x_part, inv1_ref[...])
            panel = jnp.concatenate([q0, q1], axis=1)
        else:
            panel = panel_ref[pl.ds(pl.multiple_of(i * rows, rows), rows), :]
        total = total - tdot(rq[i][...], q_ref[...])
        total = jnp.where(row >= wide, total, 0.0)
        col = info_ref[slots] + lax.broadcasted_iota(jnp.int32, (rows, width), 1)
        panel = jnp.where((row[:, :width] >= b) | (col < b), panel, 0.0)
        out_ref[:, :width] = jnp.where(col < wide, panel, total[:, :width])
        if width < cols:
            out_ref[:, width:] = total[:, width:]

    for i in range(slots):
        pl.when(pl.program_id(0) == i)(lambda i=i: at_slot(i))


def local(leaf_fronts, block_owner, root_front):
    members = lax.axis_size("mem")
    groups = lax.axis_size("grp")
    m = lax.axis_index("mem")
    g = lax.axis_index("grp")
    front = leaf_fronts[0]
    order, cols = front.shape
    owner = block_owner[0]
    per = owner.shape[0]
    b = cols // per
    count = order // b
    quarter = order // groups
    spread = members // groups
    quarter_blocks = quarter // b
    pr = PR * b
    lead_cols = min(pr, cols)
    leads = pr // lead_cols
    zone, inner = m // spread, m % spread
    smem = pl.BlockSpec(memory_space=pltpu.SMEM)
    vmem = pl.BlockSpec(memory_space=pltpu.VMEM)

    hops = bits(members)
    last = len(hops) - 1
    lead_order = [hops[-1], hops[0]] + hops[-2:0:-1]

    def lead_hop(value, at):
        bit, used = lead_order[at], sum(lead_order[:at])
        parts = []
        for root in range(leads):
            held = value[root]
            sources = [root ^ i for i in range(members) if i & ~used == 0]
            got = lax.ppermute(held, "mem", [(src, src ^ bit) for src in sources])
            parts.append(jnp.where((m ^ root) & ~used == bit, got, held))
        return parts

    table_rows, head, rest, mask, w_lead = pl.pallas_call(
        pick_pivots,
        grid=(1,),
        in_specs=[smem, smem, pl.BlockSpec((PL * b, cols), lambda i: (0, 0))],
        out_specs=[vmem] * 5,
        out_shape=(
            shape((8, b), f32), shape((3 * b, b), f32), shape((3 * b, b), f32),
            shape((8, cols), f32), shape((PL * b, lead_cols), f32),
        ),
        name="pick_pivots",
    )(owner, (m * per).reshape(1), front)
    w_lead = [w_lead] * leads

    def table_hop(value, at):
        return value + flip(value, "mem", hops[at])

    tie = lax.optimization_barrier
    for at in range(last + 1):
        table_rows = table_hop(table_rows, at)
    head = table_hop(head, 0)
    w_lead = lead_hop(w_lead, 0)
    table_rows, head, rest, w_lead = tie((table_rows, head, rest, w_lead))
    table = table_rows[0, :count].astype(jnp.int32)

    starts = [g ^ (CORE | CHIP), g ^ CHIP, g ^ CORE, g]
    places = jnp.concatenate(
        [s * quarter_blocks + jnp.arange(quarter_blocks) for s in starts] + [jnp.arange(PR)]
    )
    source = jnp.take(table, places)
    kept = (source >= PL).astype(jnp.int32)
    one = jnp.ones((1,), jnp.int32)
    ways = quarter_blocks // 2
    n = quarter_blocks

    def rows_at(first, size, adds, name, scale=one, ways=ways):
        return take_rows(
            front, mask, source[first : first + size], kept[first : first + size], scale, ways,
            adds, name,
        )

    diagonal = rows_at(0, n, [], "far_rows")
    first = rows_at(
        4 * n, PR, [(root_front, 0, 0)], "first_rows", (g == 0).astype(jnp.int32).reshape(1), PR
    )
    for at in range(1, last):
        head = table_hop(head, at)
        rest = table_hop(rest, at - 1)
    head, rest, diagonal, first, w_lead = tie((head, rest, diagonal, first, w_lead))
    near = rows_at(2 * n, n, [], "near_rows")
    first = first + flip(first, "grp", CORE)
    head = table_hop(head, last)
    rest = table_hop(rest, last - 1)
    w_lead = lead_hop(w_lead, 1)
    head, rest, w_lead, diagonal, first, near = tie((head, rest, w_lead, diagonal, first, near))
    near = flip(near, "grp", CORE)
    diagonal = flip(diagonal, "grp", CORE)
    first = first + flip(first, "grp", CHIP)
    rest = table_hop(rest, last)
    for at in range(2, last + 1):
        w_lead = lead_hop(w_lead, at)

    work = [pltpu.VMEM((b, 2 * b), f32)]
    sq = shape((b, b), f32)
    sqh = shape((b, b), bf16)
    logs = shape((8, b), f32)

    def w_spec(k):
        return pl.BlockSpec((b, cols), lambda i: (k, 0))

    p01, inv0, inv1, x01, log01 = pl.pallas_call(
        leaf_two,
        grid=(1,),
        in_specs=[vmem, w_spec(0), w_spec(1), vmem],
        out_specs=[vmem] * 5,
        out_shape=(shape((2 * b, cols), bf16), sq, sq, sqh, logs),
        scratch_shapes=work,
        name="leaf_two",
    )(head, front, front, mask)

    p01, rest, w_lead, first, diagonal = tie((p01, rest, w_lead, first, diagonal))
    far_near = flip(rows_at(n, ways, [(diagonal, 0, 0)], "far_sum"), "grp", CHIP)

    def across(value):
        far_value = flip(value, "grp", CHIP)
        both = jnp.concatenate([value, far_value], axis=0)
        return jnp.concatenate([both, flip(both, "grp", CORE)], axis=0)

    d01 = across(p01)
    corner = lead_hop([first[:, :lead_cols]] * leads, 0)
    rest, d01, corner = tie((rest, d01, corner))
    corner = lead_hop(corner, 1)
    w_lead = w_lead[0] if leads == 1 else jnp.concatenate(w_lead, axis=1)
    lead_rows = (PL * b + LOG_ROWS) * pr // cols
    pack = pl.pallas_call(
        leaf_last,
        grid=(1,),
        in_specs=[vmem, w_spec(2)] + [vmem] * 8,
        out_specs=vmem,
        out_shape=shape((b + lead_rows, cols), bf16),
        scratch_shapes=[pltpu.VMEM((b, b), f32)] + work,
        name="leaf_last",
    )(rest, front, w_lead, table_rows, mask, p01, inv0, inv1, x01, log01)

    def among(offsets):
        found = jnp.zeros((), jnp.bool_)
        for h in offsets:
            found = found | (zone == (g ^ h))
        return found

    def zone_hop(state):
        have, held, _ = state
        bit = groups // 2 // len(have)
        pairs = []
        for gi in range(groups):
            for h in have:
                for j in range(spread):
                    src = (gi ^ h) * spread + j
                    dst = (gi ^ h ^ bit) * spread + j
                    pairs.append((gi * members + src, gi * members + dst))
        got = lax.ppermute(held, ("grp", "mem"), pairs)
        new = [h ^ bit for h in have]
        return have + new, jnp.where(among(new), got, held), (new, got)

    def inner_hop(stage, i):
        offsets, value = stage
        pairs = []
        for gi in range(groups):
            for h in offsets:
                for j in range(spread):
                    at = gi * members + (gi ^ h) * spread
                    pairs.append((at + j, at + (j ^ i)))
        return lax.ppermute(value, ("grp", "mem"), pairs)

    def inner_hops(state, early=None):
        have, held, last_stage = state
        slots = [held]
        for i in range(1, spread):
            if early is None:
                slots.append(inner_hop((have, held), i))
            else:
                got = inner_hop(last_stage, i)
                slots.append(jnp.where(among(last_stage[0]), got, early[i - 1]))
        return slots

    def early_hops(state):
        return [inner_hop((state[0], state[1]), i) for i in range(1, spread)]

    s01 = zone_hop(([0], d01, None))
    pack_far = flip(pack, "grp", CHIP)
    pack, pack_far, diagonal, corner, far_near = tie(
        (pack, pack_far, diagonal, corner, far_near)
    )
    far_in = rows_at(n + ways, ways, [(diagonal, 0, 1)], "far_sum")
    for at in range(2, last + 1):
        corner = lead_hop(corner, at)
    pack = jnp.concatenate([pack, pack_far], axis=0)
    pack = jnp.concatenate([pack, flip(pack, "grp", CORE)], axis=0)
    pack, held, far_in, corner = tie((pack, s01[1], far_in, corner))
    corner = corner[0] if leads == 1 else jnp.concatenate(corner, axis=1)
    s01 = (s01[0], held, None)
    far_last = flip(far_in, "grp", CHIP)
    early01 = early_hops(s01)
    s01 = zone_hop(s01)
    d2 = pack.reshape(groups, b + lead_rows, cols)[:, :b].reshape(groups * b, cols)
    s2 = zone_hop(([0], d2, None))
    leaves = jnp.stack([g, g ^ CHIP, g ^ CORE, g ^ (CORE | CHIP)])
    q, rinv0, rinv1, rx, logs_out = pl.pallas_call(
        root_step,
        in_specs=[smem] + [vmem] * 4,
        out_shape=(shape((pr, cols), bf16), sq, sq, sqh, logs),
        scratch_shapes=work,
        compiler_params=pltpu.CompilerParams(vmem_limit_bytes=32 << 20),
        name="root_step",
    )(leaves, corner, first, d01, pack)
    sq_hop = zone_hop(([0], q, None))
    q_held, held, s01_held, s01_got = tie((sq_hop[1], s2[1], s01[1], s01[2][1]))
    s01 = (s01[0], s01_held, (s01[2][0], s01_got))
    s2 = (s2[0], held, None)
    sq_hop = zone_hop((sq_hop[0], q_held, None))
    early2 = early_hops(s2)
    s2 = zone_hop(s2)
    q_held, far_last, *early01 = tie((sq_hop[1], far_last, *early01))
    rq = inner_hops((sq_hop[0], q_held, None))
    r01 = inner_hops(s01, early01)
    r2 = inner_hops(s2, early2)

    adds = [(root_front, 0, 0), (near, 0, 0), (far_near, 0, 0), (far_last, 1, 0)]
    base = rows_at(3 * n, n, adds, "base_rows")
    slot_of = inner ^ jnp.arange(spread, dtype=jnp.int32)

    def update_body(*refs):
        update_kernel(spread, *refs)

    def whole_spec(array):
        return pl.BlockSpec(array.shape, lambda s, *pre: (0, 0))

    part = pl.pallas_call(
        update_body,
        grid_spec=pltpu.PrefetchScalarGridSpec(
            num_scalar_prefetch=1,
            grid=(spread,),
            in_specs=[pl.BlockSpec((cols, cols), lambda s, place: (place[s], 0))]
            + [whole_spec(array) for array in [d01] + r01],
            out_specs=pl.BlockSpec((cols, cols), lambda s, place: (s, 0)),
        ),
        out_shape=shape((quarter, cols), f32),
        compiler_params=pltpu.CompilerParams(vmem_limit_bytes=40 << 20),
        name="update",
    )(slot_of, base, d01, *r01)
    if leads > 1:
        first_col = jnp.minimum(m, leads - 1) * lead_cols
        panel = jnp.concatenate([rows.astype(f32).T for rows in rq], axis=0)
        panel = lax.dynamic_slice_in_dim(panel, first_col, lead_cols, 1)
    else:
        panel = jnp.zeros((8, lead_cols), f32)
    info = jnp.concatenate([g * quarter + slot_of * cols, (m * cols).reshape(1)])

    def finish_body(*refs):
        finish_kernel(spread, leads == 1, *refs)

    fixed = [d2, q, rinv0, rinv1, rx, panel] + r2 + rq
    root_factor = pl.pallas_call(
        finish_body,
        grid_spec=pltpu.PrefetchScalarGridSpec(
            num_scalar_prefetch=2,
            grid=(spread,),
            in_specs=[pl.BlockSpec((cols, cols), lambda s, place, info: (s, 0))]
            + [whole_spec(array) for array in fixed],
            out_specs=pl.BlockSpec((cols, cols), lambda s, place, info: (place[s], 0)),
        ),
        out_shape=shape((quarter, cols), f32),
        compiler_params=pltpu.CompilerParams(vmem_limit_bytes=40 << 20),
        name="finish",
    )(slot_of, info, part, *fixed)
    return root_factor, logs_out[0, : groups + 1]


def solution(mesh):
    in_specs = (P("grp", None, "mem"), P("grp", "mem"), P("grp", "mem"))
    out_specs = (P("grp", "mem"), P())
    return jax.shard_map(local, mesh=mesh, in_specs=in_specs, out_specs=out_specs, check_vma=False)
```

```python
import jax
import jax.numpy as jnp
from jax import lax
from jax.experimental import pallas as pl
from jax.experimental.pallas import tpu as pltpu
from jax.sharding import PartitionSpec as P

PL = 3
PR = 2
HIGHEST = lax.Precision.HIGHEST
ROWS = 64
SUB = 16
LOG_ROWS = 32
B_ROWS = 128
CORE, CHIP = 1, 2
f32, bf16 = jnp.float32, jnp.bfloat16


def mm(lhs, rhs):
    return jnp.dot(lhs, rhs, precision=HIGHEST, preferred_element_type=f32)


def mm_t(lhs, rhs):
    return lax.dot_general(
        lhs, rhs, (((1,), (1,)), ((), ())), precision=HIGHEST, preferred_element_type=f32
    )


def tdot(lhs, rhs):
    return lax.dot_general(lhs, rhs, (((0,), (0,)), ((), ())), preferred_element_type=f32)


def bits(size):
    out, bit = [], 1
    while bit < size:
        out.append(bit)
        bit *= 2
    return out


def flip(value, axis, bit):
    size = lax.axis_size(axis)
    return lax.ppermute(value, axis, [(i, i ^ bit) for i in range(size)])


def shape(dims, dtype):
    return jax.ShapeDtypeStruct(dims, dtype)


def invert_factor(block, work, inverse_ref):
    size = block.shape[0]
    rows = lax.broadcasted_iota(jnp.int32, (size, size), 0)
    cols = lax.broadcasted_iota(jnp.int32, (size, size), 1)
    work[:, :size] = block
    work[:, size:] = jnp.where(rows == cols, 1.0, 0.0)
    sub = lax.broadcasted_iota(jnp.int32, (ROWS, size), 0)
    lane = lax.broadcasted_iota(jnp.int32, (ROWS, size), 1)
    log_sum = jnp.zeros((1, 1), f32)
    for first in range(0, size, ROWS):
        left = work[first : first + ROWS, :size]
        right = work[first : first + ROWS, size:]
        for start in range(0, ROWS, SUB):
            at = first + start
            columns = [
                jnp.broadcast_to(left[:, at + j : at + j + 1], (ROWS, size)) for j in range(SUB)
            ]
            for j in range(SUB):
                i = start + j
                if i == ROWS - 1:
                    break
                factor = jnp.where(sub > i, columns[j], 0.0) * (1.0 / columns[j][i : i + 1, :])
                for k in range(j + 1, SUB):
                    columns[k] = columns[k] - factor * columns[k][i : i + 1, :]
                left = left - factor * left[i : i + 1, :]
                right = right - factor * right[i : i + 1, :]
        pivot = jnp.sum(jnp.where(lane == sub + first, left, 0.0), axis=1, keepdims=True)
        scale = lax.rsqrt(pivot)
        left, right = left * scale, right * scale
        inverse_ref[first : first + ROWS, :] = right
        log_sum = log_sum + jnp.sum(jnp.log(pivot), axis=0, keepdims=True)
        if first + ROWS < size:
            update = lax.dot_general(
                left, jnp.concatenate([left, right], axis=1), (((0,), (0,)), ((), ())),
                precision=HIGHEST, preferred_element_type=f32,
            )
            work[first + ROWS :, :] = work[first + ROWS :, :] - update[first + ROWS :, :]
    return log_sum


def pick_pivots(owner_ref, at_ref, front_ref, table_ref, head_ref, rest_ref, mask_ref, lead_ref):
    b = head_ref.shape[1]
    per = front_ref.shape[1] // b
    for k in range(PL):
        total = jnp.zeros(((k + 1) * b, b), f32)
        for t in range(per):
            part = front_ref[: (k + 1) * b, t * b : (t + 1) * b]
            total = total + jnp.where(owner_ref[t] == k, part, 0.0)
        if k == 0:
            head_ref[:b, :] = total
        elif k == 1:
            head_ref[b:, :] = total
        else:
            rest_ref[...] = total
    lane = lax.broadcasted_iota(jnp.int32, (8, b), 1)
    table = jnp.zeros((8, b), f32)
    for t in range(per):
        table = table + jnp.where(lane == at_ref[0] + t, owner_ref[t].astype(f32), 0.0)
        keep = jnp.where(owner_ref[t] >= PL, 1.0, 0.0).astype(f32)
        mask_ref[:, t * b : (t + 1) * b] = jnp.full((8, b), keep, f32)
    table_ref[...] = table
    lead_ref[...] = front_ref[:, : lead_ref.shape[1]]


def leaf_two(head_ref, w0_ref, w1_ref, mask_ref, p_ref, inv0_ref, inv1_ref, x_ref, log_ref, work):
    b = w0_ref.shape[0]
    c00, c01, c11 = [head_ref[i * b : (i + 1) * b, :] for i in range(3)]
    keep = mask_ref[:1, :] > 0.0
    log0 = invert_factor(c00, work, inv0_ref)
    x01 = mm(inv0_ref[...], c01).astype(bf16)
    x_ref[...] = x01
    p0 = mm(inv0_ref[...], w0_ref[...]).astype(bf16)
    log1 = invert_factor(c11 - tdot(x01, x01), work, inv1_ref)
    p1 = mm(inv1_ref[...], w1_ref[...] - tdot(x01, p0)).astype(bf16)
    p_ref[:b, :] = jnp.where(keep, p0, jnp.zeros_like(p0))
    p_ref[b:, :] = jnp.where(keep, p1, jnp.zeros_like(p1))
    log_ref[...] = jnp.broadcast_to(log0 + log1, log_ref.shape)


def leaf_last(
    rest_ref, w2_ref, w_lead_ref, table_ref, mask_ref, p_ref, inv0_ref, inv1_ref, x_ref, log_ref,
    out_ref, inv, work,
):
    b, cols = w2_ref.shape
    wide = w_lead_ref.shape[1] if w_lead_ref.shape[1] > cols else PR * b
    c02, c12, c22 = [rest_ref[i * b : (i + 1) * b, :] for i in range(3)]
    inv0, inv1, x01 = inv0_ref[...], inv1_ref[...], x_ref[...]
    x02 = mm(inv0, c02).astype(bf16)
    x12 = mm(inv1, c12 - tdot(x01, x02)).astype(bf16)
    log2 = invert_factor(c22 - tdot(x02, x02) - tdot(x12, x12), work, inv)
    inv2 = inv[...]
    keep = mask_ref[:1, :] > 0.0
    panel = mm(inv2, w2_ref[...] - tdot(x02, p_ref[:b, :]) - tdot(x12, p_ref[b:, :])).astype(bf16)
    out_ref[:b, :] = jnp.where(keep, panel, jnp.zeros_like(panel))
    lane = lax.broadcasted_iota(jnp.int32, (1, wide), 1)
    block = jnp.zeros((1, wide), f32)
    for t in range(PR):
        inside = (lane >= t * b) & (lane < (t + 1) * b)
        block = jnp.where(inside, table_ref[:1, t : t + 1], block)
    keep = block > PL - 0.5
    lead0 = mm(inv0, w_lead_ref[:b, :]).astype(bf16)
    lead1 = mm(inv1, w_lead_ref[b : 2 * b, :] - tdot(x01, lead0)).astype(bf16)
    lead2 = w_lead_ref[2 * b :, :] - tdot(x02, lead0) - tdot(x12, lead1)
    lead2 = mm(inv2, lead2).astype(bf16)
    value = log_ref[:1, :1] + log2
    line = lax.broadcasted_iota(jnp.int32, (LOG_ROWS, wide), 0)
    rows = jnp.zeros((LOG_ROWS, wide), f32)
    for i in range(3):
        part = value.astype(bf16).astype(f32)
        rows = jnp.where(line == i, part, rows)
        value = value - part
    leads = [jnp.where(keep, lead, jnp.zeros_like(lead)) for lead in (lead0, lead1, lead2)]
    whole = jnp.concatenate(leads + [rows.astype(bf16)], axis=0)
    if cols >= wide:
        split = cols // wide
        tall = whole.shape[0] // split
        for i in range(split):
            out_ref[b:, i * wide : (i + 1) * wide] = whole[i * tall : (i + 1) * tall, :]
    else:
        tall = whole.shape[0]
        for i in range(wide // cols):
            out_ref[b + i * tall : b + (i + 1) * tall, :] = whole[:, i * cols : (i + 1) * cols]


def rows_kernel(ways, spans, *refs):
    keep_ref, scale_ref = refs[1:3]
    fronts = refs[3 : 3 + ways]
    mask_ref = refs[3 + ways]
    adds = refs[4 + ways : -1]
    out_ref = refs[-1]
    step = pl.program_id(0)
    b = fronts[0].shape[0]
    keep_cols = mask_ref[:1, :] > 0.0
    for i, front_ref in enumerate(fronts):
        at = slice(i * b, (i + 1) * b)
        keep = keep_cols & (keep_ref[step * ways + i] > 0)
        total = jnp.where(keep, front_ref[...], 0.0)
        for add_ref, (first, last) in zip(adds, spans):
            use = (step >= first) & (step < last) & (scale_ref[0] > 0)
            total = total + jnp.where(use, add_ref[at, :], 0.0)
        out_ref[at, :] = total


def take_rows(front, mask, source, kept, scale, ways, adds, name):
    b = B_ROWS
    cols = front.shape[1]
    steps = source.shape[0] // ways
    spans, add_specs = [], []
    for array, first, tile in adds:
        tiles = array.shape[0] // (ways * b) - tile
        last = min(steps, first + tiles)
        spans.append((first, last))

        def index(s, *pre, first=first, last=last, tile=tile):
            return (jnp.clip(s, first, last - 1) - first + tile, 0)

        add_specs.append(pl.BlockSpec((ways * b, cols), index))
    front_specs = [
        pl.BlockSpec((b, cols), lambda s, *pre, i=i: (pre[0][s * ways + i], 0)) for i in range(ways)
    ]

    def body(*refs):
        rows_kernel(ways, spans, *refs)

    return pl.pallas_call(
        body,
        grid_spec=pltpu.PrefetchScalarGridSpec(
            num_scalar_prefetch=3,
            grid=(steps,),
            in_specs=front_specs + [pl.BlockSpec((8, cols), lambda s, *pre: (0, 0))] + add_specs,
            out_specs=pl.BlockSpec((ways * b, cols), lambda s, *pre: (s, 0)),
        ),
        out_shape=shape((source.shape[0] * b, cols), f32),
        compiler_params=pltpu.CompilerParams(vmem_limit_bytes=60 << 20),
        name=name,
    )(source, kept, scale, *([front] * ways), mask, *[array for array, _, _ in adds])


def root_step(
    leaf_ref, corner_ref, first_ref, d01_ref, pack_ref,
    q_ref, inv0_ref, inv1_ref, x_ref, log_ref, work,
):
    b = inv0_ref.shape[0]
    cols = first_ref.shape[1]
    wide = corner_ref.shape[1]
    groups = d01_ref.shape[0] // (2 * b)
    pitch = pack_ref.shape[0] // groups
    corner = corner_ref[...]
    top = first_ref[...]
    lane = lax.broadcasted_iota(jnp.int32, (8, b), 1)
    logs = jnp.zeros((8, b), f32)
    for i in range(groups):
        at = i * pitch
        d2 = pack_ref[at : at + b, :]
        packed = pack_ref[at + b : at + pitch, :]
        if cols >= wide:
            parts = [packed[:, j * wide : (j + 1) * wide] for j in range(cols // wide)]
            whole = jnp.concatenate(parts, axis=0)
        else:
            tall = (pitch - b) // (wide // cols)
            parts = [packed[j * tall : (j + 1) * tall, :] for j in range(wide // cols)]
            whole = jnp.concatenate(parts, axis=1)
        lead = whole[: PL * b, :]
        corner = corner - tdot(lead, lead)
        top = top - tdot(lead[: 2 * b, :], d01_ref[i * 2 * b : (i + 1) * 2 * b, :])
        top = top - tdot(lead[2 * b :, :], d2)
        log_sum = jnp.sum(whole[PL * b : PL * b + 16, :b].astype(f32), axis=0, keepdims=True)
        logs = jnp.where(lane == leaf_ref[i], log_sum * (1.0 / (PL * b)), logs)
    log0 = invert_factor(corner[:b, :b], work, inv0_ref)
    x = mm(inv0_ref[...], corner[:b, b:]).astype(bf16)
    x_ref[...] = x
    log1 = invert_factor(corner[b:, b:] - tdot(x, x), work, inv1_ref)
    log_ref[...] = jnp.where(lane == groups, (log0 + log1) * (1.0 / wide), logs)
    q0 = mm(inv0_ref[...], top[:b, :]).astype(bf16)
    q_ref[:b, :] = q0
    q_ref[b:, :] = mm(inv1_ref[...], top[b:, :] - tdot(x, q0)).astype(bf16)


def update_kernel(slots, *refs):
    place_ref, base_ref, d01_ref = refs[:3]
    r01, out_ref = refs[3 : 3 + slots], refs[3 + slots]

    def at_slot(i):
        out_ref[...] = base_ref[...] - tdot(r01[i][...], d01_ref[...])

    for i in range(slots):
        pl.when(pl.program_id(0) == i)(lambda i=i: at_slot(i))


def finish_kernel(slots, whole_panel, *refs):
    place_ref, info_ref, part_ref = refs[:3]
    d2_ref, q_ref, inv0_ref, inv1_ref, x_ref, panel_ref = refs[3:9]
    r2, rq = refs[9 : 9 + slots], refs[9 + slots : 9 + 2 * slots]
    out_ref = refs[9 + 2 * slots]
    rows, cols = out_ref.shape
    wide = q_ref.shape[0]
    b = wide // PR

    def at_slot(i):
        total = part_ref[...] - tdot(r2[i][...], d2_ref[...])
        row = info_ref[i] + lax.broadcasted_iota(jnp.int32, (rows, cols), 0)
        width = min(wide, cols)
        if whole_panel:
            q0 = mm_t(total[:, :b], inv0_ref[...])
            x_part = jnp.dot(q0.astype(bf16), x_ref[...], preferred_element_type=f32)
            q1 = mm_t(total[:, b:wide] - x_part, inv1_ref[...])
            panel = jnp.concatenate([q0, q1], axis=1)
        else:
            panel = panel_ref[pl.ds(pl.multiple_of(i * rows, rows), rows), :]
        total = total - tdot(rq[i][...], q_ref[...])
        total = jnp.where(row >= wide, total, 0.0)
        col = info_ref[slots] + lax.broadcasted_iota(jnp.int32, (rows, width), 1)
        panel = jnp.where((row[:, :width] >= b) | (col < b), panel, 0.0)
        out_ref[:, :width] = jnp.where(col < wide, panel, total[:, :width])
        if width < cols:
            out_ref[:, width:] = total[:, width:]

    for i in range(slots):
        pl.when(pl.program_id(0) == i)(lambda i=i: at_slot(i))


def local(leaf_fronts, block_owner, root_front):
    members = lax.axis_size("mem")
    groups = lax.axis_size("grp")
    m = lax.axis_index("mem")
    g = lax.axis_index("grp")
    front = leaf_fronts[0]
    order, cols = front.shape
    owner = block_owner[0]
    per = owner.shape[0]
    b = cols // per
    count = order // b
    quarter = order // groups
    spread = members // groups
    quarter_blocks = quarter // b
    pr = PR * b
    lead_cols = min(pr, cols)
    leads = pr // lead_cols
    zone, inner = m // spread, m % spread
    smem = pl.BlockSpec(memory_space=pltpu.SMEM)
    vmem = pl.BlockSpec(memory_space=pltpu.VMEM)

    hops = bits(members)
    last = len(hops) - 1
    lead_order = [hops[-1], hops[0]] + hops[-2:0:-1]

    def lead_hop(value, at):
        bit, used = lead_order[at], sum(lead_order[:at])
        parts = []
        for root in range(leads):
            held = value[root]
            sources = [root ^ i for i in range(members) if i & ~used == 0]
            got = lax.ppermute(held, "mem", [(src, src ^ bit) for src in sources])
            parts.append(jnp.where((m ^ root) & ~used == bit, got, held))
        return parts

    table_rows, head, rest, mask, w_lead = pl.pallas_call(
        pick_pivots,
        grid=(1,),
        in_specs=[smem, smem, pl.BlockSpec((PL * b, cols), lambda i: (0, 0))],
        out_specs=[vmem] * 5,
        out_shape=(
            shape((8, b), f32), shape((3 * b, b), f32), shape((3 * b, b), f32),
            shape((8, cols), f32), shape((PL * b, lead_cols), f32),
        ),
        name="pick_pivots",
    )(owner, (m * per).reshape(1), front)
    w_lead = [w_lead] * leads

    def table_hop(value, at):
        return value + flip(value, "mem", hops[at])

    tie = lax.optimization_barrier
    for at in range(last + 1):
        table_rows = table_hop(table_rows, at)
    head = table_hop(head, 0)
    w_lead = lead_hop(w_lead, 0)
    table_rows, head, rest, w_lead = tie((table_rows, head, rest, w_lead))
    table = table_rows[0, :count].astype(jnp.int32)

    starts = [g ^ (CORE | CHIP), g ^ CHIP, g ^ CORE, g]
    places = jnp.concatenate(
        [s * quarter_blocks + jnp.arange(quarter_blocks) for s in starts] + [jnp.arange(PR)]
    )
    source = jnp.take(table, places)
    kept = (source >= PL).astype(jnp.int32)
    one = jnp.ones((1,), jnp.int32)
    ways = quarter_blocks // 2
    n = quarter_blocks

    def rows_at(first, size, adds, name, scale=one, ways=ways):
        return take_rows(
            front, mask, source[first : first + size], kept[first : first + size], scale, ways,
            adds, name,
        )

    diagonal = rows_at(0, n, [], "far_rows")
    first = rows_at(
        4 * n, PR, [(root_front, 0, 0)], "first_rows", (g == 0).astype(jnp.int32).reshape(1), PR
    )
    for at in range(1, last):
        head = table_hop(head, at)
        rest = table_hop(rest, at - 1)
    head, rest, diagonal, first, w_lead = tie((head, rest, diagonal, first, w_lead))
    near = rows_at(2 * n, n, [], "near_rows")
    first = first + flip(first, "grp", CORE)
    head = table_hop(head, last)
    rest = table_hop(rest, last - 1)
    w_lead = lead_hop(w_lead, 1)
    head, rest, w_lead, diagonal, first, near = tie((head, rest, w_lead, diagonal, first, near))
    near = flip(near, "grp", CORE)
    diagonal = flip(diagonal, "grp", CORE)
    first = first + flip(first, "grp", CHIP)
    rest = table_hop(rest, last)
    for at in range(2, last + 1):
        w_lead = lead_hop(w_lead, at)

    work = [pltpu.VMEM((b, 2 * b), f32)]
    sq = shape((b, b), f32)
    sqh = shape((b, b), bf16)
    logs = shape((8, b), f32)

    def w_spec(k):
        return pl.BlockSpec((b, cols), lambda i: (k, 0))

    p01, inv0, inv1, x01, log01 = pl.pallas_call(
        leaf_two,
        grid=(1,),
        in_specs=[vmem, w_spec(0), w_spec(1), vmem],
        out_specs=[vmem] * 5,
        out_shape=(shape((2 * b, cols), bf16), sq, sq, sqh, logs),
        scratch_shapes=work,
        name="leaf_two",
    )(head, front, front, mask)

    p01, rest, w_lead, first = tie((p01, rest, w_lead, first))

    def across(value):
        far_value = flip(value, "grp", CHIP)
        both = jnp.concatenate([value, far_value], axis=0)
        return jnp.concatenate([both, flip(both, "grp", CORE)], axis=0)

    d01 = across(p01)
    corner = lead_hop([first[:, :lead_cols]] * leads, 0)
    rest, d01, corner = tie((rest, d01, corner))
    corner = lead_hop(corner, 1)
    w_lead = w_lead[0] if leads == 1 else jnp.concatenate(w_lead, axis=1)
    lead_rows = (PL * b + LOG_ROWS) * pr // cols
    pack = pl.pallas_call(
        leaf_last,
        grid=(1,),
        in_specs=[vmem, w_spec(2)] + [vmem] * 8,
        out_specs=vmem,
        out_shape=shape((b + lead_rows, cols), bf16),
        scratch_shapes=[pltpu.VMEM((b, b), f32)] + work,
        name="leaf_last",
    )(rest, front, w_lead, table_rows, mask, p01, inv0, inv1, x01, log01)

    def among(offsets):
        found = jnp.zeros((), jnp.bool_)
        for h in offsets:
            found = found | (zone == (g ^ h))
        return found

    def zone_hop(state):
        have, held, _ = state
        bit = groups // 2 // len(have)
        pairs = []
        for gi in range(groups):
            for h in have:
                for j in range(spread):
                    src = (gi ^ h) * spread + j
                    dst = (gi ^ h ^ bit) * spread + j
                    pairs.append((gi * members + src, gi * members + dst))
        got = lax.ppermute(held, ("grp", "mem"), pairs)
        new = [h ^ bit for h in have]
        return have + new, jnp.where(among(new), got, held), (new, got)

    def inner_hop(stage, i):
        offsets, value = stage
        pairs = []
        for gi in range(groups):
            for h in offsets:
                for j in range(spread):
                    at = gi * members + (gi ^ h) * spread
                    pairs.append((at + j, at + (j ^ i)))
        return lax.ppermute(value, ("grp", "mem"), pairs)

    def inner_hops(state, early=None):
        have, held, last_stage = state
        slots = [held]
        for i in range(1, spread):
            if early is None:
                slots.append(inner_hop((have, held), i))
            else:
                got = inner_hop(last_stage, i)
                slots.append(jnp.where(among(last_stage[0]), got, early[i - 1]))
        return slots

    def early_hops(state):
        return [inner_hop((state[0], state[1]), i) for i in range(1, spread)]

    s01 = zone_hop(([0], d01, None))
    pack_far = flip(pack, "grp", CHIP)
    pack, pack_far, diagonal, corner = tie((pack, pack_far, diagonal, corner))
    part = n // 4
    far_in = [
        rows_at(n, part, [(diagonal, 0, 0)], "far_sum", ways=part),
        rows_at(n + part, n - part, [(diagonal, 0, 1)], "far_sum", ways=part),
    ]
    for at in range(2, last + 1):
        corner = lead_hop(corner, at)
    pack = jnp.concatenate([pack, pack_far], axis=0)
    pack = jnp.concatenate([pack, flip(pack, "grp", CORE)], axis=0)
    pack, held, far_in, corner = tie((pack, s01[1], far_in, corner))
    corner = corner[0] if leads == 1 else jnp.concatenate(corner, axis=1)
    s01 = (s01[0], held, None)
    far = [flip(value, "grp", CHIP) for value in far_in]
    early01 = early_hops(s01)
    s01 = zone_hop(s01)
    d2 = pack.reshape(groups, b + lead_rows, cols)[:, :b].reshape(groups * b, cols)
    s2 = zone_hop(([0], d2, None))
    leaves = jnp.stack([g, g ^ CHIP, g ^ CORE, g ^ (CORE | CHIP)])
    q, rinv0, rinv1, rx, logs_out = pl.pallas_call(
        root_step,
        in_specs=[smem] + [vmem] * 4,
        out_shape=(shape((pr, cols), bf16), sq, sq, sqh, logs),
        scratch_shapes=work,
        compiler_params=pltpu.CompilerParams(vmem_limit_bytes=32 << 20),
        name="root_step",
    )(leaves, corner, first, d01, pack)
    q, far[0] = tie((q, far[0]))
    sq_hop = zone_hop(([0], q, None))
    q_held, held, s01_held, s01_got = tie((sq_hop[1], s2[1], s01[1], s01[2][1]))
    s01 = (s01[0], s01_held, (s01[2][0], s01_got))
    s2 = (s2[0], held, None)
    sq_hop = zone_hop((sq_hop[0], q_held, None))
    early2 = early_hops(s2)
    s2 = zone_hop(s2)
    q_held, s2_held, s2_got, *early01 = tie((sq_hop[1], s2[1], s2[2][1], *early01))
    s2 = (s2[0], s2_held, (s2[2][0], s2_got))
    rq = inner_hops((sq_hop[0], q_held, None))
    r01 = inner_hops(s01, early01)
    r2 = inner_hops(s2, early2)

    adds = [(root_front, 0, 0), (near, 0, 0), (far[0], 0, 0), (far[1], 1, 0)]
    base = rows_at(3 * n, n, adds, "base_rows", ways=part)
    slot_of = inner ^ jnp.arange(spread, dtype=jnp.int32)

    def update_body(*refs):
        update_kernel(spread, *refs)

    def whole_spec(array):
        return pl.BlockSpec(array.shape, lambda s, *pre: (0, 0))

    part = pl.pallas_call(
        update_body,
        grid_spec=pltpu.PrefetchScalarGridSpec(
            num_scalar_prefetch=1,
            grid=(spread,),
            in_specs=[pl.BlockSpec((cols, cols), lambda s, place: (place[s], 0))]
            + [whole_spec(array) for array in [d01] + r01],
            out_specs=pl.BlockSpec((cols, cols), lambda s, place: (s, 0)),
        ),
        out_shape=shape((quarter, cols), f32),
        compiler_params=pltpu.CompilerParams(vmem_limit_bytes=40 << 20),
        name="update",
    )(slot_of, base, d01, *r01)
    if leads > 1:
        first_col = jnp.minimum(m, leads - 1) * lead_cols
        panel = jnp.concatenate([rows.astype(f32).T for rows in rq], axis=0)
        panel = lax.dynamic_slice_in_dim(panel, first_col, lead_cols, 1)
    else:
        panel = jnp.zeros((8, lead_cols), f32)
    info = jnp.concatenate([g * quarter + slot_of * cols, (m * cols).reshape(1)])

    def finish_body(*refs):
        finish_kernel(spread, leads == 1, *refs)

    fixed = [d2, q, rinv0, rinv1, rx, panel] + r2 + rq
    root_factor = pl.pallas_call(
        finish_body,
        grid_spec=pltpu.PrefetchScalarGridSpec(
            num_scalar_prefetch=2,
            grid=(spread,),
            in_specs=[pl.BlockSpec((cols, cols), lambda s, place, info: (s, 0))]
            + [whole_spec(array) for array in fixed],
            out_specs=pl.BlockSpec((cols, cols), lambda s, place, info: (place[s], 0)),
        ),
        out_shape=shape((quarter, cols), f32),
        compiler_params=pltpu.CompilerParams(vmem_limit_bytes=40 << 20),
        name="finish",
    )(slot_of, info, part, *fixed)
    return root_factor, logs_out[0, : groups + 1]


def solution(mesh):
    in_specs = (P("grp", None, "mem"), P("grp", "mem"), P("grp", "mem"))
    out_specs = (P("grp", "mem"), P())
    return jax.shard_map(local, mesh=mesh, in_specs=in_specs, out_specs=out_specs, check_vma=False)
```

```python
import jax
import jax.numpy as jnp
from jax import lax
from jax.experimental import pallas as pl
from jax.experimental.pallas import tpu as pltpu
from jax.sharding import PartitionSpec as P

PL = 3
PR = 2
HIGHEST = lax.Precision.HIGHEST
ROWS = 64
SUB = 16
LOG_ROWS = 32
B_ROWS = 128
CORE, CHIP = 1, 2
f32, bf16 = jnp.float32, jnp.bfloat16


def mm(lhs, rhs):
    return jnp.dot(lhs, rhs, precision=HIGHEST, preferred_element_type=f32)


def mm_t(lhs, rhs):
    return lax.dot_general(
        lhs, rhs, (((1,), (1,)), ((), ())), precision=HIGHEST, preferred_element_type=f32
    )


def tdot(lhs, rhs):
    return lax.dot_general(lhs, rhs, (((0,), (0,)), ((), ())), preferred_element_type=f32)


def bits(size):
    out, bit = [], 1
    while bit < size:
        out.append(bit)
        bit *= 2
    return out


def flip(value, axis, bit):
    size = lax.axis_size(axis)
    return lax.ppermute(value, axis, [(i, i ^ bit) for i in range(size)])


def shape(dims, dtype):
    return jax.ShapeDtypeStruct(dims, dtype)


def invert_factor(block, work, inverse_ref):
    size = block.shape[0]
    rows = lax.broadcasted_iota(jnp.int32, (size, size), 0)
    cols = lax.broadcasted_iota(jnp.int32, (size, size), 1)
    work[:, :size] = block
    work[:, size:] = jnp.where(rows == cols, 1.0, 0.0)
    sub = lax.broadcasted_iota(jnp.int32, (ROWS, size), 0)
    lane = lax.broadcasted_iota(jnp.int32, (ROWS, size), 1)
    log_sum = jnp.zeros((1, 1), f32)
    for first in range(0, size, ROWS):
        left = work[first : first + ROWS, :size]
        right = work[first : first + ROWS, size:]
        for start in range(0, ROWS, SUB):
            at = first + start
            columns = [
                jnp.broadcast_to(left[:, at + j : at + j + 1], (ROWS, size)) for j in range(SUB)
            ]
            for j in range(SUB):
                i = start + j
                if i == ROWS - 1:
                    break
                factor = jnp.where(sub > i, columns[j], 0.0) * (1.0 / columns[j][i : i + 1, :])
                for k in range(j + 1, SUB):
                    columns[k] = columns[k] - factor * columns[k][i : i + 1, :]
                left = left - factor * left[i : i + 1, :]
                right = right - factor * right[i : i + 1, :]
        pivot = jnp.sum(jnp.where(lane == sub + first, left, 0.0), axis=1, keepdims=True)
        scale = lax.rsqrt(pivot)
        left, right = left * scale, right * scale
        inverse_ref[first : first + ROWS, :] = right
        log_sum = log_sum + jnp.sum(jnp.log(pivot), axis=0, keepdims=True)
        if first + ROWS < size:
            update = lax.dot_general(
                left, jnp.concatenate([left, right], axis=1), (((0,), (0,)), ((), ())),
                precision=HIGHEST, preferred_element_type=f32,
            )
            work[first + ROWS :, :] = work[first + ROWS :, :] - update[first + ROWS :, :]
    return log_sum


def pick_pivots(owner_ref, at_ref, front_ref, table_ref, head_ref, rest_ref, mask_ref, lead_ref):
    b = head_ref.shape[1]
    per = front_ref.shape[1] // b
    for k in range(PL):
        total = jnp.zeros(((k + 1) * b, b), f32)
        for t in range(per):
            part = front_ref[: (k + 1) * b, t * b : (t + 1) * b]
            total = total + jnp.where(owner_ref[t] == k, part, 0.0)
        if k == 0:
            head_ref[:b, :] = total
        elif k == 1:
            head_ref[b:, :] = total
        else:
            rest_ref[...] = total
    lane = lax.broadcasted_iota(jnp.int32, (8, b), 1)
    table = jnp.zeros((8, b), f32)
    for t in range(per):
        table = table + jnp.where(lane == at_ref[0] + t, owner_ref[t].astype(f32), 0.0)
        keep = jnp.where(owner_ref[t] >= PL, 1.0, 0.0).astype(f32)
        mask_ref[:, t * b : (t + 1) * b] = jnp.full((8, b), keep, f32)
    table_ref[...] = table
    lead_ref[...] = front_ref[:, : lead_ref.shape[1]]


def leaf_two(head_ref, w0_ref, w1_ref, mask_ref, p_ref, inv0_ref, inv1_ref, x_ref, log_ref, work):
    b = w0_ref.shape[0]
    c00, c01, c11 = [head_ref[i * b : (i + 1) * b, :] for i in range(3)]
    keep = mask_ref[:1, :] > 0.0
    log0 = invert_factor(c00, work, inv0_ref)
    x01 = mm(inv0_ref[...], c01).astype(bf16)
    x_ref[...] = x01
    p0 = mm(inv0_ref[...], w0_ref[...]).astype(bf16)
    log1 = invert_factor(c11 - tdot(x01, x01), work, inv1_ref)
    p1 = mm(inv1_ref[...], w1_ref[...] - tdot(x01, p0)).astype(bf16)
    p_ref[:b, :] = jnp.where(keep, p0, jnp.zeros_like(p0))
    p_ref[b:, :] = jnp.where(keep, p1, jnp.zeros_like(p1))
    log_ref[...] = jnp.broadcast_to(log0 + log1, log_ref.shape)


def leaf_last(
    rest_ref, w2_ref, w_lead_ref, table_ref, mask_ref, p_ref, inv0_ref, inv1_ref, x_ref, log_ref,
    out_ref, inv, work,
):
    b, cols = w2_ref.shape
    wide = w_lead_ref.shape[1] if w_lead_ref.shape[1] > cols else PR * b
    c02, c12, c22 = [rest_ref[i * b : (i + 1) * b, :] for i in range(3)]
    inv0, inv1, x01 = inv0_ref[...], inv1_ref[...], x_ref[...]
    x02 = mm(inv0, c02).astype(bf16)
    x12 = mm(inv1, c12 - tdot(x01, x02)).astype(bf16)
    log2 = invert_factor(c22 - tdot(x02, x02) - tdot(x12, x12), work, inv)
    inv2 = inv[...]
    keep = mask_ref[:1, :] > 0.0
    panel = mm(inv2, w2_ref[...] - tdot(x02, p_ref[:b, :]) - tdot(x12, p_ref[b:, :])).astype(bf16)
    out_ref[:b, :] = jnp.where(keep, panel, jnp.zeros_like(panel))
    lane = lax.broadcasted_iota(jnp.int32, (1, wide), 1)
    block = jnp.zeros((1, wide), f32)
    for t in range(PR):
        inside = (lane >= t * b) & (lane < (t + 1) * b)
        block = jnp.where(inside, table_ref[:1, t : t + 1], block)
    keep = block > PL - 0.5
    lead0 = mm(inv0, w_lead_ref[:b, :]).astype(bf16)
    lead1 = mm(inv1, w_lead_ref[b : 2 * b, :] - tdot(x01, lead0)).astype(bf16)
    lead2 = w_lead_ref[2 * b :, :] - tdot(x02, lead0) - tdot(x12, lead1)
    lead2 = mm(inv2, lead2).astype(bf16)
    value = log_ref[:1, :1] + log2
    line = lax.broadcasted_iota(jnp.int32, (LOG_ROWS, wide), 0)
    rows = jnp.zeros((LOG_ROWS, wide), f32)
    for i in range(3):
        part = value.astype(bf16).astype(f32)
        rows = jnp.where(line == i, part, rows)
        value = value - part
    leads = [jnp.where(keep, lead, jnp.zeros_like(lead)) for lead in (lead0, lead1, lead2)]
    whole = jnp.concatenate(leads + [rows.astype(bf16)], axis=0)
    if cols >= wide:
        split = cols // wide
        tall = whole.shape[0] // split
        for i in range(split):
            out_ref[b:, i * wide : (i + 1) * wide] = whole[i * tall : (i + 1) * tall, :]
    else:
        tall = whole.shape[0]
        for i in range(wide // cols):
            out_ref[b + i * tall : b + (i + 1) * tall, :] = whole[:, i * cols : (i + 1) * cols]


def rows_kernel(ways, spans, *refs):
    keep_ref, scale_ref = refs[1:3]
    fronts = refs[3 : 3 + ways]
    mask_ref = refs[3 + ways]
    adds = refs[4 + ways : -1]
    out_ref = refs[-1]
    step = pl.program_id(0)
    b = fronts[0].shape[0]
    keep_cols = mask_ref[:1, :] > 0.0
    for i, front_ref in enumerate(fronts):
        at = slice(i * b, (i + 1) * b)
        keep = keep_cols & (keep_ref[step * ways + i] > 0)
        total = jnp.where(keep, front_ref[...], 0.0)
        for add_ref, (first, last) in zip(adds, spans):
            use = (step >= first) & (step < last) & (scale_ref[0] > 0)
            total = total + jnp.where(use, add_ref[at, :], 0.0)
        out_ref[at, :] = total


def take_rows(front, mask, source, kept, scale, ways, adds, name):
    b = B_ROWS
    cols = front.shape[1]
    steps = source.shape[0] // ways
    spans, add_specs = [], []
    for array, first, tile in adds:
        tiles = array.shape[0] // (ways * b) - tile
        last = min(steps, first + tiles)
        spans.append((first, last))

        def index(s, *pre, first=first, last=last, tile=tile):
            return (jnp.clip(s, first, last - 1) - first + tile, 0)

        add_specs.append(pl.BlockSpec((ways * b, cols), index))
    front_specs = [
        pl.BlockSpec((b, cols), lambda s, *pre, i=i: (pre[0][s * ways + i], 0)) for i in range(ways)
    ]

    def body(*refs):
        rows_kernel(ways, spans, *refs)

    return pl.pallas_call(
        body,
        grid_spec=pltpu.PrefetchScalarGridSpec(
            num_scalar_prefetch=3,
            grid=(steps,),
            in_specs=front_specs + [pl.BlockSpec((8, cols), lambda s, *pre: (0, 0))] + add_specs,
            out_specs=pl.BlockSpec((ways * b, cols), lambda s, *pre: (s, 0)),
        ),
        out_shape=shape((source.shape[0] * b, cols), f32),
        compiler_params=pltpu.CompilerParams(vmem_limit_bytes=60 << 20),
        name=name,
    )(source, kept, scale, *([front] * ways), mask, *[array for array, _, _ in adds])


def root_step(
    leaf_ref, corner_ref, first_ref, d01_ref, pack_ref,
    q_ref, inv0_ref, inv1_ref, x_ref, log_ref, work,
):
    b = inv0_ref.shape[0]
    cols = first_ref.shape[1]
    wide = corner_ref.shape[1]
    groups = d01_ref.shape[0] // (2 * b)
    pitch = pack_ref.shape[0] // groups
    corner = corner_ref[...]
    top = first_ref[...]
    lane = lax.broadcasted_iota(jnp.int32, (8, b), 1)
    logs = jnp.zeros((8, b), f32)
    for i in range(groups):
        at = i * pitch
        d2 = pack_ref[at : at + b, :]
        packed = pack_ref[at + b : at + pitch, :]
        if cols >= wide:
            parts = [packed[:, j * wide : (j + 1) * wide] for j in range(cols // wide)]
            whole = jnp.concatenate(parts, axis=0)
        else:
            tall = (pitch - b) // (wide // cols)
            parts = [packed[j * tall : (j + 1) * tall, :] for j in range(wide // cols)]
            whole = jnp.concatenate(parts, axis=1)
        lead = whole[: PL * b, :]
        corner = corner - tdot(lead, lead)
        top = top - tdot(lead[: 2 * b, :], d01_ref[i * 2 * b : (i + 1) * 2 * b, :])
        top = top - tdot(lead[2 * b :, :], d2)
        log_sum = jnp.sum(whole[PL * b : PL * b + 16, :b].astype(f32), axis=0, keepdims=True)
        logs = jnp.where(lane == leaf_ref[i], log_sum * (1.0 / (PL * b)), logs)
    log0 = invert_factor(corner[:b, :b], work, inv0_ref)
    x = mm(inv0_ref[...], corner[:b, b:]).astype(bf16)
    x_ref[...] = x
    log1 = invert_factor(corner[b:, b:] - tdot(x, x), work, inv1_ref)
    log_ref[...] = jnp.where(lane == groups, (log0 + log1) * (1.0 / wide), logs)
    q0 = mm(inv0_ref[...], top[:b, :]).astype(bf16)
    q_ref[:b, :] = q0
    q_ref[b:, :] = mm(inv1_ref[...], top[b:, :] - tdot(x, q0)).astype(bf16)


def update_kernel(slots, *refs):
    place_ref, base_ref, d01_ref = refs[:3]
    r01, out_ref = refs[3 : 3 + slots], refs[3 + slots]

    def at_slot(i):
        out_ref[...] = base_ref[...] - tdot(r01[i][...], d01_ref[...])

    for i in range(slots):
        pl.when(pl.program_id(0) == i)(lambda i=i: at_slot(i))


def finish_kernel(slots, whole_panel, *refs):
    place_ref, info_ref, part_ref = refs[:3]
    d2_ref, q_ref, inv0_ref, inv1_ref, x_ref, panel_ref = refs[3:9]
    r2, rq = refs[9 : 9 + slots], refs[9 + slots : 9 + 2 * slots]
    out_ref = refs[9 + 2 * slots]
    rows, cols = out_ref.shape
    wide = q_ref.shape[0]
    b = wide // PR

    def at_slot(i):
        total = part_ref[...] - tdot(r2[i][...], d2_ref[...])
        row = info_ref[i] + lax.broadcasted_iota(jnp.int32, (rows, cols), 0)
        width = min(wide, cols)
        if whole_panel:
            q0 = mm_t(total[:, :b], inv0_ref[...])
            x_part = jnp.dot(q0.astype(bf16), x_ref[...], preferred_element_type=f32)
            q1 = mm_t(total[:, b:wide] - x_part, inv1_ref[...])
            panel = jnp.concatenate([q0, q1], axis=1)
        else:
            panel = panel_ref[pl.ds(pl.multiple_of(i * rows, rows), rows), :]
        total = total - tdot(rq[i][...], q_ref[...])
        total = jnp.where(row >= wide, total, 0.0)
        col = info_ref[slots] + lax.broadcasted_iota(jnp.int32, (rows, width), 1)
        panel = jnp.where((row[:, :width] >= b) | (col < b), panel, 0.0)
        out_ref[:, :width] = jnp.where(col < wide, panel, total[:, :width])
        if width < cols:
            out_ref[:, width:] = total[:, width:]

    for i in range(slots):
        pl.when(pl.program_id(0) == i)(lambda i=i: at_slot(i))


def local(leaf_fronts, block_owner, root_front):
    members = lax.axis_size("mem")
    groups = lax.axis_size("grp")
    m = lax.axis_index("mem")
    g = lax.axis_index("grp")
    front = leaf_fronts[0]
    order, cols = front.shape
    owner = block_owner[0]
    per = owner.shape[0]
    b = cols // per
    count = order // b
    quarter = order // groups
    spread = members // groups
    quarter_blocks = quarter // b
    pr = PR * b
    lead_cols = min(pr, cols)
    leads = pr // lead_cols
    zone, inner = m // spread, m % spread
    smem = pl.BlockSpec(memory_space=pltpu.SMEM)
    vmem = pl.BlockSpec(memory_space=pltpu.VMEM)

    hops = bits(members)
    last = len(hops) - 1
    lead_order = [hops[-1], hops[0]] + hops[-2:0:-1]

    def lead_hop(value, at):
        bit, used = lead_order[at], sum(lead_order[:at])
        parts = []
        for root in range(leads):
            held = value[root]
            sources = [root ^ i for i in range(members) if i & ~used == 0]
            got = lax.ppermute(held, "mem", [(src, src ^ bit) for src in sources])
            parts.append(jnp.where((m ^ root) & ~used == bit, got, held))
        return parts

    table_rows, head, rest, mask, w_lead = pl.pallas_call(
        pick_pivots,
        grid=(1,),
        in_specs=[smem, smem, pl.BlockSpec((PL * b, cols), lambda i: (0, 0))],
        out_specs=[vmem] * 5,
        out_shape=(
            shape((8, b), f32), shape((3 * b, b), f32), shape((3 * b, b), f32),
            shape((8, cols), f32), shape((PL * b, lead_cols), f32),
        ),
        name="pick_pivots",
    )(owner, (m * per).reshape(1), front)
    w_lead = [w_lead] * leads

    def table_hop(value, at):
        return value + flip(value, "mem", hops[at])

    tie = lax.optimization_barrier
    for at in range(last):
        table_rows = table_hop(table_rows, at)
    head = table_hop(head, 0)
    table_rows, head, rest, w_lead = tie((table_rows, head, rest, w_lead))
    table_rows = table_hop(table_rows, last)
    for at in range(1, last):
        head = table_hop(head, at)
        rest = table_hop(rest, at - 1)
    w_lead = lead_hop(w_lead, 0)
    table_rows, head, rest, w_lead = tie((table_rows, head, rest, w_lead))
    table = table_rows[0, :count].astype(jnp.int32)

    starts = [g ^ (CORE | CHIP), g ^ CHIP, g ^ CORE, g]
    places = jnp.concatenate(
        [s * quarter_blocks + jnp.arange(quarter_blocks) for s in starts] + [jnp.arange(PR)]
    )
    source = jnp.take(table, places)
    kept = (source >= PL).astype(jnp.int32)
    one = jnp.ones((1,), jnp.int32)
    ways = quarter_blocks // 2
    n = quarter_blocks

    def rows_at(first, size, adds, name, scale=one, ways=ways):
        return take_rows(
            front, mask, source[first : first + size], kept[first : first + size], scale, ways,
            adds, name,
        )

    first = rows_at(
        4 * n, PR, [(root_front, 0, 0)], "first_rows", (g == 0).astype(jnp.int32).reshape(1), PR
    )
    first = first + flip(first, "grp", CORE)
    head = table_hop(head, last)
    rest = table_hop(rest, last - 1)
    w_lead = lead_hop(w_lead, 1)
    diagonal = rows_at(0, n, [], "far_rows")
    near = rows_at(2 * n, n, [], "near_rows")
    head, rest, w_lead, first, diagonal, near = tie((head, rest, w_lead, first, diagonal, near))
    diagonal = flip(diagonal, "grp", CORE)
    near = flip(near, "grp", CORE)
    first = first + flip(first, "grp", CHIP)
    rest = table_hop(rest, last)
    for at in range(2, last + 1):
        w_lead = lead_hop(w_lead, at)

    work = [pltpu.VMEM((b, 2 * b), f32)]
    sq = shape((b, b), f32)
    sqh = shape((b, b), bf16)
    logs = shape((8, b), f32)

    def w_spec(k):
        return pl.BlockSpec((b, cols), lambda i: (k, 0))

    p01, inv0, inv1, x01, log01 = pl.pallas_call(
        leaf_two,
        grid=(1,),
        in_specs=[vmem, w_spec(0), w_spec(1), vmem],
        out_specs=[vmem] * 5,
        out_shape=(shape((2 * b, cols), bf16), sq, sq, sqh, logs),
        scratch_shapes=work,
        name="leaf_two",
    )(head, front, front, mask)

    p01, rest, w_lead, first = tie((p01, rest, w_lead, first))

    def across(value):
        far_value = flip(value, "grp", CHIP)
        both = jnp.concatenate([value, far_value], axis=0)
        return jnp.concatenate([both, flip(both, "grp", CORE)], axis=0)

    d01 = across(p01)
    corner = lead_hop([first[:, :lead_cols]] * leads, 0)
    rest, d01, corner = tie((rest, d01, corner))
    corner = lead_hop(corner, 1)
    w_lead = w_lead[0] if leads == 1 else jnp.concatenate(w_lead, axis=1)
    lead_rows = (PL * b + LOG_ROWS) * pr // cols
    pack = pl.pallas_call(
        leaf_last,
        grid=(1,),
        in_specs=[vmem, w_spec(2)] + [vmem] * 8,
        out_specs=vmem,
        out_shape=shape((b + lead_rows, cols), bf16),
        scratch_shapes=[pltpu.VMEM((b, b), f32)] + work,
        name="leaf_last",
    )(rest, front, w_lead, table_rows, mask, p01, inv0, inv1, x01, log01)

    def among(offsets):
        found = jnp.zeros((), jnp.bool_)
        for h in offsets:
            found = found | (zone == (g ^ h))
        return found

    def zone_hop(state):
        have, held, _ = state
        bit = groups // 2 // len(have)
        pairs = []
        for gi in range(groups):
            for h in have:
                for j in range(spread):
                    src = (gi ^ h) * spread + j
                    dst = (gi ^ h ^ bit) * spread + j
                    pairs.append((gi * members + src, gi * members + dst))
        got = lax.ppermute(held, ("grp", "mem"), pairs)
        new = [h ^ bit for h in have]
        return have + new, jnp.where(among(new), got, held), (new, got)

    def inner_hop(stage, i):
        offsets, value = stage
        pairs = []
        for gi in range(groups):
            for h in offsets:
                for j in range(spread):
                    at = gi * members + (gi ^ h) * spread
                    pairs.append((at + j, at + (j ^ i)))
        return lax.ppermute(value, ("grp", "mem"), pairs)

    def inner_hops(state, early=None):
        have, held, last_stage = state
        slots = [held]
        for i in range(1, spread):
            if early is None:
                slots.append(inner_hop((have, held), i))
            else:
                got = inner_hop(last_stage, i)
                slots.append(jnp.where(among(last_stage[0]), got, early[i - 1]))
        return slots

    def early_hops(state):
        return [inner_hop((state[0], state[1]), i) for i in range(1, spread)]

    s01 = zone_hop(([0], d01, None))
    pack, diagonal = tie((pack, diagonal))
    pack_far = flip(pack, "grp", CHIP)
    far_near = flip(rows_at(n, ways, [(diagonal, 0, 0)], "far_sum"), "grp", CHIP)
    pack, pack_far, diagonal, corner = tie((pack, pack_far, diagonal, corner))
    far_in = rows_at(n + ways, ways, [(diagonal, 0, 1)], "far_sum")
    for at in range(2, last + 1):
        corner = lead_hop(corner, at)
    pack = jnp.concatenate([pack, pack_far], axis=0)
    pack = jnp.concatenate([pack, flip(pack, "grp", CORE)], axis=0)
    pack, held, far_in, far_near, corner = tie((pack, s01[1], far_in, far_near, corner))
    corner = corner[0] if leads == 1 else jnp.concatenate(corner, axis=1)
    s01 = (s01[0], held, None)
    far_last = flip(far_in, "grp", CHIP)
    early01 = early_hops(s01)
    s01 = zone_hop(s01)
    d2 = pack.reshape(groups, b + lead_rows, cols)[:, :b].reshape(groups * b, cols)
    s2 = zone_hop(([0], d2, None))
    leaves = jnp.stack([g, g ^ CHIP, g ^ CORE, g ^ (CORE | CHIP)])
    q, rinv0, rinv1, rx, logs_out = pl.pallas_call(
        root_step,
        in_specs=[smem] + [vmem] * 4,
        out_shape=(shape((pr, cols), bf16), sq, sq, sqh, logs),
        scratch_shapes=work,
        compiler_params=pltpu.CompilerParams(vmem_limit_bytes=32 << 20),
        name="root_step",
    )(leaves, corner, first, d01, pack)
    sq_hop = zone_hop(([0], q, None))
    q_held, held, s01_held, s01_got = tie((sq_hop[1], s2[1], s01[1], s01[2][1]))
    s01 = (s01[0], s01_held, (s01[2][0], s01_got))
    s2 = (s2[0], held, None)
    sq_hop = zone_hop((sq_hop[0], q_held, None))
    early2 = early_hops(s2)
    s2 = zone_hop(s2)
    q_held, *early01 = tie((sq_hop[1], *early01))
    rq = inner_hops((sq_hop[0], q_held, None))
    r01 = inner_hops(s01, early01)
    r2 = inner_hops(s2, early2)

    adds = [(root_front, 0, 0), (near, 0, 0), (far_near, 0, 0), (far_last, 1, 0)]
    base = rows_at(3 * n, n, adds, "base_rows")
    slot_of = inner ^ jnp.arange(spread, dtype=jnp.int32)

    def update_body(*refs):
        update_kernel(spread, *refs)

    def whole_spec(array):
        return pl.BlockSpec(array.shape, lambda s, *pre: (0, 0))

    part = pl.pallas_call(
        update_body,
        grid_spec=pltpu.PrefetchScalarGridSpec(
            num_scalar_prefetch=1,
            grid=(spread,),
            in_specs=[pl.BlockSpec((cols, cols), lambda s, place: (place[s], 0))]
            + [whole_spec(array) for array in [d01] + r01],
            out_specs=pl.BlockSpec((cols, cols), lambda s, place: (s, 0)),
        ),
        out_shape=shape((quarter, cols), f32),
        compiler_params=pltpu.CompilerParams(vmem_limit_bytes=40 << 20),
        name="update",
    )(slot_of, base, d01, *r01)
    if leads > 1:
        first_col = jnp.minimum(m, leads - 1) * lead_cols
        panel = jnp.concatenate([rows.astype(f32).T for rows in rq], axis=0)
        panel = lax.dynamic_slice_in_dim(panel, first_col, lead_cols, 1)
    else:
        panel = jnp.zeros((8, lead_cols), f32)
    info = jnp.concatenate([g * quarter + slot_of * cols, (m * cols).reshape(1)])

    def finish_body(*refs):
        finish_kernel(spread, leads == 1, *refs)

    fixed = [d2, q, rinv0, rinv1, rx, panel] + r2 + rq
    root_factor = pl.pallas_call(
        finish_body,
        grid_spec=pltpu.PrefetchScalarGridSpec(
            num_scalar_prefetch=2,
            grid=(spread,),
            in_specs=[pl.BlockSpec((cols, cols), lambda s, place, info: (s, 0))]
            + [whole_spec(array) for array in fixed],
            out_specs=pl.BlockSpec((cols, cols), lambda s, place, info: (place[s], 0)),
        ),
        out_shape=shape((quarter, cols), f32),
        compiler_params=pltpu.CompilerParams(vmem_limit_bytes=40 << 20),
        name="finish",
    )(slot_of, info, part, *fixed)
    return root_factor, logs_out[0, : groups + 1]


def solution(mesh):
    in_specs = (P("grp", None, "mem"), P("grp", "mem"), P("grp", "mem"))
    out_specs = (P("grp", "mem"), P())
    return jax.shard_map(local, mesh=mesh, in_specs=in_specs, out_specs=out_specs, check_vma=False)
```

```python
import jax
import jax.numpy as jnp
from jax import lax
from jax.experimental import pallas as pl
from jax.experimental.pallas import tpu as pltpu
from jax.sharding import PartitionSpec as P

PL = 3
PR = 2
HIGHEST = lax.Precision.HIGHEST
ROWS = 64
SUB = 16
LOG_ROWS = 32
B_ROWS = 128
CORE, CHIP = 1, 2
f32, bf16 = jnp.float32, jnp.bfloat16


def mm(lhs, rhs):
    return jnp.dot(lhs, rhs, precision=HIGHEST, preferred_element_type=f32)


def mm_t(lhs, rhs):
    return lax.dot_general(
        lhs, rhs, (((1,), (1,)), ((), ())), precision=HIGHEST, preferred_element_type=f32
    )


def tdot(lhs, rhs):
    return lax.dot_general(lhs, rhs, (((0,), (0,)), ((), ())), preferred_element_type=f32)


def bits(size):
    out, bit = [], 1
    while bit < size:
        out.append(bit)
        bit *= 2
    return out


def flip(value, axis, bit):
    size = lax.axis_size(axis)
    return lax.ppermute(value, axis, [(i, i ^ bit) for i in range(size)])


def shape(dims, dtype):
    return jax.ShapeDtypeStruct(dims, dtype)


def invert_factor(block, work, inverse_ref):
    size = block.shape[0]
    rows = lax.broadcasted_iota(jnp.int32, (size, size), 0)
    cols = lax.broadcasted_iota(jnp.int32, (size, size), 1)
    work[:, :size] = block
    work[:, size:] = jnp.where(rows == cols, 1.0, 0.0)
    sub = lax.broadcasted_iota(jnp.int32, (ROWS, size), 0)
    lane = lax.broadcasted_iota(jnp.int32, (ROWS, size), 1)
    log_sum = jnp.zeros((1, 1), f32)
    for first in range(0, size, ROWS):
        left = work[first : first + ROWS, :size]
        right = work[first : first + ROWS, size:]
        for start in range(0, ROWS, SUB):
            at = first + start
            columns = [
                jnp.broadcast_to(left[:, at + j : at + j + 1], (ROWS, size)) for j in range(SUB)
            ]
            for j in range(SUB):
                i = start + j
                if i == ROWS - 1:
                    break
                factor = jnp.where(sub > i, columns[j], 0.0) * (1.0 / columns[j][i : i + 1, :])
                for k in range(j + 1, SUB):
                    columns[k] = columns[k] - factor * columns[k][i : i + 1, :]
                left = left - factor * left[i : i + 1, :]
                right = right - factor * right[i : i + 1, :]
        pivot = jnp.sum(jnp.where(lane == sub + first, left, 0.0), axis=1, keepdims=True)
        scale = lax.rsqrt(pivot)
        left, right = left * scale, right * scale
        inverse_ref[first : first + ROWS, :] = right
        log_sum = log_sum + jnp.sum(jnp.log(pivot), axis=0, keepdims=True)
        if first + ROWS < size:
            update = lax.dot_general(
                left, jnp.concatenate([left, right], axis=1), (((0,), (0,)), ((), ())),
                precision=HIGHEST, preferred_element_type=f32,
            )
            work[first + ROWS :, :] = work[first + ROWS :, :] - update[first + ROWS :, :]
    return log_sum


def pick_pivots(owner_ref, at_ref, front_ref, table_ref, head_ref, rest_ref, mask_ref, lead_ref):
    b = head_ref.shape[1]
    per = front_ref.shape[1] // b
    for k in range(PL):
        total = jnp.zeros(((k + 1) * b, b), f32)
        for t in range(per):
            part = front_ref[: (k + 1) * b, t * b : (t + 1) * b]
            total = total + jnp.where(owner_ref[t] == k, part, 0.0)
        if k == 0:
            head_ref[:b, :] = total
        elif k == 1:
            head_ref[b:, :] = total
        else:
            rest_ref[...] = total
    lane = lax.broadcasted_iota(jnp.int32, (8, b), 1)
    table = jnp.zeros((8, b), f32)
    for t in range(per):
        table = table + jnp.where(lane == at_ref[0] + t, owner_ref[t].astype(f32), 0.0)
        keep = jnp.where(owner_ref[t] >= PL, 1.0, 0.0).astype(f32)
        mask_ref[:, t * b : (t + 1) * b] = jnp.full((8, b), keep, f32)
    table_ref[...] = table
    lead_ref[...] = front_ref[:, : lead_ref.shape[1]]


def leaf_two(head_ref, w0_ref, w1_ref, mask_ref, p_ref, inv0_ref, inv1_ref, x_ref, log_ref, work):
    b = w0_ref.shape[0]
    c00, c01, c11 = [head_ref[i * b : (i + 1) * b, :] for i in range(3)]
    keep = mask_ref[:1, :] > 0.0
    log0 = invert_factor(c00, work, inv0_ref)
    x01 = mm(inv0_ref[...], c01).astype(bf16)
    x_ref[...] = x01
    p0 = mm(inv0_ref[...], w0_ref[...]).astype(bf16)
    log1 = invert_factor(c11 - tdot(x01, x01), work, inv1_ref)
    p1 = mm(inv1_ref[...], w1_ref[...] - tdot(x01, p0)).astype(bf16)
    p_ref[:b, :] = jnp.where(keep, p0, jnp.zeros_like(p0))
    p_ref[b:, :] = jnp.where(keep, p1, jnp.zeros_like(p1))
    log_ref[...] = jnp.broadcast_to(log0 + log1, log_ref.shape)


def leaf_last(
    rest_ref, w2_ref, w_lead_ref, table_ref, mask_ref, p_ref, inv0_ref, inv1_ref, x_ref, log_ref,
    out_ref, inv, work,
):
    b, cols = w2_ref.shape
    wide = w_lead_ref.shape[1] if w_lead_ref.shape[1] > cols else PR * b
    c02, c12, c22 = [rest_ref[i * b : (i + 1) * b, :] for i in range(3)]
    inv0, inv1, x01 = inv0_ref[...], inv1_ref[...], x_ref[...]
    x02 = mm(inv0, c02).astype(bf16)
    x12 = mm(inv1, c12 - tdot(x01, x02)).astype(bf16)
    log2 = invert_factor(c22 - tdot(x02, x02) - tdot(x12, x12), work, inv)
    inv2 = inv[...]
    keep = mask_ref[:1, :] > 0.0
    panel = mm(inv2, w2_ref[...] - tdot(x02, p_ref[:b, :]) - tdot(x12, p_ref[b:, :])).astype(bf16)
    out_ref[:b, :] = jnp.where(keep, panel, jnp.zeros_like(panel))
    lane = lax.broadcasted_iota(jnp.int32, (1, wide), 1)
    block = jnp.zeros((1, wide), f32)
    for t in range(PR):
        inside = (lane >= t * b) & (lane < (t + 1) * b)
        block = jnp.where(inside, table_ref[:1, t : t + 1], block)
    keep = block > PL - 0.5
    lead0 = mm(inv0, w_lead_ref[:b, :]).astype(bf16)
    lead1 = mm(inv1, w_lead_ref[b : 2 * b, :] - tdot(x01, lead0)).astype(bf16)
    lead2 = w_lead_ref[2 * b :, :] - tdot(x02, lead0) - tdot(x12, lead1)
    lead2 = mm(inv2, lead2).astype(bf16)
    value = log_ref[:1, :1] + log2
    line = lax.broadcasted_iota(jnp.int32, (LOG_ROWS, wide), 0)
    rows = jnp.zeros((LOG_ROWS, wide), f32)
    for i in range(3):
        part = value.astype(bf16).astype(f32)
        rows = jnp.where(line == i, part, rows)
        value = value - part
    leads = [jnp.where(keep, lead, jnp.zeros_like(lead)) for lead in (lead0, lead1, lead2)]
    whole = jnp.concatenate(leads + [rows.astype(bf16)], axis=0)
    if cols >= wide:
        split = cols // wide
        tall = whole.shape[0] // split
        for i in range(split):
            out_ref[b:, i * wide : (i + 1) * wide] = whole[i * tall : (i + 1) * tall, :]
    else:
        tall = whole.shape[0]
        for i in range(wide // cols):
            out_ref[b + i * tall : b + (i + 1) * tall, :] = whole[:, i * cols : (i + 1) * cols]


def rows_kernel(ways, spans, *refs):
    keep_ref, scale_ref = refs[1:3]
    fronts = refs[3 : 3 + ways]
    mask_ref = refs[3 + ways]
    adds = refs[4 + ways : -1]
    out_ref = refs[-1]
    step = pl.program_id(0)
    b = fronts[0].shape[0]
    keep_cols = mask_ref[:1, :] > 0.0
    for i, front_ref in enumerate(fronts):
        at = slice(i * b, (i + 1) * b)
        keep = keep_cols & (keep_ref[step * ways + i] > 0)
        total = jnp.where(keep, front_ref[...], 0.0)
        for add_ref, (first, last) in zip(adds, spans):
            use = (step >= first) & (step < last) & (scale_ref[0] > 0)
            total = total + jnp.where(use, add_ref[at, :], 0.0)
        out_ref[at, :] = total


def take_rows(front, mask, source, kept, scale, ways, adds, name):
    b = B_ROWS
    cols = front.shape[1]
    steps = source.shape[0] // ways
    spans, add_specs = [], []
    for array, first, tile in adds:
        tiles = array.shape[0] // (ways * b) - tile
        last = min(steps, first + tiles)
        spans.append((first, last))

        def index(s, *pre, first=first, last=last, tile=tile):
            return (jnp.clip(s, first, last - 1) - first + tile, 0)

        add_specs.append(pl.BlockSpec((ways * b, cols), index))
    front_specs = [
        pl.BlockSpec((b, cols), lambda s, *pre, i=i: (pre[0][s * ways + i], 0)) for i in range(ways)
    ]

    def body(*refs):
        rows_kernel(ways, spans, *refs)

    return pl.pallas_call(
        body,
        grid_spec=pltpu.PrefetchScalarGridSpec(
            num_scalar_prefetch=3,
            grid=(steps,),
            in_specs=front_specs + [pl.BlockSpec((8, cols), lambda s, *pre: (0, 0))] + add_specs,
            out_specs=pl.BlockSpec((ways * b, cols), lambda s, *pre: (s, 0)),
        ),
        out_shape=shape((source.shape[0] * b, cols), f32),
        compiler_params=pltpu.CompilerParams(vmem_limit_bytes=60 << 20),
        name=name,
    )(source, kept, scale, *([front] * ways), mask, *[array for array, _, _ in adds])


def root_step(
    leaf_ref, corner_ref, first_ref, d01_ref, pack_ref,
    q_ref, inv0_ref, inv1_ref, x_ref, log_ref, work,
):
    b = inv0_ref.shape[0]
    cols = first_ref.shape[1]
    wide = corner_ref.shape[1]
    groups = d01_ref.shape[0] // (2 * b)
    pitch = pack_ref.shape[0] // groups
    corner = corner_ref[...]
    top = first_ref[...]
    lane = lax.broadcasted_iota(jnp.int32, (8, b), 1)
    logs = jnp.zeros((8, b), f32)
    for i in range(groups):
        at = i * pitch
        d2 = pack_ref[at : at + b, :]
        packed = pack_ref[at + b : at + pitch, :]
        if cols >= wide:
            parts = [packed[:, j * wide : (j + 1) * wide] for j in range(cols // wide)]
            whole = jnp.concatenate(parts, axis=0)
        else:
            tall = (pitch - b) // (wide // cols)
            parts = [packed[j * tall : (j + 1) * tall, :] for j in range(wide // cols)]
            whole = jnp.concatenate(parts, axis=1)
        lead = whole[: PL * b, :]
        corner = corner - tdot(lead, lead)
        top = top - tdot(lead[: 2 * b, :], d01_ref[i * 2 * b : (i + 1) * 2 * b, :])
        top = top - tdot(lead[2 * b :, :], d2)
        log_sum = jnp.sum(whole[PL * b : PL * b + 16, :b].astype(f32), axis=0, keepdims=True)
        logs = jnp.where(lane == leaf_ref[i], log_sum * (1.0 / (PL * b)), logs)
    log0 = invert_factor(corner[:b, :b], work, inv0_ref)
    x = mm(inv0_ref[...], corner[:b, b:]).astype(bf16)
    x_ref[...] = x
    log1 = invert_factor(corner[b:, b:] - tdot(x, x), work, inv1_ref)
    log_ref[...] = jnp.where(lane == groups, (log0 + log1) * (1.0 / wide), logs)
    q0 = mm(inv0_ref[...], top[:b, :]).astype(bf16)
    q_ref[:b, :] = q0
    q_ref[b:, :] = mm(inv1_ref[...], top[b:, :] - tdot(x, q0)).astype(bf16)


def update_kernel(slots, *refs):
    place_ref, base_ref, d01_ref = refs[:3]
    r01, out_ref = refs[3 : 3 + slots], refs[3 + slots]

    def at_slot(i):
        out_ref[...] = base_ref[...] - tdot(r01[i][...], d01_ref[...])

    for i in range(slots):
        pl.when(pl.program_id(0) == i)(lambda i=i: at_slot(i))


def finish_kernel(slots, whole_panel, *refs):
    place_ref, info_ref, part_ref = refs[:3]
    d2_ref, q_ref, inv0_ref, inv1_ref, x_ref, panel_ref = refs[3:9]
    r2, rq = refs[9 : 9 + slots], refs[9 + slots : 9 + 2 * slots]
    out_ref = refs[9 + 2 * slots]
    rows, cols = out_ref.shape
    wide = q_ref.shape[0]
    b = wide // PR

    def at_slot(i):
        total = part_ref[...] - tdot(r2[i][...], d2_ref[...])
        row = info_ref[i] + lax.broadcasted_iota(jnp.int32, (rows, cols), 0)
        width = min(wide, cols)
        if whole_panel:
            q0 = mm_t(total[:, :b], inv0_ref[...])
            x_part = jnp.dot(q0.astype(bf16), x_ref[...], preferred_element_type=f32)
            q1 = mm_t(total[:, b:wide] - x_part, inv1_ref[...])
            panel = jnp.concatenate([q0, q1], axis=1)
        else:
            panel = panel_ref[pl.ds(pl.multiple_of(i * rows, rows), rows), :]
        total = total - tdot(rq[i][...], q_ref[...])
        total = jnp.where(row >= wide, total, 0.0)
        col = info_ref[slots] + lax.broadcasted_iota(jnp.int32, (rows, width), 1)
        panel = jnp.where((row[:, :width] >= b) | (col < b), panel, 0.0)
        out_ref[:, :width] = jnp.where(col < wide, panel, total[:, :width])
        if width < cols:
            out_ref[:, width:] = total[:, width:]

    for i in range(slots):
        pl.when(pl.program_id(0) == i)(lambda i=i: at_slot(i))


def local(leaf_fronts, block_owner, root_front):
    members = lax.axis_size("mem")
    groups = lax.axis_size("grp")
    m = lax.axis_index("mem")
    g = lax.axis_index("grp")
    front = leaf_fronts[0]
    order, cols = front.shape
    owner = block_owner[0]
    per = owner.shape[0]
    b = cols // per
    count = order // b
    quarter = order // groups
    spread = members // groups
    quarter_blocks = quarter // b
    pr = PR * b
    lead_cols = min(pr, cols)
    leads = pr // lead_cols
    zone, inner = m // spread, m % spread
    smem = pl.BlockSpec(memory_space=pltpu.SMEM)
    vmem = pl.BlockSpec(memory_space=pltpu.VMEM)

    hops = bits(members)
    last = len(hops) - 1
    lead_order = [hops[-1], hops[0]] + hops[-2:0:-1]

    def lead_hop(value, at):
        bit, used = lead_order[at], sum(lead_order[:at])
        parts = []
        for root in range(leads):
            held = value[root]
            sources = [root ^ i for i in range(members) if i & ~used == 0]
            got = lax.ppermute(held, "mem", [(src, src ^ bit) for src in sources])
            parts.append(jnp.where((m ^ root) & ~used == bit, got, held))
        return parts

    table_rows, head, rest, mask, w_lead = pl.pallas_call(
        pick_pivots,
        grid=(1,),
        in_specs=[smem, smem, pl.BlockSpec((PL * b, cols), lambda i: (0, 0))],
        out_specs=[vmem] * 5,
        out_shape=(
            shape((8, b), f32), shape((3 * b, b), f32), shape((3 * b, b), f32),
            shape((8, cols), f32), shape((PL * b, lead_cols), f32),
        ),
        name="pick_pivots",
    )(owner, (m * per).reshape(1), front)
    w_lead = [w_lead] * leads

    def table_hop(value, at):
        return value + flip(value, "mem", hops[at])

    tie = lax.optimization_barrier
    for at in range(last):
        table_rows = table_hop(table_rows, at)
    head = table_hop(head, 0)
    table_rows, head, rest, w_lead = tie((table_rows, head, rest, w_lead))
    table_rows = table_hop(table_rows, last)
    for at in range(1, last):
        head = table_hop(head, at)
        rest = table_hop(rest, at - 1)
    w_lead = lead_hop(w_lead, 0)
    table_rows, head, rest, w_lead = tie((table_rows, head, rest, w_lead))
    table = table_rows[0, :count].astype(jnp.int32)

    starts = [g ^ (CORE | CHIP), g ^ CHIP, g ^ CORE, g]
    places = jnp.concatenate(
        [s * quarter_blocks + jnp.arange(quarter_blocks) for s in starts] + [jnp.arange(PR)]
    )
    source = jnp.take(table, places)
    kept = (source >= PL).astype(jnp.int32)
    one = jnp.ones((1,), jnp.int32)
    ways = quarter_blocks // 2
    n = quarter_blocks

    def rows_at(first, size, adds, name, scale=one, ways=ways):
        return take_rows(
            front, mask, source[first : first + size], kept[first : first + size], scale, ways,
            adds, name,
        )

    first = rows_at(
        4 * n, PR, [(root_front, 0, 0)], "first_rows", (g == 0).astype(jnp.int32).reshape(1), PR
    )
    first = first + flip(first, "grp", CORE)
    head = table_hop(head, last)
    rest = table_hop(rest, last - 1)
    w_lead = lead_hop(w_lead, 1)
    diagonal = rows_at(0, n, [], "far_rows")
    near = rows_at(2 * n, n, [], "near_rows")
    head, rest, w_lead, first, diagonal, near = tie((head, rest, w_lead, first, diagonal, near))
    diagonal = flip(diagonal, "grp", CORE)
    near = flip(near, "grp", CORE)
    first = first + flip(first, "grp", CHIP)
    rest = table_hop(rest, last)
    for at in range(2, last + 1):
        w_lead = lead_hop(w_lead, at)

    work = [pltpu.VMEM((b, 2 * b), f32)]
    sq = shape((b, b), f32)
    sqh = shape((b, b), bf16)
    logs = shape((8, b), f32)

    def w_spec(k):
        return pl.BlockSpec((b, cols), lambda i: (k, 0))

    p01, inv0, inv1, x01, log01 = pl.pallas_call(
        leaf_two,
        grid=(1,),
        in_specs=[vmem, w_spec(0), w_spec(1), vmem],
        out_specs=[vmem] * 5,
        out_shape=(shape((2 * b, cols), bf16), sq, sq, sqh, logs),
        scratch_shapes=work,
        name="leaf_two",
    )(head, front, front, mask)

    p01, rest, w_lead, first = tie((p01, rest, w_lead, first))

    def across(value):
        far_value = flip(value, "grp", CHIP)
        both = jnp.concatenate([value, far_value], axis=0)
        return jnp.concatenate([both, flip(both, "grp", CORE)], axis=0)

    d01 = across(p01)
    corner = lead_hop([first[:, :lead_cols]] * leads, 0)
    rest, d01, corner = tie((rest, d01, corner))
    corner = lead_hop(corner, 1)
    w_lead = w_lead[0] if leads == 1 else jnp.concatenate(w_lead, axis=1)
    lead_rows = (PL * b + LOG_ROWS) * pr // cols
    pack = pl.pallas_call(
        leaf_last,
        grid=(1,),
        in_specs=[vmem, w_spec(2)] + [vmem] * 8,
        out_specs=vmem,
        out_shape=shape((b + lead_rows, cols), bf16),
        scratch_shapes=[pltpu.VMEM((b, b), f32)] + work,
        name="leaf_last",
    )(rest, front, w_lead, table_rows, mask, p01, inv0, inv1, x01, log01)

    def among(offsets):
        found = jnp.zeros((), jnp.bool_)
        for h in offsets:
            found = found | (zone == (g ^ h))
        return found

    def zone_hop(state):
        have, held, _ = state
        bit = groups // 2 // len(have)
        pairs = []
        for gi in range(groups):
            for h in have:
                for j in range(spread):
                    src = (gi ^ h) * spread + j
                    dst = (gi ^ h ^ bit) * spread + j
                    pairs.append((gi * members + src, gi * members + dst))
        got = lax.ppermute(held, ("grp", "mem"), pairs)
        new = [h ^ bit for h in have]
        return have + new, jnp.where(among(new), got, held), (new, got)

    def inner_hop(stage, i):
        offsets, value = stage
        pairs = []
        for gi in range(groups):
            for h in offsets:
                for j in range(spread):
                    at = gi * members + (gi ^ h) * spread
                    pairs.append((at + j, at + (j ^ i)))
        return lax.ppermute(value, ("grp", "mem"), pairs)

    def inner_hops(state, early=None):
        have, held, last_stage = state
        slots = [held]
        for i in range(1, spread):
            if early is None:
                slots.append(inner_hop((have, held), i))
            else:
                got = inner_hop(last_stage, i)
                slots.append(jnp.where(among(last_stage[0]), got, early[i - 1]))
        return slots

    def early_hops(state):
        return [inner_hop((state[0], state[1]), i) for i in range(1, spread)]

    s01 = zone_hop(([0], d01, None))
    pack, diagonal, corner = tie((pack, diagonal, corner))
    pack_far = flip(pack, "grp", CHIP)
    for at in range(2, last + 1):
        corner = lead_hop(corner, at)
    few = n // 4
    far_near = rows_at(n, few, [(diagonal, 0, 0)], "far_sum", ways=few)
    far_near = flip(far_near, "grp", CHIP)
    pack, pack_far, diagonal, corner = tie((pack, pack_far, diagonal, corner))
    far_in = rows_at(n + few, n - few, [(diagonal, 0, 1)], "far_sum", ways=few)
    pack = jnp.concatenate([pack, pack_far], axis=0)
    pack = jnp.concatenate([pack, flip(pack, "grp", CORE)], axis=0)
    pack, held, far_in, far_near, corner = tie((pack, s01[1], far_in, far_near, corner))
    corner = corner[0] if leads == 1 else jnp.concatenate(corner, axis=1)
    s01 = (s01[0], held, None)
    far_last = flip(far_in, "grp", CHIP)
    early01 = early_hops(s01)
    s01 = zone_hop(s01)
    d2 = pack.reshape(groups, b + lead_rows, cols)[:, :b].reshape(groups * b, cols)
    s2 = zone_hop(([0], d2, None))
    leaves = jnp.stack([g, g ^ CHIP, g ^ CORE, g ^ (CORE | CHIP)])
    q, rinv0, rinv1, rx, logs_out = pl.pallas_call(
        root_step,
        in_specs=[smem] + [vmem] * 4,
        out_shape=(shape((pr, cols), bf16), sq, sq, sqh, logs),
        scratch_shapes=work,
        compiler_params=pltpu.CompilerParams(vmem_limit_bytes=32 << 20),
        name="root_step",
    )(leaves, corner, first, d01, pack)
    sq_hop = zone_hop(([0], q, None))
    q_held, held, s01_held, s01_got = tie((sq_hop[1], s2[1], s01[1], s01[2][1]))
    s01 = (s01[0], s01_held, (s01[2][0], s01_got))
    s2 = (s2[0], held, None)
    sq_hop = zone_hop((sq_hop[0], q_held, None))
    early2 = early_hops(s2)
    s2 = zone_hop(s2)
    q_held, *early01 = tie((sq_hop[1], *early01))
    rq = inner_hops((sq_hop[0], q_held, None))
    r01 = inner_hops(s01, early01)
    r2 = inner_hops(s2, early2)

    adds = [(root_front, 0, 0), (near, 0, 0), (far_near, 0, 0), (far_last, 1, 0)]
    base = rows_at(3 * n, n, adds, "base_rows", ways=few)
    slot_of = inner ^ jnp.arange(spread, dtype=jnp.int32)

    def update_body(*refs):
        update_kernel(spread, *refs)

    def whole_spec(array):
        return pl.BlockSpec(array.shape, lambda s, *pre: (0, 0))

    part = pl.pallas_call(
        update_body,
        grid_spec=pltpu.PrefetchScalarGridSpec(
            num_scalar_prefetch=1,
            grid=(spread,),
            in_specs=[pl.BlockSpec((cols, cols), lambda s, place: (place[s], 0))]
            + [whole_spec(array) for array in [d01] + r01],
            out_specs=pl.BlockSpec((cols, cols), lambda s, place: (s, 0)),
        ),
        out_shape=shape((quarter, cols), f32),
        compiler_params=pltpu.CompilerParams(vmem_limit_bytes=40 << 20),
        name="update",
    )(slot_of, base, d01, *r01)
    if leads > 1:
        first_col = jnp.minimum(m, leads - 1) * lead_cols
        panel = jnp.concatenate([rows.astype(f32).T for rows in rq], axis=0)
        panel = lax.dynamic_slice_in_dim(panel, first_col, lead_cols, 1)
    else:
        panel = jnp.zeros((8, lead_cols), f32)
    info = jnp.concatenate([g * quarter + slot_of * cols, (m * cols).reshape(1)])

    def finish_body(*refs):
        finish_kernel(spread, leads == 1, *refs)

    fixed = [d2, q, rinv0, rinv1, rx, panel] + r2 + rq
    root_factor = pl.pallas_call(
        finish_body,
        grid_spec=pltpu.PrefetchScalarGridSpec(
            num_scalar_prefetch=2,
            grid=(spread,),
            in_specs=[pl.BlockSpec((cols, cols), lambda s, place, info: (s, 0))]
            + [whole_spec(array) for array in fixed],
            out_specs=pl.BlockSpec((cols, cols), lambda s, place, info: (place[s], 0)),
        ),
        out_shape=shape((quarter, cols), f32),
        compiler_params=pltpu.CompilerParams(vmem_limit_bytes=40 << 20),
        name="finish",
    )(slot_of, info, part, *fixed)
    return root_factor, logs_out[0, : groups + 1]


def solution(mesh):
    in_specs = (P("grp", None, "mem"), P("grp", "mem"), P("grp", "mem"))
    out_specs = (P("grp", "mem"), P())
    return jax.shard_map(local, mesh=mesh, in_specs=in_specs, out_specs=out_specs, check_vma=False)
```

```python
import jax
import jax.numpy as jnp
from jax import lax
from jax.experimental import pallas as pl
from jax.experimental.pallas import tpu as pltpu
from jax.sharding import PartitionSpec as P

PL = 3
PR = 2
HIGHEST = lax.Precision.HIGHEST
ROWS = 64
SUB = 16
LOG_ROWS = 32
B_ROWS = 128
CORE, CHIP = 1, 2
f32, bf16 = jnp.float32, jnp.bfloat16


def mm(lhs, rhs):
    return jnp.dot(lhs, rhs, precision=HIGHEST, preferred_element_type=f32)


def mm_t(lhs, rhs):
    return lax.dot_general(
        lhs, rhs, (((1,), (1,)), ((), ())), precision=HIGHEST, preferred_element_type=f32
    )


def tdot(lhs, rhs):
    return lax.dot_general(lhs, rhs, (((0,), (0,)), ((), ())), preferred_element_type=f32)


def bits(size):
    out, bit = [], 1
    while bit < size:
        out.append(bit)
        bit *= 2
    return out


def flip(value, axis, bit):
    size = lax.axis_size(axis)
    return lax.ppermute(value, axis, [(i, i ^ bit) for i in range(size)])


def shape(dims, dtype):
    return jax.ShapeDtypeStruct(dims, dtype)


def invert_factor(block, work, inverse_ref):
    size = block.shape[0]
    rows = lax.broadcasted_iota(jnp.int32, (size, size), 0)
    cols = lax.broadcasted_iota(jnp.int32, (size, size), 1)
    work[:, :size] = block
    work[:, size:] = jnp.where(rows == cols, 1.0, 0.0)
    sub = lax.broadcasted_iota(jnp.int32, (ROWS, size), 0)
    lane = lax.broadcasted_iota(jnp.int32, (ROWS, size), 1)
    log_sum = jnp.zeros((1, 1), f32)
    for first in range(0, size, ROWS):
        left = work[first : first + ROWS, :size]
        right = work[first : first + ROWS, size:]
        for start in range(0, ROWS, SUB):
            at = first + start
            columns = [
                jnp.broadcast_to(left[:, at + j : at + j + 1], (ROWS, size)) for j in range(SUB)
            ]
            for j in range(SUB):
                i = start + j
                if i == ROWS - 1:
                    break
                factor = jnp.where(sub > i, columns[j], 0.0) * (1.0 / columns[j][i : i + 1, :])
                for k in range(j + 1, SUB):
                    columns[k] = columns[k] - factor * columns[k][i : i + 1, :]
                left = left - factor * left[i : i + 1, :]
                right = right - factor * right[i : i + 1, :]
        pivot = jnp.sum(jnp.where(lane == sub + first, left, 0.0), axis=1, keepdims=True)
        scale = lax.rsqrt(pivot)
        left, right = left * scale, right * scale
        inverse_ref[first : first + ROWS, :] = right
        log_sum = log_sum + jnp.sum(jnp.log(pivot), axis=0, keepdims=True)
        if first + ROWS < size:
            update = lax.dot_general(
                left, jnp.concatenate([left, right], axis=1), (((0,), (0,)), ((), ())),
                precision=HIGHEST, preferred_element_type=f32,
            )
            work[first + ROWS :, :] = work[first + ROWS :, :] - update[first + ROWS :, :]
    return log_sum


def pick_pivots(owner_ref, at_ref, front_ref, table_ref, head_ref, rest_ref, mask_ref, lead_ref):
    b = head_ref.shape[1]
    per = front_ref.shape[1] // b
    for k in range(PL):
        total = jnp.zeros(((k + 1) * b, b), f32)
        for t in range(per):
            part = front_ref[: (k + 1) * b, t * b : (t + 1) * b]
            total = total + jnp.where(owner_ref[t] == k, part, 0.0)
        if k == 0:
            head_ref[:b, :] = total
        elif k == 1:
            head_ref[b:, :] = total
        else:
            rest_ref[...] = total
    lane = lax.broadcasted_iota(jnp.int32, (8, b), 1)
    table = jnp.zeros((8, b), f32)
    for t in range(per):
        table = table + jnp.where(lane == at_ref[0] + t, owner_ref[t].astype(f32), 0.0)
        keep = jnp.where(owner_ref[t] >= PL, 1.0, 0.0).astype(f32)
        mask_ref[:, t * b : (t + 1) * b] = jnp.full((8, b), keep, f32)
    table_ref[...] = table
    lead_ref[...] = front_ref[:, : lead_ref.shape[1]]


def leaf_two(head_ref, w0_ref, w1_ref, mask_ref, p_ref, inv0_ref, inv1_ref, x_ref, log_ref, work):
    b = w0_ref.shape[0]
    c00, c01, c11 = [head_ref[i * b : (i + 1) * b, :] for i in range(3)]
    keep = mask_ref[:1, :] > 0.0
    log0 = invert_factor(c00, work, inv0_ref)
    x01 = mm(inv0_ref[...], c01).astype(bf16)
    x_ref[...] = x01
    p0 = mm(inv0_ref[...], w0_ref[...]).astype(bf16)
    log1 = invert_factor(c11 - tdot(x01, x01), work, inv1_ref)
    p1 = mm(inv1_ref[...], w1_ref[...] - tdot(x01, p0)).astype(bf16)
    p_ref[:b, :] = jnp.where(keep, p0, jnp.zeros_like(p0))
    p_ref[b:, :] = jnp.where(keep, p1, jnp.zeros_like(p1))
    log_ref[...] = jnp.broadcast_to(log0 + log1, log_ref.shape)


def leaf_last(
    rest_ref, w2_ref, w_lead_ref, table_ref, mask_ref, p_ref, inv0_ref, inv1_ref, x_ref, log_ref,
    out_ref, inv, work,
):
    b, cols = w2_ref.shape
    wide = w_lead_ref.shape[1] if w_lead_ref.shape[1] > cols else PR * b
    c02, c12, c22 = [rest_ref[i * b : (i + 1) * b, :] for i in range(3)]
    inv0, inv1, x01 = inv0_ref[...], inv1_ref[...], x_ref[...]
    x02 = mm(inv0, c02).astype(bf16)
    x12 = mm(inv1, c12 - tdot(x01, x02)).astype(bf16)
    log2 = invert_factor(c22 - tdot(x02, x02) - tdot(x12, x12), work, inv)
    inv2 = inv[...]
    keep = mask_ref[:1, :] > 0.0
    panel = mm(inv2, w2_ref[...] - tdot(x02, p_ref[:b, :]) - tdot(x12, p_ref[b:, :])).astype(bf16)
    out_ref[:b, :] = jnp.where(keep, panel, jnp.zeros_like(panel))
    lane = lax.broadcasted_iota(jnp.int32, (1, wide), 1)
    block = jnp.zeros((1, wide), f32)
    for t in range(PR):
        inside = (lane >= t * b) & (lane < (t + 1) * b)
        block = jnp.where(inside, table_ref[:1, t : t + 1], block)
    keep = block > PL - 0.5
    lead0 = mm(inv0, w_lead_ref[:b, :]).astype(bf16)
    lead1 = mm(inv1, w_lead_ref[b : 2 * b, :] - tdot(x01, lead0)).astype(bf16)
    lead2 = w_lead_ref[2 * b :, :] - tdot(x02, lead0) - tdot(x12, lead1)
    lead2 = mm(inv2, lead2).astype(bf16)
    value = log_ref[:1, :1] + log2
    line = lax.broadcasted_iota(jnp.int32, (LOG_ROWS, wide), 0)
    rows = jnp.zeros((LOG_ROWS, wide), f32)
    for i in range(3):
        part = value.astype(bf16).astype(f32)
        rows = jnp.where(line == i, part, rows)
        value = value - part
    leads = [jnp.where(keep, lead, jnp.zeros_like(lead)) for lead in (lead0, lead1, lead2)]
    whole = jnp.concatenate(leads + [rows.astype(bf16)], axis=0)
    if cols >= wide:
        split = cols // wide
        tall = whole.shape[0] // split
        for i in range(split):
            out_ref[b:, i * wide : (i + 1) * wide] = whole[i * tall : (i + 1) * tall, :]
    else:
        tall = whole.shape[0]
        for i in range(wide // cols):
            out_ref[b + i * tall : b + (i + 1) * tall, :] = whole[:, i * cols : (i + 1) * cols]


def rows_kernel(ways, spans, *refs):
    keep_ref, scale_ref = refs[1:3]
    fronts = refs[3 : 3 + ways]
    mask_ref = refs[3 + ways]
    adds = refs[4 + ways : -1]
    out_ref = refs[-1]
    step = pl.program_id(0)
    b = fronts[0].shape[0]
    keep_cols = mask_ref[:1, :] > 0.0
    for i, front_ref in enumerate(fronts):
        at = slice(i * b, (i + 1) * b)
        keep = keep_cols & (keep_ref[step * ways + i] > 0)
        total = jnp.where(keep, front_ref[...], 0.0)
        for add_ref, (first, last) in zip(adds, spans):
            use = (step >= first) & (step < last) & (scale_ref[0] > 0)
            total = total + jnp.where(use, add_ref[at, :], 0.0)
        out_ref[at, :] = total


def take_rows(front, mask, source, kept, scale, ways, adds, name):
    b = B_ROWS
    cols = front.shape[1]
    steps = source.shape[0] // ways
    spans, add_specs = [], []
    for array, first, tile in adds:
        tiles = array.shape[0] // (ways * b) - tile
        last = min(steps, first + tiles)
        spans.append((first, last))

        def index(s, *pre, first=first, last=last, tile=tile):
            return (jnp.clip(s, first, last - 1) - first + tile, 0)

        add_specs.append(pl.BlockSpec((ways * b, cols), index))
    front_specs = [
        pl.BlockSpec((b, cols), lambda s, *pre, i=i: (pre[0][s * ways + i], 0)) for i in range(ways)
    ]

    def body(*refs):
        rows_kernel(ways, spans, *refs)

    return pl.pallas_call(
        body,
        grid_spec=pltpu.PrefetchScalarGridSpec(
            num_scalar_prefetch=3,
            grid=(steps,),
            in_specs=front_specs + [pl.BlockSpec((8, cols), lambda s, *pre: (0, 0))] + add_specs,
            out_specs=pl.BlockSpec((ways * b, cols), lambda s, *pre: (s, 0)),
        ),
        out_shape=shape((source.shape[0] * b, cols), f32),
        compiler_params=pltpu.CompilerParams(vmem_limit_bytes=60 << 20),
        name=name,
    )(source, kept, scale, *([front] * ways), mask, *[array for array, _, _ in adds])


def root_step(
    leaf_ref, corner_ref, first_ref, d01_ref, pack_ref,
    q_ref, inv0_ref, inv1_ref, x_ref, log_ref, work,
):
    b = inv0_ref.shape[0]
    cols = first_ref.shape[1]
    wide = corner_ref.shape[1]
    groups = d01_ref.shape[0] // (2 * b)
    pitch = pack_ref.shape[0] // groups
    corner = corner_ref[...]
    top = first_ref[...]
    lane = lax.broadcasted_iota(jnp.int32, (8, b), 1)
    logs = jnp.zeros((8, b), f32)
    for i in range(groups):
        at = i * pitch
        d2 = pack_ref[at : at + b, :]
        packed = pack_ref[at + b : at + pitch, :]
        if cols >= wide:
            parts = [packed[:, j * wide : (j + 1) * wide] for j in range(cols // wide)]
            whole = jnp.concatenate(parts, axis=0)
        else:
            tall = (pitch - b) // (wide // cols)
            parts = [packed[j * tall : (j + 1) * tall, :] for j in range(wide // cols)]
            whole = jnp.concatenate(parts, axis=1)
        lead = whole[: PL * b, :]
        corner = corner - tdot(lead, lead)
        top = top - tdot(lead[: 2 * b, :], d01_ref[i * 2 * b : (i + 1) * 2 * b, :])
        top = top - tdot(lead[2 * b :, :], d2)
        log_sum = jnp.sum(whole[PL * b : PL * b + 16, :b].astype(f32), axis=0, keepdims=True)
        logs = jnp.where(lane == leaf_ref[i], log_sum * (1.0 / (PL * b)), logs)
    log0 = invert_factor(corner[:b, :b], work, inv0_ref)
    x = mm(inv0_ref[...], corner[:b, b:]).astype(bf16)
    x_ref[...] = x
    log1 = invert_factor(corner[b:, b:] - tdot(x, x), work, inv1_ref)
    log_ref[...] = jnp.where(lane == groups, (log0 + log1) * (1.0 / wide), logs)
    q0 = mm(inv0_ref[...], top[:b, :]).astype(bf16)
    q_ref[:b, :] = q0
    q_ref[b:, :] = mm(inv1_ref[...], top[b:, :] - tdot(x, q0)).astype(bf16)


def update_kernel(slots, *refs):
    place_ref, base_ref, d01_ref = refs[:3]
    r01, out_ref = refs[3 : 3 + slots], refs[3 + slots]

    def at_slot(i):
        out_ref[...] = base_ref[...] - tdot(r01[i][...], d01_ref[...])

    for i in range(slots):
        pl.when(pl.program_id(0) == i)(lambda i=i: at_slot(i))


def finish_kernel(slots, whole_panel, *refs):
    place_ref, info_ref, part_ref = refs[:3]
    d2_ref, q_ref, inv0_ref, inv1_ref, x_ref, panel_ref = refs[3:9]
    r2, rq = refs[9 : 9 + slots], refs[9 + slots : 9 + 2 * slots]
    out_ref = refs[9 + 2 * slots]
    rows, cols = out_ref.shape
    wide = q_ref.shape[0]
    b = wide // PR

    def at_slot(i):
        total = part_ref[...] - tdot(r2[i][...], d2_ref[...])
        row = info_ref[i] + lax.broadcasted_iota(jnp.int32, (rows, cols), 0)
        width = min(wide, cols)
        if whole_panel:
            q0 = mm_t(total[:, :b], inv0_ref[...])
            x_part = jnp.dot(q0.astype(bf16), x_ref[...], preferred_element_type=f32)
            q1 = mm_t(total[:, b:wide] - x_part, inv1_ref[...])
            panel = jnp.concatenate([q0, q1], axis=1)
        else:
            panel = panel_ref[pl.ds(pl.multiple_of(i * rows, rows), rows), :]
        total = total - tdot(rq[i][...], q_ref[...])
        total = jnp.where(row >= wide, total, 0.0)
        col = info_ref[slots] + lax.broadcasted_iota(jnp.int32, (rows, width), 1)
        panel = jnp.where((row[:, :width] >= b) | (col < b), panel, 0.0)
        out_ref[:, :width] = jnp.where(col < wide, panel, total[:, :width])
        if width < cols:
            out_ref[:, width:] = total[:, width:]

    for i in range(slots):
        pl.when(pl.program_id(0) == i)(lambda i=i: at_slot(i))


def local(leaf_fronts, block_owner, root_front):
    members = lax.axis_size("mem")
    groups = lax.axis_size("grp")
    m = lax.axis_index("mem")
    g = lax.axis_index("grp")
    front = leaf_fronts[0]
    order, cols = front.shape
    owner = block_owner[0]
    per = owner.shape[0]
    b = cols // per
    count = order // b
    quarter = order // groups
    spread = members // groups
    quarter_blocks = quarter // b
    pr = PR * b
    lead_cols = min(pr, cols)
    leads = pr // lead_cols
    zone, inner = m // spread, m % spread
    smem = pl.BlockSpec(memory_space=pltpu.SMEM)
    vmem = pl.BlockSpec(memory_space=pltpu.VMEM)

    hops = bits(members)
    last = len(hops) - 1
    lead_order = [hops[-1], hops[0]] + hops[-2:0:-1]

    def lead_hop(value, at, lead_order=lead_order):
        bit, used = lead_order[at], sum(lead_order[:at])
        parts = []
        for root in range(leads):
            held = value[root]
            sources = [root ^ i for i in range(members) if i & ~used == 0]
            got = lax.ppermute(held, "mem", [(src, src ^ bit) for src in sources])
            parts.append(jnp.where((m ^ root) & ~used == bit, got, held))
        return parts

    table_rows, head, rest, mask, w_lead = pl.pallas_call(
        pick_pivots,
        grid=(1,),
        in_specs=[smem, smem, pl.BlockSpec((PL * b, cols), lambda i: (0, 0))],
        out_specs=[vmem] * 5,
        out_shape=(
            shape((8, b), f32), shape((3 * b, b), f32), shape((3 * b, b), f32),
            shape((8, cols), f32), shape((PL * b, lead_cols), f32),
        ),
        name="pick_pivots",
    )(owner, (m * per).reshape(1), front)
    w_lead = [w_lead] * leads

    def table_hop(value, at):
        return value + flip(value, "mem", hops[at])

    tie = lax.optimization_barrier
    for at in range(last):
        table_rows = table_hop(table_rows, at)
    head = table_hop(head, 0)
    table_rows, head, rest, w_lead = tie((table_rows, head, rest, w_lead))
    table_rows = table_hop(table_rows, last)
    for at in range(1, last):
        head = table_hop(head, at)
        rest = table_hop(rest, at - 1)
    w_lead = lead_hop(w_lead, 0)
    table_rows, head, rest, w_lead = tie((table_rows, head, rest, w_lead))
    table = table_rows[0, :count].astype(jnp.int32)

    starts = [g ^ (CORE | CHIP), g ^ CHIP, g ^ CORE, g]
    places = jnp.concatenate(
        [s * quarter_blocks + jnp.arange(quarter_blocks) for s in starts] + [jnp.arange(PR)]
    )
    source = jnp.take(table, places)
    kept = (source >= PL).astype(jnp.int32)
    one = jnp.ones((1,), jnp.int32)
    ways = quarter_blocks // 2
    n = quarter_blocks

    def rows_at(first, size, adds, name, scale=one, ways=ways):
        return take_rows(
            front, mask, source[first : first + size], kept[first : first + size], scale, ways,
            adds, name,
        )

    first = rows_at(
        4 * n, PR, [(root_front, 0, 0)], "first_rows", (g == 0).astype(jnp.int32).reshape(1), PR
    )
    first = first + flip(first, "grp", CORE)
    head = table_hop(head, last)
    rest = table_hop(rest, last - 1)
    w_lead = lead_hop(w_lead, 1)
    diagonal = rows_at(0, n, [], "far_rows")
    near = rows_at(2 * n, n, [], "near_rows")
    head, rest, w_lead, first, diagonal, near = tie((head, rest, w_lead, first, diagonal, near))
    diagonal = flip(diagonal, "grp", CORE)
    near = flip(near, "grp", CORE)
    first = first + flip(first, "grp", CHIP)
    rest = table_hop(rest, last)
    for at in range(2, last + 1):
        w_lead = lead_hop(w_lead, at)

    work = [pltpu.VMEM((b, 2 * b), f32)]
    sq = shape((b, b), f32)
    sqh = shape((b, b), bf16)
    logs = shape((8, b), f32)

    def w_spec(k):
        return pl.BlockSpec((b, cols), lambda i: (k, 0))

    p01, inv0, inv1, x01, log01 = pl.pallas_call(
        leaf_two,
        grid=(1,),
        in_specs=[vmem, w_spec(0), w_spec(1), vmem],
        out_specs=[vmem] * 5,
        out_shape=(shape((2 * b, cols), bf16), sq, sq, sqh, logs),
        scratch_shapes=work,
        name="leaf_two",
    )(head, front, front, mask)

    p01, rest, w_lead, first = tie((p01, rest, w_lead, first))

    def across(value):
        far_value = flip(value, "grp", CHIP)
        both = jnp.concatenate([value, far_value], axis=0)
        return jnp.concatenate([both, flip(both, "grp", CORE)], axis=0)

    d01 = across(p01)
    outward = hops[::-1]
    corner = lead_hop([first[:, :lead_cols]] * leads, 0, outward)
    rest, d01, corner = tie((rest, d01, corner))
    corner = lead_hop(corner, 1, outward)
    w_lead = w_lead[0] if leads == 1 else jnp.concatenate(w_lead, axis=1)
    lead_rows = (PL * b + LOG_ROWS) * pr // cols
    pack = pl.pallas_call(
        leaf_last,
        grid=(1,),
        in_specs=[vmem, w_spec(2)] + [vmem] * 8,
        out_specs=vmem,
        out_shape=shape((b + lead_rows, cols), bf16),
        scratch_shapes=[pltpu.VMEM((b, b), f32)] + work,
        name="leaf_last",
    )(rest, front, w_lead, table_rows, mask, p01, inv0, inv1, x01, log01)

    def among(offsets):
        found = jnp.zeros((), jnp.bool_)
        for h in offsets:
            found = found | (zone == (g ^ h))
        return found

    def zone_hop(state):
        have, held, _ = state
        bit = groups // 2 // len(have)
        pairs = []
        for gi in range(groups):
            for h in have:
                for j in range(spread):
                    src = (gi ^ h) * spread + j
                    dst = (gi ^ h ^ bit) * spread + j
                    pairs.append((gi * members + src, gi * members + dst))
        got = lax.ppermute(held, ("grp", "mem"), pairs)
        new = [h ^ bit for h in have]
        return have + new, jnp.where(among(new), got, held), (new, got)

    def inner_hop(stage, i):
        offsets, value = stage
        pairs = []
        for gi in range(groups):
            for h in offsets:
                for j in range(spread):
                    at = gi * members + (gi ^ h) * spread
                    pairs.append((at + j, at + (j ^ i)))
        return lax.ppermute(value, ("grp", "mem"), pairs)

    def inner_hops(state, early=None):
        have, held, last_stage = state
        slots = [held]
        for i in range(1, spread):
            if early is None:
                slots.append(inner_hop((have, held), i))
            else:
                got = inner_hop(last_stage, i)
                slots.append(jnp.where(among(last_stage[0]), got, early[i - 1]))
        return slots

    def early_hops(state):
        return [inner_hop((state[0], state[1]), i) for i in range(1, spread)]

    s01 = zone_hop(([0], d01, None))
    pack, diagonal = tie((pack, diagonal))
    pack_far = flip(pack, "grp", CHIP)
    few = n // 4
    far_near = rows_at(n, few, [(diagonal, 0, 0)], "far_sum", ways=few)
    far_near = flip(far_near, "grp", CHIP)
    pack, pack_far, diagonal, corner = tie((pack, pack_far, diagonal, corner))
    far_in = rows_at(n + few, n - few, [(diagonal, 0, 1)], "far_sum", ways=few)
    for at in range(2, last + 1):
        corner = lead_hop(corner, at, outward)
    pack = jnp.concatenate([pack, pack_far], axis=0)
    pack = jnp.concatenate([pack, flip(pack, "grp", CORE)], axis=0)
    pack, held, far_in, far_near, corner = tie((pack, s01[1], far_in, far_near, corner))
    corner = corner[0] if leads == 1 else jnp.concatenate(corner, axis=1)
    s01 = (s01[0], held, None)
    far_last = flip(far_in, "grp", CHIP)
    early01 = early_hops(s01)
    s01 = zone_hop(s01)
    d2 = pack.reshape(groups, b + lead_rows, cols)[:, :b].reshape(groups * b, cols)
    s2 = zone_hop(([0], d2, None))
    leaves = jnp.stack([g, g ^ CHIP, g ^ CORE, g ^ (CORE | CHIP)])
    q, rinv0, rinv1, rx, logs_out = pl.pallas_call(
        root_step,
        in_specs=[smem] + [vmem] * 4,
        out_shape=(shape((pr, cols), bf16), sq, sq, sqh, logs),
        scratch_shapes=work,
        compiler_params=pltpu.CompilerParams(vmem_limit_bytes=32 << 20),
        name="root_step",
    )(leaves, corner, first, d01, pack)
    sq_hop = zone_hop(([0], q, None))
    q_held, held, s01_held, s01_got = tie((sq_hop[1], s2[1], s01[1], s01[2][1]))
    s01 = (s01[0], s01_held, (s01[2][0], s01_got))
    s2 = (s2[0], held, None)
    sq_hop = zone_hop((sq_hop[0], q_held, None))
    early2 = early_hops(s2)
    s2 = zone_hop(s2)
    q_held, *early01 = tie((sq_hop[1], *early01))
    rq = inner_hops((sq_hop[0], q_held, None))
    r01 = inner_hops(s01, early01)
    r2 = inner_hops(s2, early2)

    adds = [(root_front, 0, 0), (near, 0, 0), (far_near, 0, 0), (far_last, 1, 0)]
    base = rows_at(3 * n, n, adds, "base_rows", ways=few)
    slot_of = inner ^ jnp.arange(spread, dtype=jnp.int32)

    def update_body(*refs):
        update_kernel(spread, *refs)

    def whole_spec(array):
        return pl.BlockSpec(array.shape, lambda s, *pre: (0, 0))

    part = pl.pallas_call(
        update_body,
        grid_spec=pltpu.PrefetchScalarGridSpec(
            num_scalar_prefetch=1,
            grid=(spread,),
            in_specs=[pl.BlockSpec((cols, cols), lambda s, place: (place[s], 0))]
            + [whole_spec(array) for array in [d01] + r01],
            out_specs=pl.BlockSpec((cols, cols), lambda s, place: (s, 0)),
        ),
        out_shape=shape((quarter, cols), f32),
        compiler_params=pltpu.CompilerParams(vmem_limit_bytes=40 << 20),
        name="update",
    )(slot_of, base, d01, *r01)
    if leads > 1:
        first_col = jnp.minimum(m, leads - 1) * lead_cols
        panel = jnp.concatenate([rows.astype(f32).T for rows in rq], axis=0)
        panel = lax.dynamic_slice_in_dim(panel, first_col, lead_cols, 1)
    else:
        panel = jnp.zeros((8, lead_cols), f32)
    info = jnp.concatenate([g * quarter + slot_of * cols, (m * cols).reshape(1)])

    def finish_body(*refs):
        finish_kernel(spread, leads == 1, *refs)

    fixed = [d2, q, rinv0, rinv1, rx, panel] + r2 + rq
    root_factor = pl.pallas_call(
        finish_body,
        grid_spec=pltpu.PrefetchScalarGridSpec(
            num_scalar_prefetch=2,
            grid=(spread,),
            in_specs=[pl.BlockSpec((cols, cols), lambda s, place, info: (s, 0))]
            + [whole_spec(array) for array in fixed],
            out_specs=pl.BlockSpec((cols, cols), lambda s, place, info: (place[s], 0)),
        ),
        out_shape=shape((quarter, cols), f32),
        compiler_params=pltpu.CompilerParams(vmem_limit_bytes=40 << 20),
        name="finish",
    )(slot_of, info, part, *fixed)
    return root_factor, logs_out[0, : groups + 1]


def solution(mesh):
    in_specs = (P("grp", None, "mem"), P("grp", "mem"), P("grp", "mem"))
    out_specs = (P("grp", "mem"), P())
    return jax.shard_map(local, mesh=mesh, in_specs=in_specs, out_specs=out_specs, check_vma=False)
```

```python
import jax
import jax.numpy as jnp
from jax import lax
from jax.experimental import pallas as pl
from jax.experimental.pallas import tpu as pltpu
from jax.sharding import PartitionSpec as P

PL = 3
PR = 2
HIGHEST = lax.Precision.HIGHEST
ROWS = 64
SUB = 16
LOG_ROWS = 32
B_ROWS = 128
CORE, CHIP = 1, 2
f32, bf16 = jnp.float32, jnp.bfloat16


def mm(lhs, rhs):
    return jnp.dot(lhs, rhs, precision=HIGHEST, preferred_element_type=f32)


def mm_t(lhs, rhs):
    return lax.dot_general(
        lhs, rhs, (((1,), (1,)), ((), ())), precision=HIGHEST, preferred_element_type=f32
    )


def tdot(lhs, rhs):
    return lax.dot_general(lhs, rhs, (((0,), (0,)), ((), ())), preferred_element_type=f32)


def bits(size):
    out, bit = [], 1
    while bit < size:
        out.append(bit)
        bit *= 2
    return out


def flip(value, axis, bit):
    size = lax.axis_size(axis)
    return lax.ppermute(value, axis, [(i, i ^ bit) for i in range(size)])


def shape(dims, dtype):
    return jax.ShapeDtypeStruct(dims, dtype)


def invert_factor(block, work, inverse_ref):
    size = block.shape[0]
    rows = lax.broadcasted_iota(jnp.int32, (size, size), 0)
    cols = lax.broadcasted_iota(jnp.int32, (size, size), 1)
    work[:, :size] = block
    work[:, size:] = jnp.where(rows == cols, 1.0, 0.0)
    sub = lax.broadcasted_iota(jnp.int32, (ROWS, size), 0)
    lane = lax.broadcasted_iota(jnp.int32, (ROWS, size), 1)
    log_sum = jnp.zeros((1, 1), f32)
    for first in range(0, size, ROWS):
        left = work[first : first + ROWS, :size]
        right = work[first : first + ROWS, size:]
        for start in range(0, ROWS, SUB):
            at = first + start
            columns = [
                jnp.broadcast_to(left[:, at + j : at + j + 1], (ROWS, size)) for j in range(SUB)
            ]
            for j in range(SUB):
                i = start + j
                if i == ROWS - 1:
                    break
                factor = jnp.where(sub > i, columns[j], 0.0) * (1.0 / columns[j][i : i + 1, :])
                for k in range(j + 1, SUB):
                    columns[k] = columns[k] - factor * columns[k][i : i + 1, :]
                left = left - factor * left[i : i + 1, :]
                right = right - factor * right[i : i + 1, :]
        pivot = jnp.sum(jnp.where(lane == sub + first, left, 0.0), axis=1, keepdims=True)
        scale = lax.rsqrt(pivot)
        left, right = left * scale, right * scale
        inverse_ref[first : first + ROWS, :] = right
        log_sum = log_sum + jnp.sum(jnp.log(pivot), axis=0, keepdims=True)
        if first + ROWS < size:
            update = lax.dot_general(
                left, jnp.concatenate([left, right], axis=1), (((0,), (0,)), ((), ())),
                precision=HIGHEST, preferred_element_type=f32,
            )
            work[first + ROWS :, :] = work[first + ROWS :, :] - update[first + ROWS :, :]
    return log_sum


def pick_pivots(owner_ref, at_ref, front_ref, table_ref, head_ref, rest_ref, mask_ref, lead_ref):
    b = head_ref.shape[1]
    per = front_ref.shape[1] // b
    for k in range(PL):
        total = jnp.zeros(((k + 1) * b, b), f32)
        for t in range(per):
            part = front_ref[: (k + 1) * b, t * b : (t + 1) * b]
            total = total + jnp.where(owner_ref[t] == k, part, 0.0)
        if k == 0:
            head_ref[:b, :] = total
        elif k == 1:
            head_ref[b:, :] = total
        else:
            rest_ref[...] = total
    lane = lax.broadcasted_iota(jnp.int32, (8, b), 1)
    table = jnp.zeros((8, b), f32)
    for t in range(per):
        table = table + jnp.where(lane == at_ref[0] + t, owner_ref[t].astype(f32), 0.0)
        keep = jnp.where(owner_ref[t] >= PL, 1.0, 0.0).astype(f32)
        mask_ref[:, t * b : (t + 1) * b] = jnp.full((8, b), keep, f32)
    table_ref[...] = table
    lead_ref[...] = front_ref[:, : lead_ref.shape[1]]


def leaf_two(head_ref, w0_ref, w1_ref, mask_ref, p_ref, inv0_ref, inv1_ref, x_ref, log_ref, work):
    b = w0_ref.shape[0]
    c00, c01, c11 = [head_ref[i * b : (i + 1) * b, :] for i in range(3)]
    keep = mask_ref[:1, :] > 0.0
    log0 = invert_factor(c00, work, inv0_ref)
    x01 = mm(inv0_ref[...], c01).astype(bf16)
    x_ref[...] = x01
    p0 = mm(inv0_ref[...], w0_ref[...]).astype(bf16)
    log1 = invert_factor(c11 - tdot(x01, x01), work, inv1_ref)
    p1 = mm(inv1_ref[...], w1_ref[...] - tdot(x01, p0)).astype(bf16)
    p_ref[:b, :] = jnp.where(keep, p0, jnp.zeros_like(p0))
    p_ref[b:, :] = jnp.where(keep, p1, jnp.zeros_like(p1))
    log_ref[...] = jnp.broadcast_to(log0 + log1, log_ref.shape)


def leaf_last(
    rest_ref, w2_ref, w_lead_ref, table_ref, mask_ref, p_ref, inv0_ref, inv1_ref, x_ref, log_ref,
    out_ref, inv, work,
):
    b, cols = w2_ref.shape
    wide = w_lead_ref.shape[1] if w_lead_ref.shape[1] > cols else PR * b
    c02, c12, c22 = [rest_ref[i * b : (i + 1) * b, :] for i in range(3)]
    inv0, inv1, x01 = inv0_ref[...], inv1_ref[...], x_ref[...]
    x02 = mm(inv0, c02).astype(bf16)
    x12 = mm(inv1, c12 - tdot(x01, x02)).astype(bf16)
    log2 = invert_factor(c22 - tdot(x02, x02) - tdot(x12, x12), work, inv)
    inv2 = inv[...]
    keep = mask_ref[:1, :] > 0.0
    panel = mm(inv2, w2_ref[...] - tdot(x02, p_ref[:b, :]) - tdot(x12, p_ref[b:, :])).astype(bf16)
    out_ref[:b, :] = jnp.where(keep, panel, jnp.zeros_like(panel))
    lane = lax.broadcasted_iota(jnp.int32, (1, wide), 1)
    block = jnp.zeros((1, wide), f32)
    for t in range(PR):
        inside = (lane >= t * b) & (lane < (t + 1) * b)
        block = jnp.where(inside, table_ref[:1, t : t + 1], block)
    keep = block > PL - 0.5
    lead0 = mm(inv0, w_lead_ref[:b, :]).astype(bf16)
    lead1 = mm(inv1, w_lead_ref[b : 2 * b, :] - tdot(x01, lead0)).astype(bf16)
    lead2 = w_lead_ref[2 * b :, :] - tdot(x02, lead0) - tdot(x12, lead1)
    lead2 = mm(inv2, lead2).astype(bf16)
    value = log_ref[:1, :1] + log2
    line = lax.broadcasted_iota(jnp.int32, (LOG_ROWS, wide), 0)
    rows = jnp.zeros((LOG_ROWS, wide), f32)
    for i in range(3):
        part = value.astype(bf16).astype(f32)
        rows = jnp.where(line == i, part, rows)
        value = value - part
    leads = [jnp.where(keep, lead, jnp.zeros_like(lead)) for lead in (lead0, lead1, lead2)]
    whole = jnp.concatenate(leads + [rows.astype(bf16)], axis=0)
    if cols >= wide:
        split = cols // wide
        tall = whole.shape[0] // split
        for i in range(split):
            out_ref[b:, i * wide : (i + 1) * wide] = whole[i * tall : (i + 1) * tall, :]
    else:
        tall = whole.shape[0]
        for i in range(wide // cols):
            out_ref[b + i * tall : b + (i + 1) * tall, :] = whole[:, i * cols : (i + 1) * cols]


def rows_kernel(ways, spans, *refs):
    keep_ref, scale_ref = refs[1:3]
    fronts = refs[3 : 3 + ways]
    mask_ref = refs[3 + ways]
    adds = refs[4 + ways : -1]
    out_ref = refs[-1]
    step = pl.program_id(0)
    b = fronts[0].shape[0]
    keep_cols = mask_ref[:1, :] > 0.0
    for i, front_ref in enumerate(fronts):
        at = slice(i * b, (i + 1) * b)
        keep = keep_cols & (keep_ref[step * ways + i] > 0)
        total = jnp.where(keep, front_ref[...], 0.0)
        for add_ref, (first, last) in zip(adds, spans):
            use = (step >= first) & (step < last) & (scale_ref[0] > 0)
            total = total + jnp.where(use, add_ref[at, :], 0.0)
        out_ref[at, :] = total


def take_rows(front, mask, source, kept, scale, ways, adds, name):
    b = B_ROWS
    cols = front.shape[1]
    steps = source.shape[0] // ways
    spans, add_specs = [], []
    for array, first, tile in adds:
        tiles = array.shape[0] // (ways * b) - tile
        last = min(steps, first + tiles)
        spans.append((first, last))

        def index(s, *pre, first=first, last=last, tile=tile):
            return (jnp.clip(s, first, last - 1) - first + tile, 0)

        add_specs.append(pl.BlockSpec((ways * b, cols), index))
    front_specs = [
        pl.BlockSpec((b, cols), lambda s, *pre, i=i: (pre[0][s * ways + i], 0)) for i in range(ways)
    ]

    def body(*refs):
        rows_kernel(ways, spans, *refs)

    return pl.pallas_call(
        body,
        grid_spec=pltpu.PrefetchScalarGridSpec(
            num_scalar_prefetch=3,
            grid=(steps,),
            in_specs=front_specs + [pl.BlockSpec((8, cols), lambda s, *pre: (0, 0))] + add_specs,
            out_specs=pl.BlockSpec((ways * b, cols), lambda s, *pre: (s, 0)),
        ),
        out_shape=shape((source.shape[0] * b, cols), f32),
        compiler_params=pltpu.CompilerParams(vmem_limit_bytes=60 << 20),
        name=name,
    )(source, kept, scale, *([front] * ways), mask, *[array for array, _, _ in adds])


def root_step(
    leaf_ref, corner_ref, first_ref, d01_ref, pack_ref,
    q_ref, inv0_ref, inv1_ref, x_ref, log_ref, work,
):
    b = inv0_ref.shape[0]
    cols = first_ref.shape[1]
    wide = corner_ref.shape[1]
    groups = d01_ref.shape[0] // (2 * b)
    pitch = pack_ref.shape[0] // groups
    corner = corner_ref[...]
    top = first_ref[...]
    lane = lax.broadcasted_iota(jnp.int32, (8, b), 1)
    logs = jnp.zeros((8, b), f32)
    for i in range(groups):
        at = i * pitch
        d2 = pack_ref[at : at + b, :]
        packed = pack_ref[at + b : at + pitch, :]
        if cols >= wide:
            parts = [packed[:, j * wide : (j + 1) * wide] for j in range(cols // wide)]
            whole = jnp.concatenate(parts, axis=0)
        else:
            tall = (pitch - b) // (wide // cols)
            parts = [packed[j * tall : (j + 1) * tall, :] for j in range(wide // cols)]
            whole = jnp.concatenate(parts, axis=1)
        lead = whole[: PL * b, :]
        corner = corner - tdot(lead, lead)
        top = top - tdot(lead[: 2 * b, :], d01_ref[i * 2 * b : (i + 1) * 2 * b, :])
        top = top - tdot(lead[2 * b :, :], d2)
        log_sum = jnp.sum(whole[PL * b : PL * b + 16, :b].astype(f32), axis=0, keepdims=True)
        logs = jnp.where(lane == leaf_ref[i], log_sum * (1.0 / (PL * b)), logs)
    log0 = invert_factor(corner[:b, :b], work, inv0_ref)
    x = mm(inv0_ref[...], corner[:b, b:]).astype(bf16)
    x_ref[...] = x
    log1 = invert_factor(corner[b:, b:] - tdot(x, x), work, inv1_ref)
    log_ref[...] = jnp.where(lane == groups, (log0 + log1) * (1.0 / wide), logs)
    q0 = mm(inv0_ref[...], top[:b, :]).astype(bf16)
    q_ref[:b, :] = q0
    q_ref[b:, :] = mm(inv1_ref[...], top[b:, :] - tdot(x, q0)).astype(bf16)


def update_kernel(slots, *refs):
    place_ref, base_ref, d01_ref = refs[:3]
    r01, out_ref = refs[3 : 3 + slots], refs[3 + slots]

    def at_slot(i):
        out_ref[...] = base_ref[...] - tdot(r01[i][...], d01_ref[...])

    for i in range(slots):
        pl.when(pl.program_id(0) == i)(lambda i=i: at_slot(i))


def finish_kernel(slots, whole_panel, *refs):
    place_ref, info_ref, part_ref = refs[:3]
    d2_ref, q_ref, inv0_ref, inv1_ref, x_ref, panel_ref = refs[3:9]
    r2, rq = refs[9 : 9 + slots], refs[9 + slots : 9 + 2 * slots]
    out_ref = refs[9 + 2 * slots]
    rows, cols = out_ref.shape
    wide = q_ref.shape[0]
    b = wide // PR

    def at_slot(i):
        total = part_ref[...] - tdot(r2[i][...], d2_ref[...])
        row = info_ref[i] + lax.broadcasted_iota(jnp.int32, (rows, cols), 0)
        width = min(wide, cols)
        if whole_panel:
            q0 = mm_t(total[:, :b], inv0_ref[...])
            x_part = jnp.dot(q0.astype(bf16), x_ref[...], preferred_element_type=f32)
            q1 = mm_t(total[:, b:wide] - x_part, inv1_ref[...])
            panel = jnp.concatenate([q0, q1], axis=1)
        else:
            panel = panel_ref[pl.ds(pl.multiple_of(i * rows, rows), rows), :]
        total = total - tdot(rq[i][...], q_ref[...])
        total = jnp.where(row >= wide, total, 0.0)
        col = info_ref[slots] + lax.broadcasted_iota(jnp.int32, (rows, width), 1)
        panel = jnp.where((row[:, :width] >= b) | (col < b), panel, 0.0)
        out_ref[:, :width] = jnp.where(col < wide, panel, total[:, :width])
        if width < cols:
            out_ref[:, width:] = total[:, width:]

    for i in range(slots):
        pl.when(pl.program_id(0) == i)(lambda i=i: at_slot(i))


def local(leaf_fronts, block_owner, root_front):
    members = lax.axis_size("mem")
    groups = lax.axis_size("grp")
    m = lax.axis_index("mem")
    g = lax.axis_index("grp")
    front = leaf_fronts[0]
    order, cols = front.shape
    owner = block_owner[0]
    per = owner.shape[0]
    b = cols // per
    count = order // b
    quarter = order // groups
    spread = members // groups
    quarter_blocks = quarter // b
    pr = PR * b
    lead_cols = min(pr, cols)
    leads = pr // lead_cols
    zone, inner = m // spread, m % spread
    smem = pl.BlockSpec(memory_space=pltpu.SMEM)
    vmem = pl.BlockSpec(memory_space=pltpu.VMEM)

    hops = bits(members)
    last = len(hops) - 1
    lead_order = [hops[-1], hops[0]] + hops[-2:0:-1]

    def lead_hop(value, at):
        bit, used = lead_order[at], sum(lead_order[:at])
        parts = []
        for root in range(leads):
            held = value[root]
            sources = [root ^ i for i in range(members) if i & ~used == 0]
            got = lax.ppermute(held, "mem", [(src, src ^ bit) for src in sources])
            parts.append(jnp.where((m ^ root) & ~used == bit, got, held))
        return parts

    table_rows, head, rest, mask, w_lead = pl.pallas_call(
        pick_pivots,
        grid=(1,),
        in_specs=[smem, smem, pl.BlockSpec((PL * b, cols), lambda i: (0, 0))],
        out_specs=[vmem] * 5,
        out_shape=(
            shape((8, b), f32), shape((3 * b, b), f32), shape((3 * b, b), f32),
            shape((8, cols), f32), shape((PL * b, lead_cols), f32),
        ),
        name="pick_pivots",
    )(owner, (m * per).reshape(1), front)
    w_lead = [w_lead] * leads

    def table_hop(value, at):
        return value + flip(value, "mem", hops[at])

    tie = lax.optimization_barrier
    for at in range(last + 1):
        table_rows = table_hop(table_rows, at)
    head = table_hop(head, 0)
    w_lead = lead_hop(w_lead, 0)
    table_rows, head, rest, w_lead = tie((table_rows, head, rest, w_lead))
    table = table_rows[0, :count].astype(jnp.int32)

    starts = [g ^ (CORE | CHIP), g ^ CHIP, g ^ CORE, g]
    places = jnp.concatenate(
        [s * quarter_blocks + jnp.arange(quarter_blocks) for s in starts] + [jnp.arange(PR)]
    )
    source = jnp.take(table, places)
    kept = (source >= PL).astype(jnp.int32)
    one = jnp.ones((1,), jnp.int32)
    ways = quarter_blocks // 2
    n = quarter_blocks

    def rows_at(first, size, adds, name, scale=one, ways=ways):
        return take_rows(
            front, mask, source[first : first + size], kept[first : first + size], scale, ways,
            adds, name,
        )

    diagonal = rows_at(0, n, [], "far_rows")
    first = rows_at(
        4 * n, PR, [(root_front, 0, 0)], "first_rows", (g == 0).astype(jnp.int32).reshape(1), PR
    )
    for at in range(1, last):
        head = table_hop(head, at)
        rest = table_hop(rest, at - 1)
    head, rest, diagonal, first, w_lead = tie((head, rest, diagonal, first, w_lead))
    near = rows_at(2 * n, n, [], "near_rows")
    first = first + flip(first, "grp", CORE)
    head = table_hop(head, last)
    rest = table_hop(rest, last - 1)
    w_lead = lead_hop(w_lead, 1)
    head, rest, w_lead, diagonal, first, near = tie((head, rest, w_lead, diagonal, first, near))
    near = flip(near, "grp", CORE)
    diagonal = flip(diagonal, "grp", CORE)
    first = first + flip(first, "grp", CHIP)
    rest = table_hop(rest, last)
    for at in range(2, last + 1):
        w_lead = lead_hop(w_lead, at)

    work = [pltpu.VMEM((b, 2 * b), f32)]
    sq = shape((b, b), f32)
    sqh = shape((b, b), bf16)
    logs = shape((8, b), f32)

    def w_spec(k):
        return pl.BlockSpec((b, cols), lambda i: (k, 0))

    p01, inv0, inv1, x01, log01 = pl.pallas_call(
        leaf_two,
        grid=(1,),
        in_specs=[vmem, w_spec(0), w_spec(1), vmem],
        out_specs=[vmem] * 5,
        out_shape=(shape((2 * b, cols), bf16), sq, sq, sqh, logs),
        scratch_shapes=work,
        name="leaf_two",
    )(head, front, front, mask)

    p01, rest, w_lead, first, diagonal = tie((p01, rest, w_lead, first, diagonal))
    far_near = flip(rows_at(n, ways, [(diagonal, 0, 0)], "far_sum"), "grp", CHIP)

    def across(value):
        far_value = flip(value, "grp", CHIP)
        both = jnp.concatenate([value, far_value], axis=0)
        return jnp.concatenate([both, flip(both, "grp", CORE)], axis=0)

    d01 = across(p01)
    corner = lead_hop([first[:, :lead_cols]] * leads, 0)
    rest, d01, corner = tie((rest, d01, corner))
    corner = lead_hop(corner, 1)
    w_lead = w_lead[0] if leads == 1 else jnp.concatenate(w_lead, axis=1)
    lead_rows = (PL * b + LOG_ROWS) * pr // cols
    pack = pl.pallas_call(
        leaf_last,
        grid=(1,),
        in_specs=[vmem, w_spec(2)] + [vmem] * 8,
        out_specs=vmem,
        out_shape=shape((b + lead_rows, cols), bf16),
        scratch_shapes=[pltpu.VMEM((b, b), f32)] + work,
        name="leaf_last",
    )(rest, front, w_lead, table_rows, mask, p01, inv0, inv1, x01, log01)

    def among(offsets):
        found = jnp.zeros((), jnp.bool_)
        for h in offsets:
            found = found | (zone == (g ^ h))
        return found

    def zone_hop(state):
        have, held, _ = state
        bit = groups // 2 // len(have)
        pairs = []
        for gi in range(groups):
            for h in have:
                for j in range(spread):
                    src = (gi ^ h) * spread + j
                    dst = (gi ^ h ^ bit) * spread + j
                    pairs.append((gi * members + src, gi * members + dst))
        got = lax.ppermute(held, ("grp", "mem"), pairs)
        new = [h ^ bit for h in have]
        return have + new, jnp.where(among(new), got, held), (new, got)

    def inner_hop(stage, i):
        offsets, value = stage
        pairs = []
        for gi in range(groups):
            for h in offsets:
                for j in range(spread):
                    at = gi * members + (gi ^ h) * spread
                    pairs.append((at + j, at + (j ^ i)))
        return lax.ppermute(value, ("grp", "mem"), pairs)

    def inner_hops(state, early=None):
        have, held, last_stage = state
        slots = [held]
        for i in range(1, spread):
            if early is None:
                slots.append(inner_hop((have, held), i))
            else:
                got = inner_hop(last_stage, i)
                slots.append(jnp.where(among(last_stage[0]), got, early[i - 1]))
        return slots

    def early_hops(state):
        return [inner_hop((state[0], state[1]), i) for i in range(1, spread)]

    s01 = zone_hop(([0], d01, None))
    pack_far = flip(pack, "grp", CHIP)
    pack, pack_far, diagonal, corner, far_near = tie(
        (pack, pack_far, diagonal, corner, far_near)
    )
    far_in = rows_at(n + ways, ways, [(diagonal, 0, 1)], "far_sum")
    for at in range(2, last + 1):
        corner = lead_hop(corner, at)
    pack = jnp.concatenate([pack, pack_far], axis=0)
    pack = jnp.concatenate([pack, flip(pack, "grp", CORE)], axis=0)
    pack, held, far_in, corner = tie((pack, s01[1], far_in, corner))
    corner = corner[0] if leads == 1 else jnp.concatenate(corner, axis=1)
    s01 = (s01[0], held, None)
    far_last = flip(far_in, "grp", CHIP)
    early01 = early_hops(s01)
    s01 = zone_hop(s01)
    d2 = pack.reshape(groups, b + lead_rows, cols)[:, :b].reshape(groups * b, cols)
    s2 = zone_hop(([0], d2, None))
    leaves = jnp.stack([g, g ^ CHIP, g ^ CORE, g ^ (CORE | CHIP)])
    q, rinv0, rinv1, rx, logs_out = pl.pallas_call(
        root_step,
        in_specs=[smem] + [vmem] * 4,
        out_shape=(shape((pr, cols), bf16), sq, sq, sqh, logs),
        scratch_shapes=work,
        compiler_params=pltpu.CompilerParams(vmem_limit_bytes=32 << 20),
        name="root_step",
    )(leaves, corner, first, d01, pack)
    sq_hop = zone_hop(([0], q, None))
    q_held, held, s01_held, s01_got = tie((sq_hop[1], s2[1], s01[1], s01[2][1]))
    s01 = (s01[0], s01_held, (s01[2][0], s01_got))
    s2 = (s2[0], held, None)
    sq_hop = zone_hop((sq_hop[0], q_held, None))
    s2 = zone_hop(s2)
    q_held, far_last, *early01 = tie((sq_hop[1], far_last, *early01))
    rq = inner_hops((sq_hop[0], q_held, None))
    r01 = inner_hops(s01, early01)
    r2 = inner_hops(s2)

    adds = [(root_front, 0, 0), (near, 0, 0), (far_near, 0, 0), (far_last, 1, 0)]
    base = rows_at(3 * n, n, adds, "base_rows")
    slot_of = inner ^ jnp.arange(spread, dtype=jnp.int32)

    def update_body(*refs):
        update_kernel(spread, *refs)

    def whole_spec(array):
        return pl.BlockSpec(array.shape, lambda s, *pre: (0, 0))

    part = pl.pallas_call(
        update_body,
        grid_spec=pltpu.PrefetchScalarGridSpec(
            num_scalar_prefetch=1,
            grid=(spread,),
            in_specs=[pl.BlockSpec((cols, cols), lambda s, place: (place[s], 0))]
            + [whole_spec(array) for array in [d01] + r01],
            out_specs=pl.BlockSpec((cols, cols), lambda s, place: (s, 0)),
        ),
        out_shape=shape((quarter, cols), f32),
        compiler_params=pltpu.CompilerParams(vmem_limit_bytes=40 << 20),
        name="update",
    )(slot_of, base, d01, *r01)
    if leads > 1:
        first_col = jnp.minimum(m, leads - 1) * lead_cols
        panel = jnp.concatenate([rows.astype(f32).T for rows in rq], axis=0)
        panel = lax.dynamic_slice_in_dim(panel, first_col, lead_cols, 1)
    else:
        panel = jnp.zeros((8, lead_cols), f32)
    info = jnp.concatenate([g * quarter + slot_of * cols, (m * cols).reshape(1)])

    def finish_body(*refs):
        finish_kernel(spread, leads == 1, *refs)

    fixed = [d2, q, rinv0, rinv1, rx, panel] + r2 + rq
    root_factor = pl.pallas_call(
        finish_body,
        grid_spec=pltpu.PrefetchScalarGridSpec(
            num_scalar_prefetch=2,
            grid=(spread,),
            in_specs=[pl.BlockSpec((cols, cols), lambda s, place, info: (s, 0))]
            + [whole_spec(array) for array in fixed],
            out_specs=pl.BlockSpec((cols, cols), lambda s, place, info: (place[s], 0)),
        ),
        out_shape=shape((quarter, cols), f32),
        compiler_params=pltpu.CompilerParams(vmem_limit_bytes=40 << 20),
        name="finish",
    )(slot_of, info, part, *fixed)
    return root_factor, logs_out[0, : groups + 1]


def solution(mesh):
    in_specs = (P("grp", None, "mem"), P("grp", "mem"), P("grp", "mem"))
    out_specs = (P("grp", "mem"), P())
    return jax.shard_map(local, mesh=mesh, in_specs=in_specs, out_specs=out_specs, check_vma=False)
```
